32 devices in a mesh: tm: 8 (over z, x), rows: 4 (over y, core).
Axes of the slice: x: 2, y: 2, z: 4, core: 2. Of those that a mesh axis runs over, the one named last changes fastest.
Arguments:
- frames: bfloat16 [4, 24576, 512], P('rows', 'tm'), may hold values from -6 to 6
- cotangent: bfloat16 [4, 24576, 512], P('rows', 'tm'), may hold values from -6 to 6
- lengths: int32 [4, 80], P('rows'), may hold values from 0 to 2816, as said below
- w1_master: float32 [512, 1536], P('tm'), may hold values from -0.25 to 0.25
- w1_first: float32 [512, 1536], P('tm'), may hold values from -512 to 512
- w1_second: float32 [512, 1536], P('tm'), may hold values from 4423.68 to 70778.88
- w1_average: float32 [512, 1536], P('tm'), may hold values from -0.25 to 0.25
- w2_master: float32 [1536, 512], P('tm'), may hold values from -0.15625 to 0.15625
- w2_first: float32 [1536, 512], P('tm'), may hold values from -1024 to 1024
- w2_second: float32 [1536, 512], P('tm'), may hold values from 17694.72 to 283115.53
- w2_average: float32 [1536, 512], P('tm'), may hold values from -0.15625 to 0.15625
- small_master: float32 [15, 512], replicated, may hold values from -0.6 to 1.3
- small_first: float32 [15, 512], replicated, may hold values from -896 to 896
- small_second: float32 [15, 512], replicated, may hold values from 12288 to 196608
- small_average: float32 [15, 512], replicated, may hold values from -0.6 to 1.3
Outputs:
- output: bfloat16 [4, 24576, 512], P('rows', 'tm')
- input_grad: bfloat16 [4, 24576, 512], P('rows', 'tm')
- w1_new: float32 [512, 1536], P('tm')
- w1_first_new: float32 [512, 1536], P('tm')
- w1_second_new: float32 [512, 1536], P('tm')
- w1_average_new: float32 [512, 1536], P('tm')
- w1_copy: bfloat16 [512, 1536], P('tm')
- w2_new: float32 [1536, 512], P('tm')
- w2_first_new: float32 [1536, 512], P('tm')
- w2_second_new: float32 [1536, 512], P('tm')
- w2_average_new: float32 [1536, 512], P('tm')
- w2_copy: bfloat16 [1536, 512], P('tm')
- small_new: float32 [15, 512], replicated
- small_first_new: float32 [15, 512], replicated
- small_second_new: float32 [15, 512], replicated
- small_average_new: float32 [15, 512], replicated
- small_copy: bfloat16 [15, 512], replicated
The draws below stay inside these ranges and needn't reach their ends.
Inputs may be any that keep to these rules, and one draw needn't show every extreme that they name: `lengths`: each row sums to 24576 frames; every nonzero entry is 128, 1024 or 2816, and every row holds a clip of exactly 2816 frames.
All inputs are finite; a program needn't handle non-finite values.
Results may differ from the reference program's by a relative error of at most 0.013.
Values may be sent and summed in bfloat16 or wider, within the bound.
A program may use at most 192 MiB of HBM per device.

```python
import math
import jax
import jax.numpy as jnp
from jax import lax

D = 512
FF = 1536
ADAM_STEP = 3
NROW = 4
TIME = 24576
LONGEST = 2816
MID = 1024
SHORT = 128
TOKENS = 98304


def small_law(key):
    uniform_part = jax.random.uniform(key, (15, D), jnp.float32)
    row_index = jnp.arange(15)[:, None]
    is_tap = row_index < 7
    is_gain = (row_index == 8) | (row_index == 14)
    lowest = jnp.where(is_tap, -0.6, jnp.where(is_gain, 0.7, -0.35))
    highest = jnp.where(is_tap, 0.6, jnp.where(is_gain, 1.3, 0.35))
    return (lowest + (highest - lowest) * uniform_part).astype(jnp.float32)


def draw_small_master(key, part):
    return small_law(jax.random.fold_in(key, 11))


def draw_small_average(key, part):
    return small_law(jax.random.fold_in(key, 23))


def draw_lengths(key, part):
    units = TIME // LONGEST
    tail_count = TIME % LONGEST // SHORT
    picks = jax.random.randint(jax.random.fold_in(key, 37), (NROW, units), 0, 2, dtype=jnp.int32)
    leading = jnp.arange(units, dtype=jnp.int32)[None, :] == 0
    picks = jnp.where(leading, 0, picks)
    long_unit = jnp.array([LONGEST, 0, 0, 0, 0, 0, 0, 0], jnp.int32)
    split_unit = jnp.array([MID, MID, SHORT, SHORT, SHORT, SHORT, SHORT, SHORT], jnp.int32)
    entries = jnp.where(picks[:, :, None] == 0, long_unit[None, None, :], split_unit[None, None, :])
    entries = entries.reshape(NROW, units * 8)
    tail_part = jnp.full((NROW, tail_count), SHORT, jnp.int32)
    return jnp.concatenate([entries, tail_part], axis=1).astype(jnp.int32)


def shard_levels(key, extent, split, least, top_value):
    def one(dim, parts):
        steps = jax.random.uniform(jax.random.fold_in(jax.random.fold_in(key, 6), dim), (parts,), jnp.float32, least / len(split), top_value / len(split))
        return jnp.repeat(jnp.exp(steps), extent[dim] // parts).reshape((-1,) + (1,) * (len(extent) - dim - 1))

    loudness = one(*split[0])
    for cut in split[1:]:
        loudness = loudness * one(*cut)
    return loudness


def scatter_about(key, dims, scale, most, shards=(), kind=jnp.bfloat16):
    loudness = shard_levels(key, dims, shards, -0.22, 0.18) if shards else 1.0
    values = jax.random.normal(key, dims, jnp.float32) * scale * loudness
    return jnp.minimum(jnp.maximum(values, -most), most).astype(kind)


def setup_inputs(seed: int = 0) -> dict:
    keys = jax.random.split(jax.random.key(seed), 16)
    return {
        "frames": scatter_about(keys[0], (NROW, TIME, D), 1.0, 6.0, ((0, 4), (1, 8))),
        "cotangent": scatter_about(keys[1], (NROW, TIME, D), 1.0, 6.0, ((0, 4), (1, 8))),
        "lengths": draw_lengths(jax.random.fold_in(keys[15], 71), 0),
        "w1_master": scatter_about(keys[3], (D, FF), D ** -0.5, 0.25, ((0, 8),), jnp.float32),
        "w1_first": scatter_about(keys[4], (D, FF), (0.3 * TOKENS ** 0.5), 512.0, ((0, 8),), jnp.float32),
        "w1_second": jnp.clip(jnp.exp(math.log(70778.88) - 2.7725887 * jax.random.uniform(keys[5], (D, FF), jnp.float32) ** shard_levels(keys[5], (D, FF), ((0, 8),), -0.2, 0.2)), 4423.68, 70778.88),
        "w1_average": scatter_about(keys[6], (D, FF), D ** -0.5, 0.25, ((0, 8),), jnp.float32),
        "w2_master": scatter_about(keys[7], (FF, D), FF ** -0.5, 0.15625, ((0, 8),), jnp.float32),
        "w2_first": scatter_about(keys[8], (FF, D), (0.6 * TOKENS ** 0.5), 1024.0, ((0, 8),), jnp.float32),
        "w2_second": jnp.clip(jnp.exp(math.log(283115.53) - 2.7725887 * jax.random.uniform(keys[9], (FF, D), jnp.float32) ** shard_levels(keys[9], (FF, D), ((0, 8),), -0.2, 0.2)), 17694.72, 283115.53),
        "w2_average": scatter_about(keys[10], (FF, D), FF ** -0.5, 0.15625, ((0, 8),), jnp.float32),
        "small_master": draw_small_master(jax.random.fold_in(keys[15], 71), 0),
        "small_first": scatter_about(keys[12], (15, D), (0.5 * TOKENS ** 0.5), 896.0, (), jnp.float32),
        "small_second": jnp.clip(jnp.exp(jax.random.uniform(keys[13], (15, D), jnp.float32, math.log(12288.0), math.log(196608.0))), 12288.0, 196608.0),
        "small_average": draw_small_average(jax.random.fold_in(keys[15], 71), 0),
    }


norm_eps = 1e-06
adam_eps = 1e-08
weight_decay = 0.01
beta_first = 0.5
beta_second = 0.5
average_keep = 0.75
rate_first = 0.08
rate_second = 0.05
rate_small = 0.4

@jax.custom_vjp
def low(v):
    return lax.optimization_barrier(v.astype(jnp.bfloat16)).astype(jnp.float32)

@jax.custom_vjp
def low_back(v):
    return v

def low_keep(v):
    return (low(v), None)

def low_pass(kept, grad):
    return (grad,)

def back_keep(v):
    return (v, None)

def back_low(kept, grad):
    return (low(grad),)
low.defvjp(low_keep, low_pass)
low_back.defvjp(back_keep, back_low)

def edge_masks(lengths_row, first_frame, frame_count):
    ends_at = jnp.cumsum(lengths_row, dtype=jnp.int32)
    ends_before = jnp.concatenate([jnp.zeros((1,), jnp.int32), ends_at[:-1]])
    places = first_frame + jnp.arange(frame_count, dtype=jnp.int32)
    clip_index = jnp.searchsorted(ends_at, places, side='right').astype(jnp.int32)
    clip_index = jnp.minimum(clip_index, ends_at.shape[0] - 1)
    lower = ends_before[clip_index]
    upper = ends_at[clip_index]
    mask_rows = []
    for tap_index in range(7):
        spot_now = places + (tap_index - 3)
        mask_rows.append(((spot_now >= lower) & (spot_now < upper)).astype(jnp.float32))
    return jnp.stack(mask_rows)

def depthwise(padded, tap_rows, masks, frame_count):
    summed = jnp.zeros((frame_count, padded.shape[1]), jnp.float32)
    for tap_index in range(7):
        window = padded[tap_index:tap_index + frame_count].astype(jnp.float32)
        summed = summed + tap_rows[tap_index][None, :] * window * masks[tap_index][:, None]
    return summed

def layer_norm(conv_out, norm_gain, norm_bias):
    centred = conv_out - lax.optimization_barrier(jnp.mean(conv_out, axis=-1, keepdims=True))
    spread = lax.optimization_barrier(jnp.mean(centred * centred, axis=-1, keepdims=True))
    return centred * lax.rsqrt(spread + norm_eps) * norm_gain[None, :] + norm_bias[None, :]

def exact_gelu(values):
    return jax.nn.gelu(values, approximate=False)

def adamw_step(master, first_old, second_old, average_old, gradient, rate):
    first_new = beta_first * first_old + (1.0 - beta_first) * gradient
    second_new = beta_second * second_old + (1.0 - beta_second) * gradient * gradient
    first_hat = first_new / (1.0 - beta_first ** ADAM_STEP)
    second_hat = second_new / (1.0 - beta_second ** ADAM_STEP)
    master_new = master - rate * (first_hat / (jnp.sqrt(second_hat) + adam_eps) + weight_decay * master)
    average_new = average_keep * average_old + (1.0 - average_keep) * master_new
    return (master_new, first_new, second_new, average_new, master_new.astype(jnp.bfloat16))

def forward_row(inputs, small_vals, first_vals, second_vals, masks):
    frame_count = inputs.shape[0]
    width = inputs.shape[1]
    padded = jnp.pad(inputs, ((3, 3), (0, 0)))
    conv_out = low_back(depthwise(padded, small_vals[0:7], masks, frame_count) + small_vals[7][None, :])
    normed_low = low(layer_norm(conv_out, small_vals[8], small_vals[9]))
    first_low = low(first_vals)
    second_low = low(second_vals)
    bias_one = small_vals[10:13].reshape(-1)
    bias_two = small_vals[13]
    layer_scale = small_vals[14]
    block_len = math.gcd(frame_count, 4096)

    def block_fn(pair):
        normed_part, input_part = pair
        hidden = low_back(jnp.dot(normed_part, first_low, precision=lax.Precision.HIGHEST) + bias_one[None, :])
        activated = low(exact_gelu(hidden))
        branch = low_back(jnp.dot(activated, second_low, precision=lax.Precision.HIGHEST) + bias_two[None, :])
        return input_part + layer_scale[None, :] * branch
    results = lax.map(jax.checkpoint(block_fn), (normed_low.reshape(-1, block_len, width), inputs.reshape(-1, block_len, width)))
    return results.reshape(frame_count, width)

def reference(frames, cotangent, lengths, w1_master, w1_first, w1_second, w1_average, w2_master, w2_first, w2_second, w2_average, small_master, small_first, small_second, small_average):
    frame_total = frames.shape[1]

    def row_step(carry, row_data):
        frames_row, cot_row, lengths_row = row_data
        masks = edge_masks(lengths_row, 0, frame_total)

        def forward(inputs, small_vals, first_vals, second_vals):
            return forward_row(inputs, small_vals, first_vals, second_vals, masks)
        result, pull_back = jax.vjp(forward, frames_row.astype(jnp.float32), small_master, w1_master, w2_master)
        input_grad, small_grad, grad_one, grad_two = pull_back(cot_row.astype(jnp.float32))
        carry = (carry[0] + small_grad, carry[1] + grad_one, carry[2] + grad_two)
        return (carry, (result.astype(jnp.bfloat16), input_grad.astype(jnp.bfloat16)))
    start_carry = (jnp.zeros(small_master.shape, jnp.float32), jnp.zeros(w1_master.shape, jnp.float32), jnp.zeros(w2_master.shape, jnp.float32))
    totals, stacked = lax.scan(row_step, start_carry, (frames, cotangent, lengths))
    small_total, grad_one, grad_two = totals
    output, input_grad = stacked
    one_out = adamw_step(w1_master, w1_first, w1_second, w1_average, grad_one, rate_first)
    two_out = adamw_step(w2_master, w2_first, w2_second, w2_average, grad_two, rate_second)
    small_out = adamw_step(small_master, small_first, small_second, small_average, small_total, rate_small)
    return (output, input_grad, one_out[0], one_out[1], one_out[2], one_out[3], one_out[4], two_out[0], two_out[1], two_out[2], two_out[3], two_out[4], small_out[0], small_out[1], small_out[2], small_out[3], small_out[4])
```

```python
import functools

import jax
import jax.numpy as jnp
import numpy as np
from jax import lax
from jax.experimental import pallas as pl
from jax.experimental.pallas import tpu as pltpu
from jax.sharding import PartitionSpec as P

ADAM_STEP = 3
norm_eps = 1e-06
adam_eps = 1e-08
weight_decay = 0.01
beta_first = 0.5
beta_second = 0.5
average_keep = 0.75
rate_first = 0.08
rate_second = 0.05
rate_small = 0.4

TAPS = 7
TILE = 128
GAP = 8
GRAIN = 32
HALO = 16
F32 = jnp.float32
BF16 = jnp.bfloat16
MESH = pl.DeviceIdType.MESH
RSQRT_HALF = np.float32(0.7071067811865476)
RSQRT_2PI = np.float32(0.3989422804014327)


def adamw_step(master, first_old, second_old, average_old, gradient, rate):
    first_new = beta_first * first_old + (1.0 - beta_first) * gradient
    second_new = beta_second * second_old + (1.0 - beta_second) * gradient * gradient
    first_hat = first_new / (1.0 - beta_first**ADAM_STEP)
    second_hat = second_new / (1.0 - beta_second**ADAM_STEP)
    master_new = master - rate * (
        first_hat / (jnp.sqrt(second_hat) + adam_eps) + weight_decay * master
    )
    average_new = average_keep * average_old + (1.0 - average_keep) * master_new
    return (master_new, first_new, second_new, average_new, master_new.astype(BF16))


class Plan:
    def __init__(self, nt, nr, frame_count, width, hidden):
        self.nt, self.nr, self.t, self.d, self.ff = nt, nr, frame_count, width, hidden
        self.share = hidden // nt
        self.rows1 = width // nt
        self.part = self.rows1 // nr
        self.lanes = width // nr
        self.nb = frame_count // TILE
        self.nc = width // 128
        self.runs = [32, 64, 64, 32]
        self.starts = [0, 32, 96, 160]
        self.blocks = []
        offset = 0
        for run in self.runs:
            self.blocks.append((offset, run * nt))
            offset += run * nt
        self.widest = max(size for _, size in self.blocks)
        self.m = 1024
        self.natural = []
        for run, start in zip(self.runs, self.starts):
            for k in range(nt):
                for o in range(0, run, GRAIN):
                    self.natural.append((self.share * k + start + o) // GRAIN)
        self.regrouped = [self.natural.index(g) for g in range(hidden // GRAIN)]


def lane_permuted(tile_of, source, count):
    per = 128 // GRAIN
    out = []
    for tile in range(count):
        value = None
        for q in range(per):
            run = source[tile * per + q]
            piece = tile_of(run // per)
            shift = ((q - run % per) % per) * GRAIN
            if shift:
                piece = pltpu.roll(piece, shift, 1)
            if value is None:
                value = piece
            else:
                lane = lax.broadcasted_iota(jnp.int32, piece.shape, 1)
                value = jnp.where(lane >= q * GRAIN, piece, value)
        out.append(value)
    return out


def fold(value):
    rows = value.shape[0]
    total = value[0:8]
    for g in range(1, rows // 8):
        total = total + value[8 * g : 8 * g + 8]
    return total


def kernel(
    plan,
    frames_hbm,
    cot_hbm,
    lengths_ref,
    w1_hbm,
    w2_hbm,
    small_ref,
    output_hbm,
    ingrad_hbm,
    g1_out,
    g2_out,
    small_out,
    frx,
    ct,
    nm,
    nmt,
    gb,
    gbt,
    br,
    gn,
    xf,
    xhat,
    rstd,
    w1b,
    w2b,
    m1,
    m2,
    acc1,
    acc2,
    lens,
    flags,
    b1p,
    accs,
    accb,
    tmp,
    s1w1,
    s1w2,
    r1w1,
    r1w2,
    s2w1,
    s2w2,
    r2w1,
    r2w2,
    s3w1,
    s3w2,
    r3w1,
    r3w2,
    finw1,
    finw2,
    sma,
    smr,
    smq,
    smf,
    hprev,
    hnext,
    in_sem,
    out_sem,
    send_sem,
    halo_sem,
    ag_sem,
    rs_sem,
    sm_sem,
):
    p = plan
    nt, nr, t_len = p.nt, p.nr, p.t
    me_t = lax.axis_index("tm")
    me_r = lax.axis_index("rows")
    near = me_r + 1 - 2 * (me_r % 2)
    far = (me_r + 2) % nr
    both = near + 2 - 4 * (near // 2)

    def remote(src, dst, send, recv, tm=None, rows=None):
        device = {"tm": me_t if tm is None else tm, "rows": me_r if rows is None else rows}
        return pltpu.make_async_remote_copy(
            src_ref=src, dst_ref=dst, send_sem=send, recv_sem=recv,
            device_id=device, device_id_type=MESH,
        )

    def arrived(view, sem):
        pltpu.make_async_copy(view, view, sem).wait()

    loads = [
        pltpu.make_async_copy(w1_hbm.at[pl.ds(pl.multiple_of(me_r * p.part, p.part), p.part)], m1, in_sem.at[0]),
        pltpu.make_async_copy(w2_hbm.at[:, pl.ds(pl.multiple_of(me_r * p.lanes, p.lanes), p.lanes)], m2, in_sem.at[1]),
        pltpu.make_async_copy(frames_hbm.at[0], frx.at[pl.ds(HALO, t_len)], in_sem.at[2]),
        pltpu.make_async_copy(cot_hbm.at[0], ct, in_sem.at[3]),
    ]
    for load in loads:
        load.start()

    barrier = pltpu.get_barrier_semaphore()
    for step in range(1, nt):
        pl.semaphore_signal(
            barrier, inc=1, device_id={"tm": (me_t + step) % nt, "rows": me_r}, device_id_type=MESH
        )
    for step in range(1, nr):
        pl.semaphore_signal(
            barrier, inc=1, device_id={"tm": me_t, "rows": (me_r + step) % nr}, device_id_type=MESH
        )

    lens[...] = jnp.zeros_like(lens)
    n_len = lengths_ref.shape[1]
    lens[0:1, 0:n_len] = lengths_ref[...].astype(F32)
    ends = lens[...]
    lane = lax.broadcasted_iota(jnp.int32, ends.shape, 1)
    shift = 1
    while shift < lens.shape[1]:
        ends = ends + jnp.where(lane >= shift, pltpu.roll(ends, shift, 1), 0.0)
        shift *= 2
    n_flag = flags.shape[0]
    spot = me_t * t_len + TILE * lax.broadcasted_iota(jnp.int32, (n_flag, lens.shape[1]), 0)
    hit = (ends[0:1, :] == spot.astype(F32)) | (spot == 0)
    edge = jnp.max(jnp.where(hit, 1.0, 0.0), axis=1, keepdims=True)
    flags[...] = jnp.broadcast_to(edge, flags.shape)
    accs[...] = jnp.zeros_like(accs)
    accb[...] = jnp.zeros_like(accb)
    bias_tiles = lane_permuted(
        lambda i: jnp.broadcast_to(small_ref[10 + i // p.nc : 11 + i // p.nc, 128 * (i % p.nc) : 128 * (i % p.nc) + 128], (8, 128)),
        p.natural,
        p.ff // 128,
    )
    for i, tile in enumerate(bias_tiles):
        b1p[:, 128 * i : 128 * i + 128] = tile

    loads[0].wait()
    loads[1].wait()
    own1 = lane_permuted(lambda i: m1[:, 128 * i : 128 * i + 128], p.natural, p.ff // 128)
    for i, tile in enumerate(own1):
        w1b[me_t, me_r, :, 128 * i : 128 * i + 128] = tile.astype(BF16)
    for (jo, _), run, start in zip(p.blocks, p.runs, p.starts):
        w2b[me_r, pl.ds(pl.multiple_of(jo + run * me_t, run), run), :] = m2[start : start + run, :].astype(BF16)

    pl.semaphore_wait(barrier, nt + nr - 2)

    def halo_sends():
        after, before = (me_t + 1) % nt, (me_t + nt - 1) % nt
        return [
            remote(frames_hbm.at[0, pl.ds(t_len - HALO, HALO)], frx.at[pl.ds(0, HALO)], send_sem.at[0], halo_sem.at[0], tm=after),
            remote(frames_hbm.at[0, pl.ds(0, HALO)], frx.at[pl.ds(HALO + t_len, HALO)], send_sem.at[1], halo_sem.at[1], tm=before),
        ]

    def w1_part(j, q):
        jo, size = p.blocks[j]
        return w1b.at[:, q, :, pl.ds(jo, size)]

    def w2_part(j, q):
        jo, size = p.blocks[j]
        return w2b.at[q, pl.ds(jo, size), :]

    def spread_sends(j):
        jo, size = p.blocks[j]
        run = p.runs[j]
        out = []
        for step in range(1, nt):
            peer = (me_t + step) % nt
            one = w1b.at[me_t, me_r, :, pl.ds(jo, size)]
            two = w2b.at[me_r, pl.ds(pl.multiple_of(jo + run * me_t, run), run), :]
            out.append(remote(one, one, send_sem.at[2 + j], ag_sem.at[j, 0], tm=peer))
            out.append(remote(two, two, send_sem.at[2 + j], ag_sem.at[j, 0], tm=peer))
        return out

    def spread_wait(j):
        jo, size = p.blocks[j]
        arrived(w1b.at[pl.ds(0, nt - 1), pl.ds(0, 2), :, pl.ds(jo, size)], ag_sem.at[j, 0])

    def far_sends(j):
        return [
            remote(w1_part(j, me_r), w1_part(j, me_r), send_sem.at[6 + j], ag_sem.at[j, 1], rows=far),
            remote(w2_part(j, me_r), w2_part(j, me_r), send_sem.at[6 + j], ag_sem.at[j, 1], rows=far),
        ]

    def far_wait(j):
        jo, size = p.blocks[j]
        arrived(w1b.at[:, pl.ds(0, 2), :, pl.ds(jo, size)], ag_sem.at[j, 1])

    def near_sends(j, q):
        return [
            remote(w1_part(j, q), w1_part(j, q), send_sem.at[10 + j], ag_sem.at[j, 2], rows=near),
            remote(w2_part(j, q), w2_part(j, q), send_sem.at[10 + j], ag_sem.at[j, 2], rows=near),
        ]

    def near_wait(j):
        jo, size = p.blocks[j]
        arrived(w1b.at[:, :, :, pl.ds(jo, size)], ag_sem.at[j, 2])

    def start(copies):
        for copy in copies:
            copy.start()

    def gather_one(j):
        spread_wait(j)
        start(far_sends(j))
        start(near_sends(j, me_r))

    def gather_two(j):
        far_wait(j)
        start(near_sends(j, far))

    start(halo_sends())
    for j in range(len(p.blocks)):
        start(spread_sends(j))

    loads[2].wait()
    loads[3].wait()

    gain = small_ref[8:9, :]
    shift_row = small_ref[9:10, :]
    scale = small_ref[14:15, :]

    def forward_tile(b):
        row = pl.multiple_of(b * TILE, TILE)
        starts_here = flags[pl.ds(b, 1), :]
        ends_here = flags[pl.ds(b + 1, 1), :]
        lead = frx[pl.ds(row, HALO), :].astype(F32)
        trail = frx[pl.ds(row + HALO + TILE, HALO), :].astype(F32)
        for c in range(p.nc):
            cols = slice(128 * c, 128 * c + 128)
            xf[b, c, GAP : GAP + TILE, :] = frx[pl.ds(row + HALO, TILE), cols].astype(F32)
            xf[b, c, 0:GAP, :] = jnp.where(starts_here > 0.5, 0.0, lead[HALO - GAP :, cols])
            xf[b, c, GAP + TILE :, :] = jnp.where(ends_here > 0.5, 0.0, trail[0:GAP, cols])
        for c in range(p.nc):
            cols = slice(128 * c, 128 * c + 128)
            total = jnp.broadcast_to(small_ref[7:8, cols], (TILE, 128))
            for k in range(TAPS):
                first = GAP - 3 + k
                total = total + small_ref[k : k + 1, cols] * xf[b, c, first : first + TILE, :]
            tmp[:, cols] = total
        step = 32
        for q in range(TILE // step):
            rows = pl.ds(row + q * step, step)
            value = tmp[q * step : q * step + step, :]
            centred = value - jnp.sum(value, axis=1, keepdims=True) * (1.0 / p.d)
            spread = jnp.sum(centred * centred, axis=1, keepdims=True) * (1.0 / p.d)
            inverse = lax.rsqrt(spread + norm_eps)
            unit = centred * inverse
            rstd[rows, :] = jnp.broadcast_to(inverse, (step, 128))
            xhat[rows, :] = unit.astype(BF16)
            nm[rows, :] = (unit * gain + shift_row).astype(BF16)
            low = (scale * ct[rows, :].astype(F32)).astype(BF16)
            gb[rows, :] = low
            accs[10] += fold(low.astype(F32))
        nmt[:, pl.ds(row, TILE)] = nm[pl.ds(row, TILE), :].T
        gbt[:, pl.ds(row, TILE)] = gb[pl.ds(row, TILE), :].T

    def forward_tiles(low, high):
        @pl.loop(low, high)
        def _(b):
            forward_tile(b)

    nb = p.nb
    cut = [1 + (nb - 2) * i // 4 for i in range(5)]
    forward_tiles(cut[0], cut[1])
    gather_one(0)
    forward_tiles(cut[1], cut[2])
    gather_two(0)
    forward_tiles(cut[2], cut[3])
    gather_one(1)
    forward_tiles(cut[3], cut[4])
    arrived(frx.at[pl.ds(0, HALO)], halo_sem.at[0])
    arrived(frx.at[pl.ds(HALO + t_len, HALO)], halo_sem.at[1])

    @pl.loop(0, 2)
    def _(i):
        forward_tile(i * (nb - 1))

    near_wait(0)

    def parts_of(j):
        jo, size = p.blocks[j]
        start_row, run = p.starts[j], p.runs[j]
        return jo, size, start_row, run

    def pair_sends(j):
        jo, size, _, _ = parts_of(j)
        out = []
        for slot, q in ((0, near), (1, both)):
            out.append(remote(s1w1.at[:, q, :, pl.ds(jo, size)], r1w1.at[slot, :, :, pl.ds(jo, size)], send_sem.at[14 + j], rs_sem.at[j, 0], rows=near))
            out.append(remote(s1w2.at[q, pl.ds(jo, size), :], r1w2.at[slot, pl.ds(jo, size), :], send_sem.at[14 + j], rs_sem.at[j, 0], rows=near))
        return out

    def cross_sends(j):
        jo, size, _, _ = parts_of(j)
        return [
            remote(s2w1.at[:, :, pl.ds(jo, size)], r2w1.at[:, :, pl.ds(jo, size)], send_sem.at[18 + j], rs_sem.at[j, 1], rows=far),
            remote(s2w2.at[pl.ds(jo, size), :], r2w2.at[pl.ds(jo, size), :], send_sem.at[18 + j], rs_sem.at[j, 1], rows=far),
        ]

    def holder_sends(j):
        jo, size, start_row, run = parts_of(j)
        out = []
        for step in range(1, nt):
            peer = (me_t + step) % nt
            out.append(remote(s3w1.at[peer, :, pl.ds(jo, size)], r3w1.at[me_t, :, pl.ds(jo, size)], send_sem.at[22 + j], rs_sem.at[j, 2], tm=peer))
            out.append(remote(s3w2.at[pl.ds(pl.multiple_of(jo + run * peer, run), run), :], r3w2.at[me_t, pl.ds(start_row, run), :], send_sem.at[22 + j], rs_sem.at[j, 2], tm=peer))
        return out

    def final_sends(j):
        jo, size, start_row, run = parts_of(j)
        out = []
        for step in range(1, nr):
            peer = (me_r + step) % nr
            one = finw1.at[me_r, :, pl.ds(jo, size)]
            two = finw2.at[me_r, pl.ds(start_row, run), :]
            out.append(remote(one, one, send_sem.at[26 + j], rs_sem.at[j, 3], rows=peer))
            out.append(remote(two, two, send_sem.at[26 + j], rs_sem.at[j, 3], rows=peer))
        return out

    def sum_zero(j):
        jo, size, _, _ = parts_of(j)
        one = acc1[:, 0:size].astype(BF16).reshape(nt, nr, p.part, size)
        s1w1[:, :, :, pl.ds(jo, size)] = one
        two = acc2[:, 0:size].astype(BF16).T
        for q in range(nr):
            s1w2[q, pl.ds(jo, size), :] = two[:, p.lanes * q : p.lanes * q + p.lanes]
        start(pair_sends(j))

    def sum_one(j):
        jo, size, _, _ = parts_of(j)
        cols = pl.ds(jo, size)
        arrived(s1w1.at[:, :, :, cols], rs_sem.at[j, 0])
        one = s1w1[:, far, :, cols].astype(F32) + r1w1[1, :, :, cols].astype(F32)
        s2w1[:, :, cols] = one.astype(BF16)
        two = s1w2[far, cols, :].astype(F32) + r1w2[1, cols, :].astype(F32)
        s2w2[cols, :] = two.astype(BF16)
        start(cross_sends(j))

    def sum_two(j):
        jo, size, start_row, run = parts_of(j)
        cols = pl.ds(jo, size)
        arrived(s1w1.at[:, pl.ds(0, 2), :, cols], rs_sem.at[j, 1])
        one = s1w1[:, me_r, :, cols].astype(F32) + r1w1[0, :, :, cols].astype(F32) + r2w1[:, :, cols].astype(F32)
        s3w1[:, :, cols] = one.astype(BF16)
        two = s1w2[me_r, cols, :].astype(F32) + r1w2[0, cols, :].astype(F32) + r2w2[cols, :].astype(F32)
        s3w2[cols, :] = two.astype(BF16)
        r3w1[me_t, :, cols] = s3w1[me_t, :, cols]
        r3w2[me_t, pl.ds(start_row, run), :] = s3w2[pl.ds(pl.multiple_of(jo + run * me_t, run), run), :]
        start(holder_sends(j))

    def sum_three(j):
        jo, size, start_row, run = parts_of(j)
        cols = pl.ds(jo, size)
        arrived(s1w1.at[pl.ds(0, nt - 1), pl.ds(0, 2), :, cols], rs_sem.at[j, 2])
        one = r3w1[0, :, cols].astype(F32)
        two = r3w2[0, pl.ds(start_row, run), :].astype(F32)
        for k in range(1, nt):
            one = one + r3w1[k, :, cols].astype(F32)
            two = two + r3w2[k, pl.ds(start_row, run), :].astype(F32)
        finw1[me_r, :, cols] = one
        finw2[me_r, pl.ds(start_row, run), :] = two
        start(final_sends(j))

    def sum_wait(j):
        jo, size, _, _ = parts_of(j)
        arrived(s1w1.at[pl.ds(0, 3 * nt // 4), pl.ds(0, 2), :, pl.ds(jo, size)], rs_sem.at[j, 3])

    m = p.m
    per = m // TILE

    def rows_add(ref, i, value, first):
        for s in range(per):
            for c in range(p.nc):
                piece = value[TILE * s : TILE * s + TILE, 128 * c : 128 * c + 128]
                place = (i * per + s, c, slice(GAP, GAP + TILE), slice(None))
                ref[place] = piece if first else ref[place] + piece

    def main_block(j, between):
        jo, size = p.blocks[j]
        cols = pl.ds(jo, size)
        acc1[:, 0:size] = jnp.zeros((p.d, size), F32)
        acc2[:, 0:size] = jnp.zeros((p.d, size), F32)

        @pl.loop(0, t_len // m)
        def _(i):
            for at, task in between:
                pl.when(i == at)(task)
            rows = pl.ds(pl.multiple_of(i * m, m), m)
            w1 = w1b[:, :, :, cols].reshape(p.d, size)
            w2 = jnp.concatenate([w2b[q, cols, :] for q in range(nr)], axis=1)
            hidden = jnp.dot(nm[rows, :], w1, preferred_element_type=F32) + b1p[0:1, cols]
            grad_act = lax.dot_general(
                gb[rows, :], w2, (((1,), (1,)), ((), ())), preferred_element_type=F32
            )
            prob = 0.5 * (1.0 + lax.erf(hidden * RSQRT_HALF))
            bell = jnp.exp(hidden * hidden * np.float32(-0.5)) * RSQRT_2PI
            act = (hidden * prob).astype(BF16)
            grad_hidden = (grad_act * (prob + hidden * bell)).astype(BF16)
            accb[:, cols] += fold(grad_hidden.astype(F32))
            rows_add(br, i, jnp.dot(act, w2, preferred_element_type=F32), j == 0)
            back = lax.dot_general(
                grad_hidden, w1, (((1,), (1,)), ((), ())), preferred_element_type=F32
            )
            gn[rows, :] = back if j == 0 else gn[rows, :] + back
            acc1[:, 0:size] += jnp.dot(nmt[:, rows], grad_hidden, preferred_element_type=F32)
            acc2[:, 0:size] += jnp.dot(gbt[:, rows], act, preferred_element_type=F32)

    main_block(0, [(1, lambda: gather_two(1)), (2, lambda: gather_one(2))])
    sum_zero(0)
    near_wait(1)
    main_block(
        1, [(0, lambda: gather_two(2)), (1, lambda: sum_one(0)), (1, lambda: gather_one(3)), (2, lambda: sum_two(0)), (2, lambda: gather_two(3))]
    )
    sum_zero(1)
    near_wait(2)
    main_block(2, [(0, lambda: sum_three(0)), (1, lambda: sum_one(1))])
    sum_zero(2)
    sum_two(1)
    near_wait(3)
    main_block(3, [(1, lambda: sum_one(2)), (2, lambda: sum_three(1))])
    sum_zero(3)
    sum_two(2)

    def output_copy(b):
        rows = pl.ds(pl.multiple_of(b * TILE, TILE), TILE)
        return pltpu.make_async_copy(nm.at[rows], output_hbm.at[0, rows], out_sem.at[0])

    def ingrad_copy(b):
        rows = pl.ds(pl.multiple_of(b * TILE, TILE), TILE)
        return pltpu.make_async_copy(gb.at[rows], ingrad_hbm.at[0, rows], out_sem.at[1])

    bias_two = small_ref[13:14, :]

    def backward_tile(b):
        row = pl.multiple_of(b * TILE, TILE)
        step = 32
        for q in range(TILE // step):
            rows = pl.ds(row + q * step, step)
            place = slice(GAP + q * step, GAP + q * step + step)
            branch = jnp.concatenate([br[b, c, place, :] for c in range(p.nc)], axis=1) + bias_two
            source = frx[pl.ds(row + HALO + q * step, step), :].astype(F32)
            nm[rows, :] = (source + scale * branch).astype(BF16)
            accs[11] += fold(ct[rows, :].astype(F32) * branch)
            grad = gn[rows, :]
            unit = xhat[rows, :].astype(F32)
            accs[8] += fold(grad * unit)
            accs[9] += fold(grad)
            u = grad * gain
            mean_u = jnp.sum(u, axis=1, keepdims=True) * (1.0 / p.d)
            mean_x = jnp.sum(u * unit, axis=1, keepdims=True) * (1.0 / p.d)
            inverse = rstd[rows, :]
            inverse = jnp.concatenate([inverse] * p.nc, axis=1)
            low = ((u - mean_u - unit * mean_x) * inverse).astype(BF16).astype(F32)
            accs[7] += fold(low)
            for c in range(p.nc):
                br[b, c, place, :] = low[:, 128 * c : 128 * c + 128]
        for c in range(p.nc):
            cols = slice(128 * c, 128 * c + 128)
            low = br[b, c, GAP : GAP + TILE, :]
            for k in range(TAPS):
                first = GAP - 3 + k
                accs[k, :, cols] += fold(low * xf[b, c, first : first + TILE, :])
        output_copy(b).start()

    def backward_tiles(low, high):
        @pl.loop(low, high)
        def _(b):
            backward_tile(b)

    def edge_sends():
        after, before = (me_t + 1) % nt, (me_t + nt - 1) % nt
        return [
            remote(br.at[nb - 1, :, pl.ds(TILE, GAP), :], hprev, send_sem.at[30], halo_sem.at[2], tm=after),
            remote(br.at[0, :, pl.ds(GAP, GAP), :], hnext, send_sem.at[31], halo_sem.at[3], tm=before),
        ]

    @pl.loop(0, 2)
    def _(i):
        backward_tile(i * (nb - 1))

    start(edge_sends())
    sum_one(3)
    cut = [1 + (nb - 2) * i // 4 for i in range(5)]
    backward_tiles(cut[0], cut[1])
    sum_three(2)
    backward_tiles(cut[1], cut[2])
    sum_two(3)
    backward_tiles(cut[2], cut[4])
    sum_three(3)

    hidden_tiles = lane_permuted(lambda i: accb[:, 128 * i : 128 * i + 128], p.regrouped, p.ff // 128)
    for c in range(p.nc):
        cols = slice(128 * c, 128 * c + 128)
        line = []
        for k in range(10):
            line.append(jnp.sum(accs[k, :, cols], axis=0, keepdims=True))
        for i in range(3):
            line.append(jnp.sum(hidden_tiles[i * p.nc + c], axis=0, keepdims=True))
        for k in (10, 11):
            line.append(jnp.sum(accs[k, :, cols], axis=0, keepdims=True))
        line.append(jnp.zeros((1, 128), F32))
        sma[c] = jnp.concatenate(line, axis=0)

    def small_one_sends():
        out = []
        for step in range(1, nr):
            peer = (me_r + step) % nr
            out.append(remote(sma.at[peer], smr.at[me_r], send_sem.at[32], sm_sem.at[0], rows=peer))
        return out

    def small_two_sends():
        out = []
        for step in range(1, nt):
            peer = (me_t + step) % nt
            out.append(remote(smq.at[nt], smq.at[me_t], send_sem.at[33], sm_sem.at[1], tm=peer))
        return out

    def small_three_sends():
        out = []
        for step in range(1, nr):
            peer = (me_r + step) % nr
            out.append(remote(smf.at[me_r], smf.at[me_r], send_sem.at[34], sm_sem.at[2], rows=peer))
        return out

    smr[me_r] = sma[me_r]
    start(small_one_sends())

    def small_two():
        arrived(smr.at[pl.ds(0, nr - 1)], sm_sem.at[0])
        total = smr[0]
        for k in range(1, nr):
            total = total + smr[k]
        smq[nt] = total
        smq[me_t] = total
        start(small_two_sends())

    def small_three():
        arrived(smq.at[pl.ds(0, nt - 1)], sm_sem.at[1])
        total = smq[0]
        for k in range(1, nt):
            total = total + smq[k]
        smf[me_r] = total
        start(small_three_sends())

    def exchange_edges(b):
        same = flags[pl.ds(b, 1), :] < 0.5
        for c in range(p.nc):
            br[b, c, 0:GAP, :] = jnp.where(same, br[b - 1, c, TILE : TILE + GAP, :], 0.0)
            br[b - 1, c, GAP + TILE :, :] = jnp.where(same, br[b, c, GAP : GAP + GAP, :], 0.0)

    def input_tile(b):
        row = pl.multiple_of(b * TILE, TILE)
        for c in range(p.nc):
            cols = slice(128 * c, 128 * c + 128)
            total = ct[pl.ds(row, TILE), cols].astype(F32)
            for k in range(TAPS):
                first = GAP + 3 - k
                total = total + small_ref[k : k + 1, cols] * br[b, c, first : first + TILE, :]
            gb[pl.ds(row, TILE), cols] = total.astype(BF16)
        ingrad_copy(b).start()

    exchange_edges(1)

    def input_tiles(low, high):
        @pl.loop(low, high)
        def _(b):
            exchange_edges(b + 1)
            input_tile(b)

    cut = [1 + (nb - 2) * i // 4 for i in range(5)]
    input_tiles(cut[0], cut[1])
    small_two()
    input_tiles(cut[1], cut[3])
    small_three()
    input_tiles(cut[3], cut[4])
    arrived(hprev, halo_sem.at[2])
    arrived(hnext, halo_sem.at[3])
    for c in range(p.nc):
        br[0, c, 0:GAP, :] = jnp.where(flags[0:1, :] < 0.5, hprev[c], 0.0)
        br[nb - 1, c, GAP + TILE :, :] = jnp.where(flags[nb : nb + 1, :] < 0.5, hnext[c], 0.0)

    @pl.loop(0, 2)
    def _(i):
        input_tile(i * (nb - 1))

    for j in range(len(p.blocks)):
        sum_wait(j)
    for q in range(nr):
        tiles = lane_permuted(lambda i, q=q: finw1[q, :, 128 * i : 128 * i + 128], p.regrouped, p.ff // 128)
        for i, tile in enumerate(tiles):
            g1_out[p.part * q : p.part * q + p.part, 128 * i : 128 * i + 128] = tile
        g2_out[:, p.lanes * q : p.lanes * q + p.lanes] = finw2[q]
    arrived(smf.at[pl.ds(0, nr - 1)], sm_sem.at[2])
    for c in range(p.nc):
        small_out[:, 128 * c : 128 * c + 128] = smf[c]

    sent = halo_sends() + edge_sends() + small_one_sends() + small_two_sends() + small_three_sends()
    for j in range(len(p.blocks)):
        sent += spread_sends(j) + far_sends(j) + near_sends(j, me_r) + near_sends(j, far)
        sent += pair_sends(j) + cross_sends(j) + holder_sends(j) + final_sends(j)
    for copy in sent:
        copy.wait_send()
    whole = pl.ds(0, t_len)
    pltpu.make_async_copy(nm.at[whole], output_hbm.at[0, whole], out_sem.at[0]).wait()
    pltpu.make_async_copy(gb.at[whole], ingrad_hbm.at[0, whole], out_sem.at[1]).wait()


def call(plan, frames, cotangent, lengths, w1_master, w2_master, small_master):
    p = plan
    t, d, ff, nt, nr, nb, nc = p.t, p.d, p.ff, p.nt, p.nr, p.nb, p.nc
    vmem = pl.BlockSpec(memory_space=pltpu.VMEM)
    anyplace = pl.BlockSpec(memory_space=pl.ANY)
    n_lens = -(-lengths.shape[1] // 128) * 128
    v = pltpu.VMEM
    scratch = [
        v((t + 2 * HALO, d), BF16),
        v((t, d), BF16),
        v((t, d), BF16),
        v((d, t), BF16),
        v((t, d), BF16),
        v((d, t), BF16),
        v((nb, nc, TILE + 2 * GAP, 128), F32),
        v((t, d), F32),
        v((nb, nc, TILE + 2 * GAP, 128), F32),
        v((t, d), BF16),
        v((t, 128), F32),
        v((nt, nr, p.part, ff), BF16),
        v((nr, ff, p.lanes), BF16),
        v((p.part, ff), F32),
        v((p.share, p.lanes), F32),
        v((d, p.widest), F32),
        v((d, p.widest), F32),
        v((8, n_lens), F32),
        v((-(-(nb + 1) // 8) * 8, 128), F32),
        v((8, ff), F32),
        v((12, 8, d), F32),
        v((8, ff), F32),
        v((TILE, d), F32),
        v((nt, nr, p.part, ff), BF16),
        v((nr, ff, p.lanes), BF16),
        v((2, nt, p.part, ff), BF16),
        v((2, ff, p.lanes), BF16),
        v((nt, p.part, ff), BF16),
        v((ff, p.lanes), BF16),
        v((nt, p.part, ff), BF16),
        v((ff, p.lanes), BF16),
        v((nt, p.part, ff), BF16),
        v((ff, p.lanes), BF16),
        v((nt, p.part, ff), BF16),
        v((nt, p.share, p.lanes), BF16),
        v((nr, p.part, ff), F32),
        v((nr, p.share, p.lanes), F32),
        v((nr, 16, p.lanes), F32),
        v((nr, 16, p.lanes), F32),
        v((nt + 1, 16, p.lanes), F32),
        v((nr, 16, p.lanes), F32),
        v((nc, GAP, 128), F32),
        v((nc, GAP, 128), F32),
        pltpu.SemaphoreType.DMA((4,)),
        pltpu.SemaphoreType.DMA((2,)),
        pltpu.SemaphoreType.DMA((35,)),
        pltpu.SemaphoreType.DMA((4,)),
        pltpu.SemaphoreType.DMA((4, 3)),
        pltpu.SemaphoreType.DMA((4, 4)),
        pltpu.SemaphoreType.DMA((3,)),
    ]
    return pl.pallas_call(
        functools.partial(kernel, plan),
        out_shape=(
            jax.ShapeDtypeStruct((1, t, d), BF16),
            jax.ShapeDtypeStruct((1, t, d), BF16),
            jax.ShapeDtypeStruct((p.rows1, ff), F32),
            jax.ShapeDtypeStruct((p.share, d), F32),
            jax.ShapeDtypeStruct((16, d), F32),
        ),
        in_specs=[anyplace, anyplace, vmem, anyplace, anyplace, vmem],
        out_specs=(anyplace, anyplace, vmem, vmem, vmem),
        scratch_shapes=scratch,
        compiler_params=pltpu.CompilerParams(
            collective_id=0, has_side_effects=True, vmem_limit_bytes=67_000_000
        ),
    )(frames, cotangent, lengths, w1_master, w2_master, small_master)


def padded_2(array, sides, width):
    for axis, dim in sides:
        devices, length = (lax.axis_size(axis), array.shape[dim])
        up = [(i, (i + 1) % devices) for i in range(devices - 1)]
        down = [(j, i) for i, j in up]
        last = lax.slice_in_dim(array, length - width, length, axis=dim)
        leading = lax.slice_in_dim(array, 0, width, axis=dim)
        before = lax.ppermute(last, axis, up)
        after = lax.ppermute(leading, axis, down)
        array = jnp.concatenate([before, array, after], axis=dim)
    return array


def cut_along(array, dim, devices):
    before, after = (array.shape[:dim], array.shape[dim + 1 :])
    return jnp.moveaxis(array.reshape(*before, devices, -1, *after), dim, 0)


def sent_and_summed(array, axis, dim):
    devices = lax.axis_size(axis)
    pieces = lax.all_to_all(cut_along(array, dim, devices), axis, 0, 0, tiled=True)
    return jnp.sum(pieces.astype(jnp.float32), axis=0)


def edge_masks(lengths_row, first_frame, frame_count):
    ends_at = jnp.cumsum(lengths_row, dtype=jnp.int32)
    places = first_frame + jnp.arange(frame_count, dtype=jnp.int32)
    passed = ends_at[None, :] <= places[:, None]
    lower = jnp.max(jnp.where(passed, ends_at[None, :], 0), axis=1)
    upper = jnp.min(jnp.where(passed, ends_at[-1], ends_at[None, :]), axis=1)
    mask_rows = []
    for tap_index in range(7):
        spot_now = places + (tap_index - 3)
        mask_rows.append(((spot_now >= lower) & (spot_now < upper)).astype(jnp.float32))
    return jnp.stack(mask_rows)


def depthwise(padded, tap_rows, masks, frame_count):
    summed = jnp.zeros((frame_count, padded.shape[1]), jnp.float32)
    for tap_index in range(7):
        window = padded[tap_index : tap_index + frame_count].astype(jnp.float32)
        summed = summed + tap_rows[tap_index][None, :] * window * masks[tap_index][:, None]
    return summed


def layer_norm(conv_out, norm_gain, norm_bias):
    centred = conv_out - jnp.mean(conv_out, axis=-1, keepdims=True)
    spread = jnp.mean(centred * centred, axis=-1, keepdims=True)
    return centred * lax.rsqrt(spread + norm_eps) * norm_gain[None, :] + norm_bias[None, :]


def exact_gelu(values):
    return jax.nn.gelu(values, approximate=False)


def frame_product(left_side, right_side):
    return lax.dot_general(
        left_side, right_side, (((0,), (0,)), ((), ())), preferred_element_type=jnp.float32
    )


def plain_body(
    frames,
    cotangent,
    lengths,
    w1_master,
    w1_first,
    w1_second,
    w1_average,
    w2_master,
    w2_first,
    w2_second,
    w2_average,
    small_master,
    small_first,
    small_second,
    small_average,
):
    frame_count = frames.shape[1]
    width = frames.shape[2]
    w1_low, w2_low = (
        lax.all_gather(w1_master.astype(jnp.bfloat16), "tm", axis=0, tiled=True),
        lax.all_gather(w2_master.astype(jnp.bfloat16), "tm", axis=0, tiled=True),
    )
    inputs = frames[0]
    upstream = cotangent[0].astype(jnp.float32)
    masks = edge_masks(lengths[0], lax.axis_index("tm") * frame_count, frame_count)
    tap_rows = small_master[0:7]
    layer_scale = small_master[14]
    padded = padded_2(inputs, (("tm", 0),), 3)
    conv_out = depthwise(padded, tap_rows, masks, frame_count) + small_master[7][None, :]
    normed, norm_back = jax.vjp(layer_norm, conv_out, small_master[8], small_master[9])
    normed_low = normed.astype(jnp.bfloat16)
    hidden = (
        jnp.dot(normed_low, w1_low, preferred_element_type=jnp.float32)
        + small_master[10:13].reshape(-1)[None, :]
    )
    activated, gelu_back = jax.vjp(exact_gelu, hidden)
    act_low = activated.astype(jnp.bfloat16)
    branch = (
        jnp.dot(act_low, w2_low, preferred_element_type=jnp.float32) + small_master[13][None, :]
    )
    output = (inputs.astype(jnp.float32) + layer_scale[None, :] * branch).astype(jnp.bfloat16)
    grad_scale = jnp.sum(upstream * branch, axis=0)
    grad_branch = (layer_scale[None, :] * upstream).astype(jnp.bfloat16)
    grad_act = lax.dot_general(
        grad_branch, w2_low, (((1,), (1,)), ((), ())), preferred_element_type=jnp.float32
    )
    grad_hidden = gelu_back(grad_act)[0].astype(jnp.bfloat16)
    grad_normed = lax.dot_general(
        grad_hidden, w1_low, (((1,), (1,)), ((), ())), preferred_element_type=jnp.float32
    )
    grad_conv, grad_gain, grad_shift = norm_back(grad_normed)
    grad_low = grad_conv.astype(jnp.bfloat16)
    grad_pad = padded_2(grad_low, (("tm", 0),), 3)
    input_grad = (upstream + depthwise(grad_pad, tap_rows[::-1], masks, frame_count)).astype(
        jnp.bfloat16
    )
    grad_float = grad_low.astype(jnp.float32)
    grad_taps = jnp.stack(
        [
            jnp.sum(
                grad_float
                * padded[tap_index : tap_index + frame_count].astype(jnp.float32)
                * masks[tap_index][:, None],
                axis=0,
            )
            for tap_index in range(7)
        ]
    )
    middle_rows = jnp.stack([jnp.sum(grad_float, axis=0), grad_gain, grad_shift])
    bias_rows = jnp.sum(grad_hidden.astype(jnp.float32), axis=0).reshape(3, width)
    last_rows = jnp.stack([jnp.sum(grad_branch.astype(jnp.float32), axis=0), grad_scale])
    small_grad = jnp.concatenate([grad_taps, middle_rows, bias_rows, last_rows], axis=0)
    full_one = frame_product(normed_low, grad_hidden)
    full_two = frame_product(act_low, grad_branch)
    share_one, share_two = (
        sent_and_summed(full_one.astype(jnp.bfloat16), "tm", 0),
        sent_and_summed(full_two.astype(jnp.bfloat16), "tm", 0),
    )
    grad_one, grad_two = (
        lax.psum(share_one.astype(jnp.bfloat16), "rows").astype(jnp.float32),
        lax.psum(share_two.astype(jnp.bfloat16), "rows").astype(jnp.float32),
    )
    small_total = lax.psum(small_grad, ("tm", "rows"))
    one_out = adamw_step(w1_master, w1_first, w1_second, w1_average, grad_one, rate_first)
    two_out = adamw_step(w2_master, w2_first, w2_second, w2_average, grad_two, rate_second)
    small_out = adamw_step(
        small_master, small_first, small_second, small_average, small_total, rate_small
    )
    return (
        output[None],
        input_grad[None],
        one_out[0],
        one_out[1],
        one_out[2],
        one_out[3],
        one_out[4],
        two_out[0],
        two_out[1],
        two_out[2],
        two_out[3],
        two_out[4],
        small_out[0],
        small_out[1],
        small_out[2],
        small_out[3],
        small_out[4],
    )


def body(
    frames,
    cotangent,
    lengths,
    w1_master,
    w1_first,
    w1_second,
    w1_average,
    w2_master,
    w2_first,
    w2_second,
    w2_average,
    small_master,
    small_first,
    small_second,
    small_average,
):
    nt, nr = lax.axis_size("tm"), lax.axis_size("rows")
    plan = Plan(nt, nr, frames.shape[1], frames.shape[2], w1_master.shape[1])
    output, input_grad, grad_one, grad_two, small_total = call(
        plan, frames, cotangent, lengths, w1_master, w2_master, small_master
    )
    one_out = adamw_step(w1_master, w1_first, w1_second, w1_average, grad_one, rate_first)
    two_out = adamw_step(w2_master, w2_first, w2_second, w2_average, grad_two, rate_second)
    small_out = adamw_step(
        small_master, small_first, small_second, small_average, small_total[:15], rate_small
    )
    return (output, input_grad, *one_out, *two_out, *small_out)


def solution(mesh):
    in_specs = (
        P("rows", "tm", None),
        P("rows", "tm", None),
        P("rows", None),
        P("tm", None),
        P("tm", None),
        P("tm", None),
        P("tm", None),
        P("tm", None),
        P("tm", None),
        P("tm", None),
        P("tm", None),
        P(),
        P(),
        P(),
        P(),
    )
    out_specs = (
        P("rows", "tm", None),
        P("rows", "tm", None),
        P("tm", None),
        P("tm", None),
        P("tm", None),
        P("tm", None),
        P("tm", None),
        P("tm", None),
        P("tm", None),
        P("tm", None),
        P("tm", None),
        P("tm", None),
        P(),
        P(),
        P(),
        P(),
        P(),
    )
    fits = mesh.shape["tm"] == 8 and mesh.shape["rows"] == 4
    return jax.shard_map(body if fits else plain_body, mesh=mesh, in_specs=in_specs, out_specs=out_specs, check_vma=False)
```

```python
import functools

import jax
import jax.numpy as jnp
import numpy as np
from jax import lax
from jax.experimental import pallas as pl
from jax.experimental.pallas import tpu as pltpu
from jax.sharding import PartitionSpec as P

ADAM_STEP = 3
norm_eps = 1e-06
adam_eps = 1e-08
weight_decay = 0.01
beta_first = 0.5
beta_second = 0.5
average_keep = 0.75
rate_first = 0.08
rate_second = 0.05
rate_small = 0.4

TAPS = 7
TILE = 128
GAP = 8
GRAIN = 32
HALO = 16
F32 = jnp.float32
BF16 = jnp.bfloat16
MESH = pl.DeviceIdType.MESH
RSQRT_HALF = np.float32(0.7071067811865476)
RSQRT_2PI = np.float32(0.3989422804014327)


def adamw_step(master, first_old, second_old, average_old, gradient, rate):
    first_new = beta_first * first_old + (1.0 - beta_first) * gradient
    second_new = beta_second * second_old + (1.0 - beta_second) * gradient * gradient
    first_hat = first_new / (1.0 - beta_first**ADAM_STEP)
    second_hat = second_new / (1.0 - beta_second**ADAM_STEP)
    master_new = master - rate * (
        first_hat / (jnp.sqrt(second_hat) + adam_eps) + weight_decay * master
    )
    average_new = average_keep * average_old + (1.0 - average_keep) * master_new
    return (master_new, first_new, second_new, average_new, master_new.astype(BF16))


class Plan:
    def __init__(self, nt, nr, frame_count, width, hidden):
        self.nt, self.nr, self.t, self.d, self.ff = nt, nr, frame_count, width, hidden
        self.share = hidden // nt
        self.rows1 = width // nt
        self.part = self.rows1 // nr
        self.lanes = width // nr
        self.nb = frame_count // TILE
        self.nc = width // 128
        self.runs = [32, 32, 64, 32, 32]
        self.starts = [0, 32, 64, 128, 160]
        self.blocks = []
        offset = 0
        for run in self.runs:
            self.blocks.append((offset, run * nt))
            offset += run * nt
        self.widest = max(size for _, size in self.blocks)
        self.m = 1024
        self.natural = []
        for run, start in zip(self.runs, self.starts):
            for k in range(nt):
                for o in range(0, run, GRAIN):
                    self.natural.append((self.share * k + start + o) // GRAIN)
        self.regrouped = [self.natural.index(g) for g in range(hidden // GRAIN)]


def lane_permuted(tile_of, source, count):
    per = 128 // GRAIN
    out = []
    for tile in range(count):
        value = None
        for q in range(per):
            run = source[tile * per + q]
            piece = tile_of(run // per)
            shift = ((q - run % per) % per) * GRAIN
            if shift:
                piece = pltpu.roll(piece, shift, 1)
            if value is None:
                value = piece
            else:
                lane = lax.broadcasted_iota(jnp.int32, piece.shape, 1)
                value = jnp.where(lane >= q * GRAIN, piece, value)
        out.append(value)
    return out


def fold(value):
    rows = value.shape[0]
    total = value[0:8]
    for g in range(1, rows // 8):
        total = total + value[8 * g : 8 * g + 8]
    return total


def kernel(
    plan,
    frames_hbm,
    cot_hbm,
    lengths_ref,
    w1_hbm,
    w1_first_hbm,
    w1_second_hbm,
    w1_average_hbm,
    w2_hbm,
    w2_first_hbm,
    w2_second_hbm,
    w2_average_hbm,
    small_ref,
    nm,
    gb,
    g1_out,
    g2_out,
    small_out,
    state1,
    state2,
    frx,
    ct,
    nmt,
    gbt,
    br,
    gn,
    xf,
    xhat,
    rstd,
    w1b,
    w2b,
    acc1,
    acc2,
    lens,
    flags,
    b1p,
    accs,
    accb,
    tmp,
    s1w1,
    s1w2,
    r1w1,
    r1w2,
    r2w1,
    r2w2,
    r3w1,
    r3w2,
    finw1,
    finw2,
    sma,
    smr,
    smq,
    smf,
    hprev,
    hnext,
    in_sem,
    send_sem,
    halo_sem,
    ag_sem,
    rs_sem,
    sm_sem,
):
    p = plan
    nt, nr, t_len = p.nt, p.nr, p.t
    me_t = lax.axis_index("tm")
    me_r = lax.axis_index("rows")
    near = me_r + 1 - 2 * (me_r % 2)
    far = (me_r + 2) % nr
    both = near + 2 - 4 * (near // 2)

    def remote(src, dst, send, recv, tm=None, rows=None):
        device = {"tm": me_t if tm is None else tm, "rows": me_r if rows is None else rows}
        return pltpu.make_async_remote_copy(
            src_ref=src, dst_ref=dst, send_sem=send, recv_sem=recv,
            device_id=device, device_id_type=MESH,
        )

    def arrived(view, sem):
        pltpu.make_async_copy(view, view, sem).wait()

    loads = [
        pltpu.make_async_copy(w1_hbm, state1.at[0], in_sem.at[0]),
        pltpu.make_async_copy(w2_hbm, state2.at[0], in_sem.at[1]),
        pltpu.make_async_copy(frames_hbm.at[0], frx.at[pl.ds(HALO, t_len)], in_sem.at[2]),
        pltpu.make_async_copy(cot_hbm.at[0], ct, in_sem.at[3]),
    ]
    for load in loads:
        load.start()

    barrier = pltpu.get_barrier_semaphore()
    for step in range(1, nt):
        pl.semaphore_signal(
            barrier, inc=1, device_id={"tm": (me_t + step) % nt, "rows": me_r}, device_id_type=MESH
        )
    for step in range(1, nr):
        pl.semaphore_signal(
            barrier, inc=1, device_id={"tm": me_t, "rows": (me_r + step) % nr}, device_id_type=MESH
        )

    lens[...] = jnp.zeros_like(lens)
    n_len = lengths_ref.shape[1]
    lens[0:1, 0:n_len] = lengths_ref[...].astype(F32)
    ends = lens[...]
    lane = lax.broadcasted_iota(jnp.int32, ends.shape, 1)
    shift = 1
    while shift < lens.shape[1]:
        ends = ends + jnp.where(lane >= shift, pltpu.roll(ends, shift, 1), 0.0)
        shift *= 2
    n_flag = flags.shape[0]
    spot = me_t * t_len + TILE * lax.broadcasted_iota(jnp.int32, (n_flag, lens.shape[1]), 0)
    hit = (ends[0:1, :] == spot.astype(F32)) | (spot == 0)
    edge = jnp.max(jnp.where(hit, 1.0, 0.0), axis=1, keepdims=True)
    flags[...] = jnp.broadcast_to(edge, flags.shape)
    accs[...] = jnp.zeros_like(accs)
    accb[...] = jnp.zeros_like(accb)
    bias_tiles = lane_permuted(
        lambda i: jnp.broadcast_to(small_ref[10 + i // p.nc : 11 + i // p.nc, 128 * (i % p.nc) : 128 * (i % p.nc) + 128], (8, 128)),
        p.natural,
        p.ff // 128,
    )
    for i, tile in enumerate(bias_tiles):
        b1p[:, 128 * i : 128 * i + 128] = tile

    loads[0].wait()
    loads[1].wait()
    own_rows = pl.ds(pl.multiple_of(me_r * p.part, p.part), p.part)
    own_lanes = pl.ds(pl.multiple_of(me_r * p.lanes, p.lanes), p.lanes)
    own1 = lane_permuted(lambda i: state1[0, own_rows, 128 * i : 128 * i + 128], p.natural, p.ff // 128)
    for i, tile in enumerate(own1):
        w1b[me_t, me_r, :, 128 * i : 128 * i + 128] = tile.astype(BF16)
    for (jo, _), run, start in zip(p.blocks, p.runs, p.starts):
        w2b[me_r, pl.ds(pl.multiple_of(jo + run * me_t, run), run), :] = state2[0, start : start + run, own_lanes].astype(BF16)

    pl.semaphore_wait(barrier, nt + nr - 2)

    def halo_sends():
        after, before = (me_t + 1) % nt, (me_t + nt - 1) % nt
        return [
            remote(frames_hbm.at[0, pl.ds(t_len - HALO, HALO)], frx.at[pl.ds(0, HALO)], send_sem.at[7, 0], halo_sem.at[0], tm=after),
            remote(frames_hbm.at[0, pl.ds(0, HALO)], frx.at[pl.ds(HALO + t_len, HALO)], send_sem.at[7, 1], halo_sem.at[1], tm=before),
        ]

    def w1_part(j, q):
        jo, size = p.blocks[j]
        return w1b.at[:, q, :, pl.ds(jo, size)]

    def w2_part(j, q):
        jo, size = p.blocks[j]
        return w2b.at[q, pl.ds(jo, size), :]

    def spread_sends(j):
        jo, size = p.blocks[j]
        run = p.runs[j]
        out = []
        for step in range(1, nt):
            peer = (me_t + step) % nt
            one = w1b.at[me_t, me_r, :, pl.ds(jo, size)]
            two = w2b.at[me_r, pl.ds(pl.multiple_of(jo + run * me_t, run), run), :]
            out.append(remote(one, one, send_sem.at[0, j], ag_sem.at[j, 0], tm=peer))
            out.append(remote(two, two, send_sem.at[0, j], ag_sem.at[j, 0], tm=peer))
        return out

    def spread_wait(j):
        jo, size = p.blocks[j]
        arrived(w1b.at[pl.ds(0, nt - 1), pl.ds(0, 2), :, pl.ds(jo, size)], ag_sem.at[j, 0])

    def far_sends(j):
        return [
            remote(w1_part(j, me_r), w1_part(j, me_r), send_sem.at[1, j], ag_sem.at[j, 1], rows=far),
            remote(w2_part(j, me_r), w2_part(j, me_r), send_sem.at[1, j], ag_sem.at[j, 1], rows=far),
        ]

    def far_wait(j):
        jo, size = p.blocks[j]
        arrived(w1b.at[:, pl.ds(0, 2), :, pl.ds(jo, size)], ag_sem.at[j, 1])

    def near_sends(j, q):
        return [
            remote(w1_part(j, q), w1_part(j, q), send_sem.at[2, j], ag_sem.at[j, 2], rows=near),
            remote(w2_part(j, q), w2_part(j, q), send_sem.at[2, j], ag_sem.at[j, 2], rows=near),
        ]

    def near_wait(j):
        jo, size = p.blocks[j]
        arrived(w1b.at[:, :, :, pl.ds(jo, size)], ag_sem.at[j, 2])

    def start(copies):
        for copy in copies:
            copy.start()

    def gather_one(j):
        spread_wait(j)
        start(far_sends(j))
        start(near_sends(j, me_r))

    def gather_two(j):
        far_wait(j)
        start(near_sends(j, far))

    start(halo_sends())
    for j in range(len(p.blocks)):
        start(spread_sends(j))

    rest = [
        pltpu.make_async_copy(source, target, in_sem.at[4])
        for source, target in (
            (w1_first_hbm, state1.at[1]),
            (w1_second_hbm, state1.at[2]),
            (w1_average_hbm, state1.at[3]),
            (w2_first_hbm, state2.at[1]),
            (w2_second_hbm, state2.at[2]),
            (w2_average_hbm, state2.at[3]),
        )
    ]
    for load in rest:
        load.start()
    loads[2].wait()
    loads[3].wait()

    gain = small_ref[8:9, :]
    shift_row = small_ref[9:10, :]
    scale = small_ref[14:15, :]

    first_row = jnp.where(lax.broadcasted_iota(jnp.int32, (8, TILE), 0) == 0, 1.0, 0.0).astype(BF16)

    def turn_tile(b):
        row = pl.multiple_of(b * TILE, TILE)
        nmt[:, pl.ds(row, TILE)] = nm[pl.ds(row, TILE), :].T
        gbt[:, pl.ds(row, TILE)] = gb[pl.ds(row, TILE), :].T

    def forward_tile(b, turned=None):
        if turned is not None:
            turn_tile(turned)
        row = pl.multiple_of(b * TILE, TILE)
        starts_here = flags[pl.ds(b, 1), :]
        ends_here = flags[pl.ds(b + 1, 1), :]
        lead = frx[pl.ds(row, HALO), :].astype(F32)
        trail = frx[pl.ds(row + HALO + TILE, HALO), :].astype(F32)
        for c in range(p.nc):
            cols = slice(128 * c, 128 * c + 128)
            xf[b, c, GAP : GAP + TILE, :] = frx[pl.ds(row + HALO, TILE), cols].astype(F32)
            xf[b, c, 0:GAP, :] = jnp.where(starts_here > 0.5, 0.0, lead[HALO - GAP :, cols])
            xf[b, c, GAP + TILE :, :] = jnp.where(ends_here > 0.5, 0.0, trail[0:GAP, cols])
        for c in range(p.nc):
            cols = slice(128 * c, 128 * c + 128)
            total = jnp.broadcast_to(small_ref[7:8, cols], (TILE, 128))
            for k in range(TAPS):
                first = GAP - 3 + k
                total = total + small_ref[k : k + 1, cols] * xf[b, c, first : first + TILE, :]
            tmp[:, cols] = total
        step = 32
        for q in range(TILE // step):
            rows = pl.ds(row + q * step, step)
            value = tmp[q * step : q * step + step, :]
            centred = value - jnp.sum(value, axis=1, keepdims=True) * (1.0 / p.d)
            spread = jnp.sum(centred * centred, axis=1, keepdims=True) * (1.0 / p.d)
            inverse = lax.rsqrt(spread + norm_eps)
            unit = centred * inverse
            rstd[rows, :] = jnp.broadcast_to(inverse, (step, 128))
            xhat[rows, :] = unit.astype(BF16)
            nm[rows, :] = (unit * gain + shift_row).astype(BF16)
            low = (scale * ct[rows, :].astype(F32)).astype(BF16)
            gb[rows, :] = low
        accs[10] += jnp.dot(first_row, gb[pl.ds(row, TILE), :], preferred_element_type=F32)

    def forward_tiles(low, high):
        @pl.loop(low, high)
        def _(b):
            forward_tile(b, b - 1)

    nb = p.nb
    cut = [2, nb * 3 // 8, nb * 5 // 8, nb * 7 // 8, nb]
    forward_tile(1)
    forward_tiles(cut[0], cut[1])
    gather_one(0)
    forward_tiles(cut[1], cut[2])
    gather_one(1)
    forward_tiles(cut[2], cut[3])
    gather_two(0)
    arrived(frx.at[pl.ds(HALO + t_len, HALO)], halo_sem.at[1])
    forward_tiles(cut[3], cut[4])
    arrived(frx.at[pl.ds(0, HALO)], halo_sem.at[0])
    forward_tile(0, nb - 1)
    turn_tile(0)
    near_wait(0)

    def parts_of(j):
        jo, size = p.blocks[j]
        start_row, run = p.starts[j], p.runs[j]
        return jo, size, start_row, run

    def pair_sends(j):
        jo, size, _, _ = parts_of(j)
        out = []
        for slot, q in ((0, near), (1, both)):
            out.append(remote(s1w1.at[:, q, :, pl.ds(jo, size)], r1w1.at[slot, :, :, pl.ds(jo, size)], send_sem.at[3, j], rs_sem.at[j, 0], rows=near))
            out.append(remote(s1w2.at[q, pl.ds(jo, size), :], r1w2.at[slot, pl.ds(jo, size), :], send_sem.at[3, j], rs_sem.at[j, 0], rows=near))
        return out

    def cross_sends(j):
        jo, size, _, _ = parts_of(j)
        return [
            remote(r1w1.at[1, :, :, pl.ds(jo, size)], r2w1.at[:, :, pl.ds(jo, size)], send_sem.at[4, j], rs_sem.at[j, 1], rows=far),
            remote(r1w2.at[1, pl.ds(jo, size), :], r2w2.at[pl.ds(jo, size), :], send_sem.at[4, j], rs_sem.at[j, 1], rows=far),
        ]

    def holder_sends(j):
        jo, size, start_row, run = parts_of(j)
        out = []
        for step in range(1, nt):
            peer = (me_t + step) % nt
            out.append(remote(r1w1.at[0, peer, :, pl.ds(jo, size)], r3w1.at[me_t, :, pl.ds(jo, size)], send_sem.at[5, j], rs_sem.at[j, 2], tm=peer))
            out.append(remote(r1w2.at[0, pl.ds(pl.multiple_of(jo + run * peer, run), run), :], r3w2.at[me_t, pl.ds(start_row, run), :], send_sem.at[5, j], rs_sem.at[j, 2], tm=peer))
        return out

    def final_sends(j):
        jo, size, start_row, run = parts_of(j)
        out = []
        for step in range(1, nr):
            peer = (me_r + step) % nr
            one = finw1.at[me_r, :, pl.ds(jo, size)]
            two = finw2.at[me_r, pl.ds(start_row, run), :]
            out.append(remote(one, one, send_sem.at[6, j], rs_sem.at[j, 3], rows=peer))
            out.append(remote(two, two, send_sem.at[6, j], rs_sem.at[j, 3], rows=peer))
        return out

    def sum_zero(j):
        jo, size, _, _ = parts_of(j)
        one = acc1[:, 0:size].astype(BF16).reshape(nt, nr, p.part, size)
        s1w1[:, :, :, pl.ds(jo, size)] = one
        two = acc2[:, 0:size].astype(BF16).T
        for q in range(nr):
            s1w2[q, pl.ds(jo, size), :] = two[:, p.lanes * q : p.lanes * q + p.lanes]
        start(pair_sends(j))

    def sum_one(j):
        jo, size, _, _ = parts_of(j)
        cols = pl.ds(jo, size)
        arrived(s1w1.at[:, :, :, cols], rs_sem.at[j, 0])
        one = s1w1[:, far, :, cols].astype(F32) + r1w1[1, :, :, cols].astype(F32)
        r1w1[1, :, :, cols] = one.astype(BF16)
        two = s1w2[far, cols, :].astype(F32) + r1w2[1, cols, :].astype(F32)
        r1w2[1, cols, :] = two.astype(BF16)
        start(cross_sends(j))

    def sum_two(j):
        jo, size, start_row, run = parts_of(j)
        cols = pl.ds(jo, size)
        arrived(s1w1.at[:, pl.ds(0, 2), :, cols], rs_sem.at[j, 1])
        one = s1w1[:, me_r, :, cols].astype(F32) + r1w1[0, :, :, cols].astype(F32) + r2w1[:, :, cols].astype(F32)
        r1w1[0, :, :, cols] = one.astype(BF16)
        two = s1w2[me_r, cols, :].astype(F32) + r1w2[0, cols, :].astype(F32) + r2w2[cols, :].astype(F32)
        r1w2[0, cols, :] = two.astype(BF16)
        r3w1[me_t, :, cols] = r1w1[0, me_t, :, cols]
        r3w2[me_t, pl.ds(start_row, run), :] = r1w2[0, pl.ds(pl.multiple_of(jo + run * me_t, run), run), :]
        start(holder_sends(j))

    def sum_three(j):
        jo, size, start_row, run = parts_of(j)
        cols = pl.ds(jo, size)
        arrived(s1w1.at[pl.ds(0, nt - 1), pl.ds(0, 2), :, cols], rs_sem.at[j, 2])
        one = r3w1[0, :, cols].astype(F32)
        two = r3w2[0, pl.ds(start_row, run), :].astype(F32)
        for k in range(1, nt):
            one = one + r3w1[k, :, cols].astype(F32)
            two = two + r3w2[k, pl.ds(start_row, run), :].astype(F32)
        finw1[me_r, :, cols] = one
        finw2[me_r, pl.ds(start_row, run), :] = two
        start(final_sends(j))

    def sum_wait(j):
        jo, size, _, _ = parts_of(j)
        arrived(s1w1.at[pl.ds(0, 3 * nt // 4), pl.ds(0, 2), :, pl.ds(jo, size)], rs_sem.at[j, 3])

    m = p.m
    per = m // TILE

    def rows_add(ref, i, value, first):
        for s in range(per):
            for c in range(p.nc):
                piece = value[TILE * s : TILE * s + TILE, 128 * c : 128 * c + 128]
                place = (i * per + s, c, slice(GAP, GAP + TILE), slice(None))
                ref[place] = piece if first else ref[place] + piece

    def main_block(j, between):
        jo, size = p.blocks[j]
        cols = pl.ds(jo, size)
        acc1[:, 0:size] = jnp.zeros((p.d, size), F32)
        acc2[:, 0:size] = jnp.zeros((p.d, size), F32)

        @pl.loop(0, t_len // m)
        def _(i):
            for at, task in between:
                pl.when(i == at)(task)
            rows = pl.ds(pl.multiple_of(i * m, m), m)
            w1 = w1b[:, :, :, cols].reshape(p.d, size)
            w2 = jnp.concatenate([w2b[q, cols, :] for q in range(nr)], axis=1)
            hidden = jnp.dot(nm[rows, :], w1, preferred_element_type=F32) + b1p[0:1, cols]
            grad_act = lax.dot_general(
                gb[rows, :], w2, (((1,), (1,)), ((), ())), preferred_element_type=F32
            )
            prob = 0.5 * (1.0 + lax.erf(hidden * RSQRT_HALF))
            bell = jnp.exp(hidden * hidden * np.float32(-0.5)) * RSQRT_2PI
            act = (hidden * prob).astype(BF16)
            grad_hidden = (grad_act * (prob + hidden * bell)).astype(BF16)
            accb[:, cols] += fold(grad_hidden.astype(F32))
            branch = jnp.dot(act, w2, preferred_element_type=F32)
            br[rows, :] = branch if j == 0 else br[rows, :] + branch
            back = lax.dot_general(
                grad_hidden, w1, (((1,), (1,)), ((), ())), preferred_element_type=F32
            )
            rows_add(gn, i, back, j == 0)
            acc1[:, 0:size] += jnp.dot(nmt[:, rows], grad_hidden, preferred_element_type=F32)
            acc2[:, 0:size] += jnp.dot(gbt[:, rows], act, preferred_element_type=F32)

    def then(*calls):
        return [(at, functools.partial(task, j)) for at, task, j in calls]

    main_block(0, then((1, gather_two, 1), (2, gather_one, 2)))
    sum_zero(0)
    near_wait(1)
    main_block(1, then((1, sum_one, 0), (2, gather_two, 2), (2, gather_one, 3)))
    sum_zero(1)
    near_wait(2)
    main_block(2, then((1, sum_two, 0), (1, sum_one, 1), (1, gather_one, 4), (2, gather_two, 3)))
    sum_zero(2)
    sum_two(1)
    near_wait(3)
    main_block(3, then((1, sum_one, 2), (1, gather_two, 4), (2, sum_three, 0)))
    sum_zero(3)
    near_wait(4)
    main_block(4, then((0, sum_three, 1), (1, sum_one, 3), (2, sum_two, 2)))
    sum_zero(4)

    bias_two = small_ref[13:14, :]

    def backward_tile(b):
        row = pl.multiple_of(b * TILE, TILE)
        step = 32
        for q in range(TILE // step):
            rows = pl.ds(row + q * step, step)
            place = slice(GAP + q * step, GAP + q * step + step)
            accs[11] += fold(ct[rows, :].astype(F32) * (br[rows, :] + bias_two))
            grad = jnp.concatenate([gn[b, c, place, :] for c in range(p.nc)], axis=1)
            unit = xhat[rows, :].astype(F32)
            both_of = grad * unit
            accs[8] += fold(both_of)
            accs[9] += fold(grad)
            u = grad * gain
            mean_u = jnp.sum(u, axis=1, keepdims=True) * (1.0 / p.d)
            mean_x = jnp.sum(both_of * gain, axis=1, keepdims=True) * (1.0 / p.d)
            inverse = rstd[rows, :]
            inverse = jnp.concatenate([inverse] * p.nc, axis=1)
            rounded = ((u - mean_u - unit * mean_x) * inverse).astype(BF16)
            accs[7] += jnp.dot(first_row[:, 0:step], rounded, preferred_element_type=F32)
            low = rounded.astype(F32)
            for c in range(p.nc):
                gn[b, c, place, :] = low[:, 128 * c : 128 * c + 128]
        for c in range(p.nc):
            cols = slice(128 * c, 128 * c + 128)
            low = gn[b, c, GAP : GAP + TILE, :]
            for k in range(TAPS):
                first = GAP - 3 + k
                accs[k, :, cols] += fold(low * xf[b, c, first : first + TILE, :])

    def backward_tiles(low, high):
        @pl.loop(low, high)
        def _(b):
            backward_tile(b)

    def edge_sends():
        after, before = (me_t + 1) % nt, (me_t + nt - 1) % nt
        return [
            remote(gn.at[nb - 1, :, pl.ds(TILE, GAP), :], hprev, send_sem.at[7, 2], halo_sem.at[2], tm=after),
            remote(gn.at[0, :, pl.ds(GAP, GAP), :], hnext, send_sem.at[7, 3], halo_sem.at[3], tm=before),
        ]

    @pl.loop(0, 2)
    def _(i):
        backward_tile(i * (nb - 1))

    start(edge_sends())
    sum_two(3)
    cut = [1, 1 + (nb - 2) // 4, 1 + (nb - 2) * 3 // 4, nb - 1]
    backward_tiles(cut[0], cut[1])
    sum_one(4)
    backward_tiles(cut[1], cut[2])
    sum_three(2)
    backward_tiles(cut[2], cut[3])
    sum_two(4)

    hidden_tiles = lane_permuted(lambda i: accb[:, 128 * i : 128 * i + 128], p.regrouped, p.ff // 128)
    for c in range(p.nc):
        cols = slice(128 * c, 128 * c + 128)
        line = []
        for k in range(10):
            line.append(jnp.sum(accs[k, :, cols], axis=0, keepdims=True))
        for i in range(3):
            line.append(jnp.sum(hidden_tiles[i * p.nc + c], axis=0, keepdims=True))
        for k in (10, 11):
            line.append(jnp.sum(accs[k, :, cols], axis=0, keepdims=True))
        line.append(jnp.zeros((1, 128), F32))
        sma[c] = jnp.concatenate(line, axis=0)

    def small_one_sends():
        out = []
        for step in range(1, nr):
            peer = (me_r + step) % nr
            out.append(remote(sma.at[peer], smr.at[me_r], send_sem.at[7, 4], sm_sem.at[0], rows=peer))
        return out

    def small_two_sends():
        out = []
        for step in range(1, nt):
            peer = (me_t + step) % nt
            out.append(remote(smq.at[nt], smq.at[me_t], send_sem.at[8, 0], sm_sem.at[1], tm=peer))
        return out

    def small_three_sends():
        out = []
        for step in range(1, nr):
            peer = (me_r + step) % nr
            out.append(remote(smf.at[me_r], smf.at[me_r], send_sem.at[8, 1], sm_sem.at[2], rows=peer))
        return out

    smr[me_r] = sma[me_r]
    start(small_one_sends())

    def small_two():
        arrived(smr.at[pl.ds(0, nr - 1)], sm_sem.at[0])
        total = smr[0]
        for k in range(1, nr):
            total = total + smr[k]
        smq[nt] = total
        smq[me_t] = total
        start(small_two_sends())

    def small_three():
        arrived(smq.at[pl.ds(0, nt - 1)], sm_sem.at[1])
        total = smq[0]
        for k in range(1, nt):
            total = total + smq[k]
        smf[me_r] = total
        start(small_three_sends())

    def exchange_edges(b):
        same = flags[pl.ds(b, 1), :] < 0.5
        for c in range(p.nc):
            gn[b, c, 0:GAP, :] = jnp.where(same, gn[b - 1, c, TILE : TILE + GAP, :], 0.0)
            gn[b - 1, c, GAP + TILE :, :] = jnp.where(same, gn[b, c, GAP : GAP + GAP, :], 0.0)

    def last_tile(b):
        row = pl.multiple_of(b * TILE, TILE)
        rows = pl.ds(row, TILE)
        for c in range(p.nc):
            cols = slice(128 * c, 128 * c + 128)
            source = frx[pl.ds(row + HALO, TILE), cols].astype(F32)
            branch = br[rows, cols] + bias_two[:, cols]
            nm[rows, cols] = (source + scale[:, cols] * branch).astype(BF16)
            total = ct[rows, cols].astype(F32)
            for k in range(TAPS):
                first = GAP + 3 - k
                total = total + small_ref[k : k + 1, cols] * gn[b, c, first : first + TILE, :]
            gb[rows, cols] = total.astype(BF16)

    exchange_edges(1)

    def last_tiles(low, high):
        @pl.loop(low, high)
        def _(b):
            exchange_edges(b + 1)
            last_tile(b)

    cut = [1, 1 + (nb - 2) * 4 // 10, 1 + (nb - 2) * 7 // 10, nb - 1]
    last_tiles(cut[0], cut[1])
    small_two()
    last_tiles(cut[1], cut[2])
    sum_three(3)
    last_tiles(cut[2], cut[3])
    arrived(hprev, halo_sem.at[2])
    arrived(hnext, halo_sem.at[3])
    for c in range(p.nc):
        gn[0, c, 0:GAP, :] = jnp.where(flags[0:1, :] < 0.5, hprev[c], 0.0)
        gn[nb - 1, c, GAP + TILE :, :] = jnp.where(flags[nb : nb + 1, :] < 0.5, hnext[c], 0.0)

    @pl.loop(0, 2)
    def _(i):
        last_tile(i * (nb - 1))

    small_three()
    sum_three(4)

    for j in range(len(p.blocks)):
        sum_wait(j)
    for q in range(nr):
        tiles = lane_permuted(lambda i, q=q: finw1[q, :, 128 * i : 128 * i + 128], p.regrouped, p.ff // 128)
        for i, tile in enumerate(tiles):
            g1_out[p.part * q : p.part * q + p.part, 128 * i : 128 * i + 128] = tile
        g2_out[:, p.lanes * q : p.lanes * q + p.lanes] = finw2[q]
    arrived(smf.at[pl.ds(0, nr - 1)], sm_sem.at[2])
    for c in range(p.nc):
        small_out[:, 128 * c : 128 * c + 128] = smf[c]

    sent = halo_sends() + edge_sends() + small_one_sends() + small_two_sends() + small_three_sends()
    for j in range(len(p.blocks)):
        sent += spread_sends(j) + far_sends(j) + near_sends(j, me_r) + near_sends(j, far)
        sent += pair_sends(j) + cross_sends(j) + holder_sends(j) + final_sends(j)
    for copy in sent:
        copy.wait_send()
    for load in rest:
        load.wait()


def finish_kernel(
    nm, gb, grad1, grad2, grad_small, state1, state2,
    small_master, small_first, small_second, small_average,
    output, ingrad, *rest,
):
    outs1, outs2, outs_small = rest[0:5], rest[5:10], rest[10:15]
    new1, low1, new2, low2, sem = rest[15:]
    copies = [
        pltpu.make_async_copy(nm, output.at[0], sem.at[0]),
        pltpu.make_async_copy(gb, ingrad.at[0], sem.at[1]),
    ]
    for copy in copies:
        copy.start()
    count = 2
    for grad, state, new, low, outs, rate in (
        (grad1, state1, new1, low1, outs1, rate_first),
        (grad2, state2, new2, low2, outs2, rate_second),
    ):
        step = 32
        for q in range(grad.shape[0] // step):
            rows = slice(q * step, q * step + step)
            got = adamw_step(
                state[0, rows], state[1, rows], state[2, rows], state[3, rows], grad[rows], rate
            )
            for k in range(4):
                new[k, rows] = got[k]
            low[rows] = got[4]
        for k in range(5):
            source = low if k == 4 else new.at[k]
            copy = pltpu.make_async_copy(source, outs[k], sem.at[count])
            copy.start()
            copies.append(copy)
            count += 1
    got = adamw_step(
        small_master[...], small_first[...], small_second[...], small_average[...], grad_small[0:15], rate_small
    )
    for k in range(5):
        outs_small[k][...] = got[k]
    for copy in copies:
        copy.wait()


def finish(kept, smalls, t):
    vmem = pl.BlockSpec(memory_space=pltpu.VMEM)
    anyplace = pl.BlockSpec(memory_space=pl.ANY)
    kept = [pltpu.with_memory_space_constraint(value, pltpu.VMEM) for value in kept]
    nm, _, grad1, grad2 = kept[:4]
    whole = jax.ShapeDtypeStruct((1, t, nm.shape[1]), BF16)

    def five(shape):
        return [jax.ShapeDtypeStruct(shape, F32)] * 4 + [jax.ShapeDtypeStruct(shape, BF16)]

    v = pltpu.VMEM
    return pl.pallas_call(
        finish_kernel,
        out_shape=(whole, whole, *five(grad1.shape), *five(grad2.shape), *five(smalls[0].shape)),
        in_specs=[vmem] * 11,
        out_specs=(anyplace,) * 12 + (vmem,) * 5,
        scratch_shapes=[
            v((4, *grad1.shape), F32),
            v(grad1.shape, BF16),
            v((4, *grad2.shape), F32),
            v(grad2.shape, BF16),
            pltpu.SemaphoreType.DMA((12,)),
        ],
        compiler_params=pltpu.CompilerParams(vmem_limit_bytes=8_000_000),
    )(*kept, *smalls)


def call(plan, frames, cotangent, lengths, one, two, small_master):
    p = plan
    t, d, ff, nt, nr, nb, nc = p.t, p.d, p.ff, p.nt, p.nr, p.nb, p.nc
    vmem = pl.BlockSpec(memory_space=pltpu.VMEM)
    anyplace = pl.BlockSpec(memory_space=pl.ANY)
    n_lens = -(-lengths.shape[1] // 128) * 128
    v = pltpu.VMEM
    scratch = [
        v((t + 2 * HALO, d), BF16),
        v((t, d), BF16),
        v((d, t), BF16),
        v((d, t), BF16),
        v((t, d), F32),
        v((nb, nc, TILE + 2 * GAP, 128), F32),
        v((nb, nc, TILE + 2 * GAP, 128), F32),
        v((t, d), BF16),
        v((t, 128), F32),
        v((nt, nr, p.part, ff), BF16),
        v((nr, ff, p.lanes), BF16),
        v((d, p.widest), F32),
        v((d, p.widest), F32),
        v((8, n_lens), F32),
        v((-(-(nb + 1) // 8) * 8, 128), F32),
        v((8, ff), F32),
        v((12, 8, d), F32),
        v((8, ff), F32),
        v((TILE, d), F32),
        v((nt, nr, p.part, ff), BF16),
        v((nr, ff, p.lanes), BF16),
        v((2, nt, p.part, ff), BF16),
        v((2, ff, p.lanes), BF16),
        v((nt, p.part, ff), BF16),
        v((ff, p.lanes), BF16),
        v((nt, p.part, ff), BF16),
        v((nt, p.share, p.lanes), BF16),
        v((nr, p.part, ff), F32),
        v((nr, p.share, p.lanes), F32),
        v((nr, 16, p.lanes), F32),
        v((nr, 16, p.lanes), F32),
        v((nt + 1, 16, p.lanes), F32),
        v((nr, 16, p.lanes), F32),
        v((nc, GAP, 128), F32),
        v((nc, GAP, 128), F32),
        pltpu.SemaphoreType.DMA((5,)),
        pltpu.SemaphoreType.DMA((9, len(p.blocks))),
        pltpu.SemaphoreType.DMA((4,)),
        pltpu.SemaphoreType.DMA((len(p.blocks), 3)),
        pltpu.SemaphoreType.DMA((len(p.blocks), 4)),
        pltpu.SemaphoreType.DMA((3,)),
    ]
    return pl.pallas_call(
        functools.partial(kernel, plan),
        out_shape=(
            v((t, d), BF16),
            v((t, d), BF16),
            v((p.rows1, ff), F32),
            v((p.share, d), F32),
            v((16, d), F32),
            v((4, p.rows1, ff), F32),
            v((4, p.share, d), F32),
        ),
        in_specs=[anyplace, anyplace, vmem] + [anyplace] * 8 + [vmem],
        out_specs=(vmem,) * 7,
        scratch_shapes=scratch,
        compiler_params=pltpu.CompilerParams(
            collective_id=0, has_side_effects=True, vmem_limit_bytes=56_500_000
        ),
    )(frames, cotangent, lengths, *one, *two, small_master)


def padded_2(array, sides, width):
    for axis, dim in sides:
        devices, length = (lax.axis_size(axis), array.shape[dim])
        up = [(i, (i + 1) % devices) for i in range(devices - 1)]
        down = [(j, i) for i, j in up]
        last = lax.slice_in_dim(array, length - width, length, axis=dim)
        leading = lax.slice_in_dim(array, 0, width, axis=dim)
        before = lax.ppermute(last, axis, up)
        after = lax.ppermute(leading, axis, down)
        array = jnp.concatenate([before, array, after], axis=dim)
    return array


def cut_along(array, dim, devices):
    before, after = (array.shape[:dim], array.shape[dim + 1 :])
    return jnp.moveaxis(array.reshape(*before, devices, -1, *after), dim, 0)


def sent_and_summed(array, axis, dim):
    devices = lax.axis_size(axis)
    pieces = lax.all_to_all(cut_along(array, dim, devices), axis, 0, 0, tiled=True)
    return jnp.sum(pieces.astype(jnp.float32), axis=0)


def edge_masks(lengths_row, first_frame, frame_count):
    ends_at = jnp.cumsum(lengths_row, dtype=jnp.int32)
    places = first_frame + jnp.arange(frame_count, dtype=jnp.int32)
    passed = ends_at[None, :] <= places[:, None]
    lower = jnp.max(jnp.where(passed, ends_at[None, :], 0), axis=1)
    upper = jnp.min(jnp.where(passed, ends_at[-1], ends_at[None, :]), axis=1)
    mask_rows = []
    for tap_index in range(7):
        spot_now = places + (tap_index - 3)
        mask_rows.append(((spot_now >= lower) & (spot_now < upper)).astype(jnp.float32))
    return jnp.stack(mask_rows)


def depthwise(padded, tap_rows, masks, frame_count):
    summed = jnp.zeros((frame_count, padded.shape[1]), jnp.float32)
    for tap_index in range(7):
        window = padded[tap_index : tap_index + frame_count].astype(jnp.float32)
        summed = summed + tap_rows[tap_index][None, :] * window * masks[tap_index][:, None]
    return summed


def layer_norm(conv_out, norm_gain, norm_bias):
    centred = conv_out - jnp.mean(conv_out, axis=-1, keepdims=True)
    spread = jnp.mean(centred * centred, axis=-1, keepdims=True)
    return centred * lax.rsqrt(spread + norm_eps) * norm_gain[None, :] + norm_bias[None, :]


def exact_gelu(values):
    return jax.nn.gelu(values, approximate=False)


def frame_product(left_side, right_side):
    return lax.dot_general(
        left_side, right_side, (((0,), (0,)), ((), ())), preferred_element_type=jnp.float32
    )


def plain_body(
    frames,
    cotangent,
    lengths,
    w1_master,
    w1_first,
    w1_second,
    w1_average,
    w2_master,
    w2_first,
    w2_second,
    w2_average,
    small_master,
    small_first,
    small_second,
    small_average,
):
    frame_count = frames.shape[1]
    width = frames.shape[2]
    w1_low, w2_low = (
        lax.all_gather(w1_master.astype(jnp.bfloat16), "tm", axis=0, tiled=True),
        lax.all_gather(w2_master.astype(jnp.bfloat16), "tm", axis=0, tiled=True),
    )
    inputs = frames[0]
    upstream = cotangent[0].astype(jnp.float32)
    masks = edge_masks(lengths[0], lax.axis_index("tm") * frame_count, frame_count)
    tap_rows = small_master[0:7]
    layer_scale = small_master[14]
    padded = padded_2(inputs, (("tm", 0),), 3)
    conv_out = depthwise(padded, tap_rows, masks, frame_count) + small_master[7][None, :]
    normed, norm_back = jax.vjp(layer_norm, conv_out, small_master[8], small_master[9])
    normed_low = normed.astype(jnp.bfloat16)
    hidden = (
        jnp.dot(normed_low, w1_low, preferred_element_type=jnp.float32)
        + small_master[10:13].reshape(-1)[None, :]
    )
    activated, gelu_back = jax.vjp(exact_gelu, hidden)
    act_low = activated.astype(jnp.bfloat16)
    branch = (
        jnp.dot(act_low, w2_low, preferred_element_type=jnp.float32) + small_master[13][None, :]
    )
    output = (inputs.astype(jnp.float32) + layer_scale[None, :] * branch).astype(jnp.bfloat16)
    grad_scale = jnp.sum(upstream * branch, axis=0)
    grad_branch = (layer_scale[None, :] * upstream).astype(jnp.bfloat16)
    grad_act = lax.dot_general(
        grad_branch, w2_low, (((1,), (1,)), ((), ())), preferred_element_type=jnp.float32
    )
    grad_hidden = gelu_back(grad_act)[0].astype(jnp.bfloat16)
    grad_normed = lax.dot_general(
        grad_hidden, w1_low, (((1,), (1,)), ((), ())), preferred_element_type=jnp.float32
    )
    grad_conv, grad_gain, grad_shift = norm_back(grad_normed)
    grad_low = grad_conv.astype(jnp.bfloat16)
    grad_pad = padded_2(grad_low, (("tm", 0),), 3)
    input_grad = (upstream + depthwise(grad_pad, tap_rows[::-1], masks, frame_count)).astype(
        jnp.bfloat16
    )
    grad_float = grad_low.astype(jnp.float32)
    grad_taps = jnp.stack(
        [
            jnp.sum(
                grad_float
                * padded[tap_index : tap_index + frame_count].astype(jnp.float32)
                * masks[tap_index][:, None],
                axis=0,
            )
            for tap_index in range(7)
        ]
    )
    middle_rows = jnp.stack([jnp.sum(grad_float, axis=0), grad_gain, grad_shift])
    bias_rows = jnp.sum(grad_hidden.astype(jnp.float32), axis=0).reshape(3, width)
    last_rows = jnp.stack([jnp.sum(grad_branch.astype(jnp.float32), axis=0), grad_scale])
    small_grad = jnp.concatenate([grad_taps, middle_rows, bias_rows, last_rows], axis=0)
    full_one = frame_product(normed_low, grad_hidden)
    full_two = frame_product(act_low, grad_branch)
    share_one, share_two = (
        sent_and_summed(full_one.astype(jnp.bfloat16), "tm", 0),
        sent_and_summed(full_two.astype(jnp.bfloat16), "tm", 0),
    )
    grad_one, grad_two = (
        lax.psum(share_one.astype(jnp.bfloat16), "rows").astype(jnp.float32),
        lax.psum(share_two.astype(jnp.bfloat16), "rows").astype(jnp.float32),
    )
    small_total = lax.psum(small_grad, ("tm", "rows"))
    one_out = adamw_step(w1_master, w1_first, w1_second, w1_average, grad_one, rate_first)
    two_out = adamw_step(w2_master, w2_first, w2_second, w2_average, grad_two, rate_second)
    small_out = adamw_step(
        small_master, small_first, small_second, small_average, small_total, rate_small
    )
    return (
        output[None],
        input_grad[None],
        one_out[0],
        one_out[1],
        one_out[2],
        one_out[3],
        one_out[4],
        two_out[0],
        two_out[1],
        two_out[2],
        two_out[3],
        two_out[4],
        small_out[0],
        small_out[1],
        small_out[2],
        small_out[3],
        small_out[4],
    )


def body(
    frames,
    cotangent,
    lengths,
    w1_master,
    w1_first,
    w1_second,
    w1_average,
    w2_master,
    w2_first,
    w2_second,
    w2_average,
    small_master,
    small_first,
    small_second,
    small_average,
):
    nt, nr = lax.axis_size("tm"), lax.axis_size("rows")
    plan = Plan(nt, nr, frames.shape[1], frames.shape[2], w1_master.shape[1])
    kept = call(
        plan,
        frames,
        cotangent,
        lengths,
        (w1_master, w1_first, w1_second, w1_average),
        (w2_master, w2_first, w2_second, w2_average),
        small_master,
    )
    return finish(kept, (small_master, small_first, small_second, small_average), plan.t)


def solution(mesh):
    in_specs = (
        P("rows", "tm", None),
        P("rows", "tm", None),
        P("rows", None),
        P("tm", None),
        P("tm", None),
        P("tm", None),
        P("tm", None),
        P("tm", None),
        P("tm", None),
        P("tm", None),
        P("tm", None),
        P(),
        P(),
        P(),
        P(),
    )
    out_specs = (
        P("rows", "tm", None),
        P("rows", "tm", None),
        P("tm", None),
        P("tm", None),
        P("tm", None),
        P("tm", None),
        P("tm", None),
        P("tm", None),
        P("tm", None),
        P("tm", None),
        P("tm", None),
        P("tm", None),
        P(),
        P(),
        P(),
        P(),
        P(),
    )
    fits = mesh.shape["tm"] == 8 and mesh.shape["rows"] == 4
    return jax.shard_map(body if fits else plain_body, mesh=mesh, in_specs=in_specs, out_specs=out_specs, check_vma=False)
```

```python
import functools

import jax
import jax.numpy as jnp
import numpy as np
from jax import lax
from jax.experimental import pallas as pl
from jax.experimental.pallas import tpu as pltpu
from jax.sharding import PartitionSpec as P

ADAM_STEP = 3
norm_eps = 1e-06
adam_eps = 1e-08
weight_decay = 0.01
beta_first = 0.5
beta_second = 0.5
average_keep = 0.75
rate_first = 0.08
rate_second = 0.05
rate_small = 0.4

TAPS = 7
TILE = 128
GAP = 8
GRAIN = 16
HALO = 16
F32 = jnp.float32
BF16 = jnp.bfloat16
MESH = pl.DeviceIdType.MESH
RSQRT_HALF = np.float32(0.7071067811865476)
RSQRT_2PI = np.float32(0.3989422804014327)


def adamw_step(master, first_old, second_old, average_old, gradient, rate):
    first_new = beta_first * first_old + (1.0 - beta_first) * gradient
    second_new = beta_second * second_old + (1.0 - beta_second) * gradient * gradient
    first_hat = first_new / (1.0 - beta_first**ADAM_STEP)
    second_hat = second_new / (1.0 - beta_second**ADAM_STEP)
    master_new = master - rate * (
        first_hat / (jnp.sqrt(second_hat) + adam_eps) + weight_decay * master
    )
    average_new = average_keep * average_old + (1.0 - average_keep) * master_new
    return (master_new, first_new, second_new, average_new, master_new.astype(BF16))


class Plan:
    def __init__(self, nt, nr, frame_count, width, hidden):
        self.nt, self.nr, self.t, self.d, self.ff = nt, nr, frame_count, width, hidden
        self.share = hidden // nt
        self.rows1 = width // nt
        self.part = self.rows1 // nr
        self.lanes = width // nr
        self.nb = frame_count // TILE
        self.nc = width // 128
        self.chunks = []
        offset = begin = 0
        for run in (16, 16, 32, 32, 32, 32, 32):
            self.chunks.append((offset, run * nt, run, begin))
            offset += run * nt
            begin += run
        self.members = [(0, 1), (2,), (3, 4), (5, 6)]
        self.blocks = [
            (self.chunks[own[0]][0], sum(self.chunks[j][1] for j in own)) for own in self.members
        ]
        self.widest = max(size for _, size in self.blocks)
        self.m = 1024
        self.natural = []
        for _, _, run, begin in self.chunks:
            for k in range(nt):
                for o in range(0, run, GRAIN):
                    self.natural.append((self.share * k + begin + o) // GRAIN)
        self.regrouped = [self.natural.index(g) for g in range(hidden // GRAIN)]


def lane_permuted(tile_of, source, count):
    per = 128 // GRAIN
    out = []
    for tile in range(count):
        value, before = None, None
        for q in range(per):
            run = source[tile * per + q]
            now = (run // per, (q - run % per) % per)
            if now == before:
                continue
            before = now
            piece = tile_of(now[0])
            if now[1]:
                piece = pltpu.roll(piece, now[1] * GRAIN, 1)
            if value is None:
                value = piece
            else:
                lane = lax.broadcasted_iota(jnp.int32, piece.shape, 1)
                value = jnp.where(lane >= q * GRAIN, piece, value)
        out.append(value)
    return out


def fold(value):
    rows = value.shape[0]
    total = value[0:8]
    for g in range(1, rows // 8):
        total = total + value[8 * g : 8 * g + 8]
    return total


def kernel(
    plan,
    frames_hbm,
    cot_hbm,
    lengths_ref,
    w1_hbm,
    w1_first_hbm,
    w1_second_hbm,
    w1_average_hbm,
    w2_hbm,
    w2_first_hbm,
    w2_second_hbm,
    w2_average_hbm,
    small_ref,
    nm,
    gb,
    finw1,
    finw2,
    small_out,
    state1,
    state2,
    frx,
    ct,
    nmt,
    gbt,
    br,
    gn,
    xf,
    xhat,
    rstd,
    w1b,
    w2b,
    acc1,
    acc2,
    lens,
    flags,
    b1p,
    accs,
    accb,
    tmp,
    s1w1,
    s1w2,
    r1w1,
    r1w2,
    r2w1,
    r2w2,
    r3w1,
    r3w2,
    sma,
    smr,
    smq,
    smf,
    hprev,
    hnext,
    in_sem,
    send_sem,
    halo_sem,
    ag_sem,
    rs_sem,
    sm_sem,
):
    p = plan
    nt, nr, t_len = p.nt, p.nr, p.t
    me_t = lax.axis_index("tm")
    me_r = lax.axis_index("rows")
    near = me_r + 1 - 2 * (me_r % 2)
    far = (me_r + 2) % nr
    both = near + 2 - 4 * (near // 2)

    def remote(src, dst, send, recv, tm=None, rows=None):
        device = {"tm": me_t if tm is None else tm, "rows": me_r if rows is None else rows}
        return pltpu.make_async_remote_copy(
            src_ref=src, dst_ref=dst, send_sem=send, recv_sem=recv,
            device_id=device, device_id_type=MESH,
        )

    def arrived(view, sem):
        pltpu.make_async_copy(view, view, sem).wait()

    loads = [
        pltpu.make_async_copy(w1_hbm, state1.at[0], in_sem.at[0]),
        pltpu.make_async_copy(w2_hbm, state2.at[0], in_sem.at[1]),
        pltpu.make_async_copy(frames_hbm.at[0], frx.at[pl.ds(HALO, t_len)], in_sem.at[2]),
        pltpu.make_async_copy(cot_hbm.at[0], ct, in_sem.at[3]),
    ]
    for load in loads:
        load.start()

    barrier = pltpu.get_barrier_semaphore()
    for step in range(1, nt):
        pl.semaphore_signal(
            barrier, inc=1, device_id={"tm": (me_t + step) % nt, "rows": me_r}, device_id_type=MESH
        )
    for step in range(1, nr):
        pl.semaphore_signal(
            barrier, inc=1, device_id={"tm": me_t, "rows": (me_r + step) % nr}, device_id_type=MESH
        )

    lens[...] = jnp.zeros_like(lens)
    n_len = lengths_ref.shape[1]
    lens[0:1, 0:n_len] = lengths_ref[...].astype(F32)
    ends = lens[...]
    lane = lax.broadcasted_iota(jnp.int32, ends.shape, 1)
    shift = 1
    while shift < lens.shape[1]:
        ends = ends + jnp.where(lane >= shift, pltpu.roll(ends, shift, 1), 0.0)
        shift *= 2
    n_flag = flags.shape[0]
    spot = me_t * t_len + TILE * lax.broadcasted_iota(jnp.int32, (n_flag, lens.shape[1]), 0)
    hit = (ends[0:1, :] == spot.astype(F32)) | (spot == 0)
    edge = jnp.max(jnp.where(hit, 1.0, 0.0), axis=1, keepdims=True)
    flags[...] = jnp.broadcast_to(edge, flags.shape)
    accs[...] = jnp.zeros_like(accs)
    accb[...] = jnp.zeros_like(accb)
    bias_tiles = lane_permuted(
        lambda i: jnp.broadcast_to(small_ref[10 + i // p.nc : 11 + i // p.nc, 128 * (i % p.nc) : 128 * (i % p.nc) + 128], (8, 128)),
        p.natural,
        p.ff // 128,
    )
    for i, tile in enumerate(bias_tiles):
        b1p[:, 128 * i : 128 * i + 128] = tile

    loads[0].wait()
    loads[1].wait()
    own_rows = pl.ds(pl.multiple_of(me_r * p.part, p.part), p.part)
    own_lanes = pl.ds(pl.multiple_of(me_r * p.lanes, p.lanes), p.lanes)
    own1 = lane_permuted(lambda i: state1[0, own_rows, 128 * i : 128 * i + 128], p.natural, p.ff // 128)
    for i, tile in enumerate(own1):
        w1b[me_t, me_r, :, 128 * i : 128 * i + 128] = tile.astype(BF16)
    for jo, _, run, begin in p.chunks:
        w2b[me_r, pl.ds(pl.multiple_of(jo + run * me_t, run), run), :] = state2[0, begin : begin + run, own_lanes].astype(BF16)

    pl.semaphore_wait(barrier, nt + nr - 2)

    def halo_sends():
        after, before = (me_t + 1) % nt, (me_t + nt - 1) % nt
        return [
            remote(frames_hbm.at[0, pl.ds(t_len - HALO, HALO)], frx.at[pl.ds(0, HALO)], send_sem.at[7, 0], halo_sem.at[0], tm=after),
            remote(frames_hbm.at[0, pl.ds(0, HALO)], frx.at[pl.ds(HALO + t_len, HALO)], send_sem.at[7, 1], halo_sem.at[1], tm=before),
        ]

    def w1_part(j, q):
        jo, size = p.chunks[j][:2]
        return w1b.at[:, q, :, pl.ds(jo, size)]

    def w2_part(j, q):
        jo, size = p.chunks[j][:2]
        return w2b.at[q, pl.ds(jo, size), :]

    def spread_sends(j):
        jo, size, run, _ = p.chunks[j]
        out = []
        for step in range(1, nt):
            peer = (me_t + step) % nt
            one = w1b.at[me_t, me_r, :, pl.ds(jo, size)]
            two = w2b.at[me_r, pl.ds(pl.multiple_of(jo + run * me_t, run), run), :]
            out.append(remote(one, one, send_sem.at[0, j], ag_sem.at[j, 0], tm=peer))
            out.append(remote(two, two, send_sem.at[0, j], ag_sem.at[j, 0], tm=peer))
        return out

    def spread_wait(j):
        jo, size = p.chunks[j][:2]
        arrived(w1b.at[pl.ds(0, nt - 1), pl.ds(0, 2), :, pl.ds(jo, size)], ag_sem.at[j, 0])

    def far_sends(j):
        return [
            remote(w1_part(j, me_r), w1_part(j, me_r), send_sem.at[1, j], ag_sem.at[j, 1], rows=far),
            remote(w2_part(j, me_r), w2_part(j, me_r), send_sem.at[1, j], ag_sem.at[j, 1], rows=far),
        ]

    def far_wait(j):
        jo, size = p.chunks[j][:2]
        arrived(w1b.at[:, pl.ds(0, 2), :, pl.ds(jo, size)], ag_sem.at[j, 1])

    def near_sends(j, q):
        return [
            remote(w1_part(j, q), w1_part(j, q), send_sem.at[2, j], ag_sem.at[j, 2], rows=near),
            remote(w2_part(j, q), w2_part(j, q), send_sem.at[2, j], ag_sem.at[j, 2], rows=near),
        ]

    def near_wait(j):
        jo, size = p.chunks[j][:2]
        arrived(w1b.at[:, :, :, pl.ds(jo, size)], ag_sem.at[j, 2])

    def start(copies):
        for copy in copies:
            copy.start()

    def gather_one(j):
        spread_wait(j)
        start(far_sends(j))
        start(near_sends(j, me_r))

    def gather_two(j):
        far_wait(j)
        start(near_sends(j, far))

    def spread(j):
        start(spread_sends(j))

    spread(0)
    spread(1)
    start(halo_sends())

    rest = [
        pltpu.make_async_copy(source, target, in_sem.at[4])
        for source, target in (
            (w1_first_hbm, state1.at[1]),
            (w1_second_hbm, state1.at[2]),
            (w1_average_hbm, state1.at[3]),
            (w2_first_hbm, state2.at[1]),
            (w2_second_hbm, state2.at[2]),
            (w2_average_hbm, state2.at[3]),
        )
    ]
    for load in rest:
        load.start()
    loads[2].wait()
    loads[3].wait()

    gain = small_ref[8:9, :]
    shift_row = small_ref[9:10, :]
    scale = small_ref[14:15, :]

    first_row = jnp.where(lax.broadcasted_iota(jnp.int32, (8, TILE), 0) == 0, 1.0, 0.0).astype(BF16)

    def turn_tile(b):
        row = pl.multiple_of(b * TILE, TILE)
        nmt[:, pl.ds(row, TILE)] = nm[pl.ds(row, TILE), :].T
        gbt[:, pl.ds(row, TILE)] = gb[pl.ds(row, TILE), :].T

    def forward_tile(b, turned=None):
        if turned is not None:
            turn_tile(turned)
        row = pl.multiple_of(b * TILE, TILE)
        starts_here = flags[pl.ds(b, 1), :]
        ends_here = flags[pl.ds(b + 1, 1), :]
        lead = frx[pl.ds(row, HALO), :].astype(F32)
        trail = frx[pl.ds(row + HALO + TILE, HALO), :].astype(F32)
        for c in range(p.nc):
            cols = slice(128 * c, 128 * c + 128)
            xf[b, c, GAP : GAP + TILE, :] = frx[pl.ds(row + HALO, TILE), cols].astype(F32)
            xf[b, c, 0:GAP, :] = jnp.where(starts_here > 0.5, 0.0, lead[HALO - GAP :, cols])
            xf[b, c, GAP + TILE :, :] = jnp.where(ends_here > 0.5, 0.0, trail[0:GAP, cols])
        for c in range(p.nc):
            cols = slice(128 * c, 128 * c + 128)
            total = jnp.broadcast_to(small_ref[7:8, cols], (TILE, 128))
            for k in range(TAPS):
                first = GAP - 3 + k
                total = total + small_ref[k : k + 1, cols] * xf[b, c, first : first + TILE, :]
            tmp[:, cols] = total
        step = 32
        for q in range(TILE // step):
            rows = pl.ds(row + q * step, step)
            value = tmp[q * step : q * step + step, :]
            centred = value - jnp.sum(value, axis=1, keepdims=True) * (1.0 / p.d)
            spread = jnp.sum(centred * centred, axis=1, keepdims=True) * (1.0 / p.d)
            inverse = lax.rsqrt(spread + norm_eps)
            unit = centred * inverse
            rstd[rows, :] = jnp.broadcast_to(inverse, (step, 128))
            xhat[rows, :] = unit.astype(BF16)
            nm[rows, :] = (unit * gain + shift_row).astype(BF16)
            low = (scale * ct[rows, :].astype(F32)).astype(BF16)
            gb[rows, :] = low
        accs[10] += jnp.dot(first_row, gb[pl.ds(row, TILE), :], preferred_element_type=F32)

    def forward_tiles(low, high):
        @pl.loop(low, high)
        def _(b):
            forward_tile(b, b - 1)

    nb = p.nb
    forward_tile(1)
    forward_tiles(2, nb // 4 - 1)
    spread(2)
    forward_tiles(nb // 4 - 1, nb * 5 // 12)
    gather_one(0)
    spread(3)
    spread(4)
    forward_tiles(nb * 5 // 12, nb * 7 // 12)
    gather_one(1)
    forward_tiles(nb * 7 // 12, nb * 3 // 4)
    gather_two(0)
    arrived(frx.at[pl.ds(HALO + t_len, HALO)], halo_sem.at[1])
    forward_tiles(nb * 3 // 4, nb)
    gather_two(1)
    gather_one(2)
    arrived(frx.at[pl.ds(0, HALO)], halo_sem.at[0])
    forward_tile(0, nb - 1)
    turn_tile(0)
    near_wait(0)
    near_wait(1)

    def parts_of(j):
        jo, size, run, begin = p.chunks[j]
        return jo, size, begin, run

    def pair_sends(j):
        jo, size, _, _ = parts_of(j)
        out = []
        for slot, q in ((0, near), (1, both)):
            out.append(remote(s1w1.at[:, q, :, pl.ds(jo, size)], r1w1.at[slot, :, :, pl.ds(jo, size)], send_sem.at[3, j], rs_sem.at[j, 0], rows=near))
            out.append(remote(s1w2.at[q, pl.ds(jo, size), :], r1w2.at[slot, pl.ds(jo, size), :], send_sem.at[3, j], rs_sem.at[j, 0], rows=near))
        return out

    def cross_sends(j):
        jo, size, _, _ = parts_of(j)
        return [
            remote(r1w1.at[1, :, :, pl.ds(jo, size)], r2w1.at[:, :, pl.ds(jo, size)], send_sem.at[4, j], rs_sem.at[j, 1], rows=far),
            remote(r1w2.at[1, pl.ds(jo, size), :], r2w2.at[pl.ds(jo, size), :], send_sem.at[4, j], rs_sem.at[j, 1], rows=far),
        ]

    def holder_sends(j):
        jo, size, start_row, run = parts_of(j)
        out = []
        for step in range(1, nt):
            peer = (me_t + step) % nt
            out.append(remote(r1w1.at[0, peer, :, pl.ds(jo, size)], r3w1.at[me_t, :, pl.ds(jo, size)], send_sem.at[5, j], rs_sem.at[j, 2], tm=peer))
            out.append(remote(r1w2.at[0, pl.ds(pl.multiple_of(jo + run * peer, run), run), :], r3w2.at[me_t, pl.ds(start_row, run), :], send_sem.at[5, j], rs_sem.at[j, 2], tm=peer))
        return out

    def final_sends(j):
        jo, size, start_row, run = parts_of(j)
        out = []
        for step in range(1, nr):
            peer = (me_r + step) % nr
            one = finw1.at[me_r, :, pl.ds(jo, size)]
            two = finw2.at[me_r, pl.ds(start_row, run), :]
            out.append(remote(one, one, send_sem.at[6, j], rs_sem.at[j, 3], rows=peer))
            out.append(remote(two, two, send_sem.at[6, j], rs_sem.at[j, 3], rows=peer))
        return out

    def sum_zero(block):
        first = p.blocks[block][0]
        for j in p.members[block]:
            jo, size, _, _ = parts_of(j)
            cols = slice(jo - first, jo - first + size)
            s1w1[:, :, :, pl.ds(jo, size)] = acc1[:, cols].astype(BF16).reshape(nt, nr, p.part, size)
            two = acc2[:, cols].astype(BF16).T
            for q in range(nr):
                s1w2[q, pl.ds(jo, size), :] = two[:, p.lanes * q : p.lanes * q + p.lanes]
            start(pair_sends(j))

    def sum_one(j):
        jo, size, _, _ = parts_of(j)
        cols = pl.ds(jo, size)
        arrived(s1w1.at[:, :, :, cols], rs_sem.at[j, 0])
        one = s1w1[:, far, :, cols].astype(F32) + r1w1[1, :, :, cols].astype(F32)
        r1w1[1, :, :, cols] = one.astype(BF16)
        two = s1w2[far, cols, :].astype(F32) + r1w2[1, cols, :].astype(F32)
        r1w2[1, cols, :] = two.astype(BF16)
        start(cross_sends(j))

    def sum_two(j):
        jo, size, start_row, run = parts_of(j)
        cols = pl.ds(jo, size)
        arrived(s1w1.at[:, pl.ds(0, 2), :, cols], rs_sem.at[j, 1])
        one = s1w1[:, me_r, :, cols].astype(F32) + r1w1[0, :, :, cols].astype(F32) + r2w1[:, :, cols].astype(F32)
        r1w1[0, :, :, cols] = one.astype(BF16)
        two = s1w2[me_r, cols, :].astype(F32) + r1w2[0, cols, :].astype(F32) + r2w2[cols, :].astype(F32)
        r1w2[0, cols, :] = two.astype(BF16)
        r3w1[me_t, :, cols] = r1w1[0, me_t, :, cols]
        r3w2[me_t, pl.ds(start_row, run), :] = r1w2[0, pl.ds(pl.multiple_of(jo + run * me_t, run), run), :]
        start(holder_sends(j))

    def sum_three(j):
        jo, size, start_row, run = parts_of(j)
        cols = pl.ds(jo, size)
        arrived(s1w1.at[pl.ds(0, nt - 1), pl.ds(0, 2), :, cols], rs_sem.at[j, 2])
        one = r3w1[0, :, cols].astype(F32)
        two = r3w2[0, pl.ds(start_row, run), :].astype(F32)
        for k in range(1, nt):
            one = one + r3w1[k, :, cols].astype(F32)
            two = two + r3w2[k, pl.ds(start_row, run), :].astype(F32)
        finw1[me_r, :, cols] = one
        finw2[me_r, pl.ds(start_row, run), :] = two
        start(final_sends(j))

    def sum_wait(j):
        jo, size, _, _ = parts_of(j)
        arrived(s1w1.at[pl.ds(0, 3 * nt // 4), pl.ds(0, 2), :, pl.ds(jo, size)], rs_sem.at[j, 3])

    m = p.m
    per = m // TILE

    def rows_add(ref, i, value, first):
        for s in range(per):
            for c in range(p.nc):
                piece = value[TILE * s : TILE * s + TILE, 128 * c : 128 * c + 128]
                place = (i * per + s, c, slice(GAP, GAP + TILE), slice(None))
                ref[place] = piece if first else ref[place] + piece

    bias_two = small_ref[13:14, :]
    last = len(p.blocks) - 1

    def weights_of(j):
        jo, size = p.blocks[j]
        cols = pl.ds(jo, size)
        w1 = w1b[:, :, :, cols].reshape(p.d, size)
        return w1, jnp.concatenate([w2b[q, cols, :] for q in range(nr)], axis=1)

    def back_dot(grad_hidden, w1):
        return lax.dot_general(
            grad_hidden, w1, (((1,), (1,)), ((), ())), preferred_element_type=F32
        )

    def main_block(j, between):
        jo, size = p.blocks[j]
        cols = pl.ds(jo, size)

        @pl.loop(0, t_len // m)
        def _(i):
            for at, task in between:
                pl.when(i == at)(task)
            rows = pl.ds(pl.multiple_of(i * m, m), m)
            w1, w2 = weights_of(j)
            hidden = jnp.dot(nm[rows, :], w1, preferred_element_type=F32) + b1p[0:1, cols]
            grad_act = back_dot(gb[rows, :], w2)
            prob = 0.5 * (1.0 + lax.erf(hidden * RSQRT_HALF))
            bell = jnp.exp(hidden * hidden * np.float32(-0.5)) * RSQRT_2PI
            act = (hidden * prob).astype(BF16)
            grad_hidden = (grad_act * (prob + hidden * bell)).astype(BF16)
            accb[:, cols] += fold(grad_hidden.astype(F32))
            if j == last:
                nm[rows, 0:size] = act
                gb[rows, 0:size] = grad_hidden
            else:
                branch = jnp.dot(act, w2, preferred_element_type=F32)
                br[rows, :] = branch + bias_two if j == 0 else br[rows, :] + branch
                rows_add(gn, i, back_dot(grad_hidden, w1), j == 0)
            one = jnp.dot(nmt[:, rows], grad_hidden, preferred_element_type=F32)
            two = jnp.dot(gbt[:, rows], act, preferred_element_type=F32)
            acc1[:, 0:size] = one + jnp.where(i > 0, acc1[:, 0:size], 0.0)
            acc2[:, 0:size] = two + jnp.where(i > 0, acc2[:, 0:size], 0.0)

    def then(*calls):
        return [(at, functools.partial(task, j)) for at, task, j in calls]

    main_block(0, then((1, gather_one, 3), (1, spread, 5), (1, spread, 6), (2, gather_two, 2), (2, gather_one, 4)))
    sum_zero(0)
    near_wait(2)
    main_block(
        1,
        then((1, sum_one, 0), (1, sum_one, 1), (1, gather_two, 3), (1, gather_one, 5), (2, gather_two, 4), (2, gather_one, 6)),
    )
    sum_zero(1)
    near_wait(3)
    near_wait(4)
    main_block(
        2,
        then((1, sum_one, 2), (1, sum_two, 0), (1, sum_two, 1), (1, gather_two, 5), (2, gather_two, 6)),
    )
    sum_zero(2)
    sum_two(2)
    sum_three(0)
    sum_three(1)
    near_wait(5)
    near_wait(6)
    main_block(3, then((1, sum_one, 3), (1, sum_one, 4)))
    sum_zero(3)
    sum_two(3)
    sum_three(2)

    unit_rows = 2 * TILE

    def backward_dots(u):
        size = p.blocks[last][1]
        rows = pl.ds(pl.multiple_of(u * unit_rows, unit_rows), unit_rows)
        w1, w2 = weights_of(last)
        branch = jnp.dot(nm[rows, 0:size], w2, preferred_element_type=F32)
        br[rows, :] += branch
        back = back_dot(gb[rows, 0:size], w1)
        for s in range(2):
            for c in range(p.nc):
                piece = back[TILE * s : TILE * s + TILE, 128 * c : 128 * c + 128]
                gn[2 * u + s, c, GAP : GAP + TILE, :] += piece

    def backward_tile(b):
        row = pl.multiple_of(b * TILE, TILE)
        step = 32
        for q in range(TILE // step):
            rows = pl.ds(row + q * step, step)
            place = slice(GAP + q * step, GAP + q * step + step)
            accs[11] += fold(ct[rows, :].astype(F32) * br[rows, :])
            grad = jnp.concatenate([gn[b, c, place, :] for c in range(p.nc)], axis=1)
            unit = xhat[rows, :].astype(F32)
            both_of = grad * unit
            accs[8] += fold(both_of)
            accs[9] += fold(grad)
            u = grad * gain
            mean_u = jnp.sum(u, axis=1, keepdims=True) * (1.0 / p.d)
            mean_x = jnp.sum(both_of * gain, axis=1, keepdims=True) * (1.0 / p.d)
            inverse = rstd[rows, :]
            inverse = jnp.concatenate([inverse] * p.nc, axis=1)
            rounded = ((u - mean_u - unit * mean_x) * inverse).astype(BF16)
            low = rounded.astype(F32)
            accs[7] += fold(low)
            for c in range(p.nc):
                gn[b, c, place, :] = low[:, 128 * c : 128 * c + 128]
        for c in range(p.nc):
            cols = slice(128 * c, 128 * c + 128)
            low = gn[b, c, GAP : GAP + TILE, :]
            for k in range(TAPS):
                first = GAP - 3 + k
                accs[k, :, cols] += fold(low * xf[b, c, first : first + TILE, :])

    def edge_sends():
        after, before = (me_t + 1) % nt, (me_t + nt - 1) % nt
        return [
            remote(gn.at[nb - 1, :, pl.ds(TILE, GAP), :], hprev, send_sem.at[7, 2], halo_sem.at[2], tm=after),
            remote(gn.at[0, :, pl.ds(GAP, GAP), :], hnext, send_sem.at[7, 3], halo_sem.at[3], tm=before),
        ]

    backward_dots(0)
    units = nb // 2

    @pl.loop(0, units - 1)
    def _(u):
        for at, task in then(
            (1, sum_one, 5), (1, sum_one, 6), (2, sum_two, 4), (6, sum_two, 5), (6, sum_three, 3), (8, sum_three, 4), (9, sum_two, 6)
        ):
            pl.when(u == at)(task)
        backward_dots(u + 1)
        backward_tile(2 * u)
        backward_tile(2 * u + 1)

    @pl.loop(nb - 2, nb)
    def _(b):
        backward_tile(b)

    start(edge_sends())

    hidden_tiles = lane_permuted(lambda i: accb[:, 128 * i : 128 * i + 128], p.regrouped, p.ff // 128)
    for c in range(p.nc):
        cols = slice(128 * c, 128 * c + 128)
        line = []
        for k in range(10):
            line.append(jnp.sum(accs[k, :, cols], axis=0, keepdims=True))
        for i in range(3):
            line.append(jnp.sum(hidden_tiles[i * p.nc + c], axis=0, keepdims=True))
        for k in (10, 11):
            line.append(jnp.sum(accs[k, :, cols], axis=0, keepdims=True))
        line.append(jnp.zeros((1, 128), F32))
        sma[c] = jnp.concatenate(line, axis=0)

    def small_one_sends():
        out = []
        for step in range(1, nr):
            peer = (me_r + step) % nr
            out.append(remote(sma.at[peer], smr.at[me_r], send_sem.at[7, 4], sm_sem.at[0], rows=peer))
        return out

    def small_two_sends():
        out = []
        for step in range(1, nt):
            peer = (me_t + step) % nt
            out.append(remote(smq.at[nt], smq.at[me_t], send_sem.at[8, 0], sm_sem.at[1], tm=peer))
        return out

    def small_three_sends():
        out = []
        for step in range(1, nr):
            peer = (me_r + step) % nr
            out.append(remote(smf.at[me_r], smf.at[me_r], send_sem.at[8, 1], sm_sem.at[2], rows=peer))
        return out

    smr[me_r] = sma[me_r]
    start(small_one_sends())

    def small_two():
        arrived(smr.at[pl.ds(0, nr - 1)], sm_sem.at[0])
        total = smr[0]
        for k in range(1, nr):
            total = total + smr[k]
        smq[nt] = total
        smq[me_t] = total
        start(small_two_sends())

    def small_three():
        arrived(smq.at[pl.ds(0, nt - 1)], sm_sem.at[1])
        total = smq[0]
        for k in range(1, nt):
            total = total + smq[k]
        smf[me_r] = total
        start(small_three_sends())

    def exchange_edges(b):
        same = flags[pl.ds(b, 1), :] < 0.5
        for c in range(p.nc):
            gn[b, c, 0:GAP, :] = jnp.where(same, gn[b - 1, c, TILE : TILE + GAP, :], 0.0)
            gn[b - 1, c, GAP + TILE :, :] = jnp.where(same, gn[b, c, GAP : GAP + GAP, :], 0.0)

    def last_tile(b):
        row = pl.multiple_of(b * TILE, TILE)
        rows = pl.ds(row, TILE)
        for c in range(p.nc):
            cols = slice(128 * c, 128 * c + 128)
            source = frx[pl.ds(row + HALO, TILE), cols].astype(F32)
            nm[rows, cols] = (source + scale[:, cols] * br[rows, cols]).astype(BF16)
            total = ct[rows, cols].astype(F32)
            for k in range(TAPS):
                first = GAP + 3 - k
                total = total + small_ref[k : k + 1, cols] * gn[b, c, first : first + TILE, :]
            gb[rows, cols] = total.astype(BF16)

    exchange_edges(1)

    def last_tiles(low, high):
        @pl.loop(low, high)
        def _(b):
            exchange_edges(b + 1)
            last_tile(b)

    cut = [1, 1 + (nb - 2) // 2, 1 + (nb - 2) * 3 // 4, nb - 1]
    last_tiles(cut[0], cut[1])
    small_two()
    sum_three(5)
    last_tiles(cut[1], cut[2])
    sum_three(6)
    last_tiles(cut[2], cut[3])
    arrived(hprev, halo_sem.at[2])
    arrived(hnext, halo_sem.at[3])
    for c in range(p.nc):
        gn[0, c, 0:GAP, :] = jnp.where(flags[0:1, :] < 0.5, hprev[c], 0.0)
        gn[nb - 1, c, GAP + TILE :, :] = jnp.where(flags[nb : nb + 1, :] < 0.5, hnext[c], 0.0)

    @pl.loop(0, 2)
    def _(i):
        last_tile(i * (nb - 1))

    small_three()

    for j in range(len(p.chunks)):
        sum_wait(j)
    arrived(smf.at[pl.ds(0, nr - 1)], sm_sem.at[2])
    for c in range(p.nc):
        small_out[:, 128 * c : 128 * c + 128] = smf[c]

    sent = halo_sends() + edge_sends() + small_one_sends() + small_two_sends() + small_three_sends()
    for j in range(len(p.chunks)):
        sent += spread_sends(j) + far_sends(j) + near_sends(j, me_r) + near_sends(j, far)
        sent += pair_sends(j) + cross_sends(j) + holder_sends(j) + final_sends(j)
    for copy in sent:
        copy.wait_send()
    for load in rest:
        load.wait()


def finish_kernel(
    plan,
    nm, gb, grad1, grad2, grad_small, state1, state2,
    small_master, small_first, small_second, small_average,
    output, ingrad, *rest,
):
    p = plan
    outs1, outs2, outs_small = rest[0:5], rest[5:10], rest[10:15]
    new1, low1, new2, low2, sem = rest[15:]
    copies = [
        pltpu.make_async_copy(nm, output.at[0], sem.at[0]),
        pltpu.make_async_copy(gb, ingrad.at[0], sem.at[1]),
    ]
    for copy in copies:
        copy.start()

    def first_grad(q):
        tiles = lane_permuted(
            lambda i: grad1[q, :, 128 * i : 128 * i + 128], p.regrouped, p.ff // 128
        )
        return jnp.concatenate(tiles, axis=1)

    def second_grad(q):
        rows = slice(q * p.part, q * p.part + p.part)
        return jnp.concatenate([grad2[k, rows, :] for k in range(p.nr)], axis=1)

    count = 2
    for grad, state, new, low, outs, rate in (
        (first_grad, state1, new1, low1, outs1, rate_first),
        (second_grad, state2, new2, low2, outs2, rate_second),
    ):
        for q in range(low.shape[0] // p.part):
            rows = slice(q * p.part, q * p.part + p.part)
            got = adamw_step(
                state[0, rows], state[1, rows], state[2, rows], state[3, rows], grad(q), rate
            )
            for k in range(4):
                new[k, rows] = got[k]
            low[rows] = got[4]
        for k in range(5):
            source = low if k == 4 else new.at[k]
            copy = pltpu.make_async_copy(source, outs[k], sem.at[count])
            copy.start()
            copies.append(copy)
            count += 1
    got = adamw_step(
        small_master[...], small_first[...], small_second[...], small_average[...], grad_small[0:15], rate_small
    )
    for k in range(5):
        outs_small[k][...] = got[k]
    for copy in copies:
        copy.wait()


def finish(plan, kept, smalls):
    vmem = pl.BlockSpec(memory_space=pltpu.VMEM)
    anyplace = pl.BlockSpec(memory_space=pl.ANY)
    kept = [pltpu.with_memory_space_constraint(value, pltpu.VMEM) for value in kept]
    shape1, shape2 = (plan.rows1, plan.ff), (plan.share, plan.d)
    whole = jax.ShapeDtypeStruct((1, plan.t, plan.d), BF16)

    def five(shape):
        return [jax.ShapeDtypeStruct(shape, F32)] * 4 + [jax.ShapeDtypeStruct(shape, BF16)]

    v = pltpu.VMEM
    return pl.pallas_call(
        functools.partial(finish_kernel, plan),
        out_shape=(whole, whole, *five(shape1), *five(shape2), *five(smalls[0].shape)),
        in_specs=[vmem] * 11,
        out_specs=(anyplace,) * 12 + (vmem,) * 5,
        scratch_shapes=[
            v((4, *shape1), F32),
            v(shape1, BF16),
            v((4, *shape2), F32),
            v(shape2, BF16),
            pltpu.SemaphoreType.DMA((12,)),
        ],
        compiler_params=pltpu.CompilerParams(vmem_limit_bytes=8_000_000),
    )(*kept, *smalls)


def call(plan, frames, cotangent, lengths, one, two, small_master):
    p = plan
    t, d, ff, nt, nr, nb, nc = p.t, p.d, p.ff, p.nt, p.nr, p.nb, p.nc
    vmem = pl.BlockSpec(memory_space=pltpu.VMEM)
    anyplace = pl.BlockSpec(memory_space=pl.ANY)
    n_lens = -(-lengths.shape[1] // 128) * 128
    v = pltpu.VMEM
    scratch = [
        v((t + 2 * HALO, d), BF16),
        v((t, d), BF16),
        v((d, t), BF16),
        v((d, t), BF16),
        v((t, d), F32),
        v((nb, nc, TILE + 2 * GAP, 128), F32),
        v((nb, nc, TILE + 2 * GAP, 128), F32),
        v((t, d), BF16),
        v((t, 128), F32),
        v((nt, nr, p.part, ff), BF16),
        v((nr, ff, p.lanes), BF16),
        v((d, p.widest), F32),
        v((d, p.widest), F32),
        v((8, n_lens), F32),
        v((-(-(nb + 1) // 8) * 8, 128), F32),
        v((8, ff), F32),
        v((12, 8, d), F32),
        v((8, ff), F32),
        v((TILE, d), F32),
        v((nt, nr, p.part, ff), BF16),
        v((nr, ff, p.lanes), BF16),
        v((2, nt, p.part, ff), BF16),
        v((2, ff, p.lanes), BF16),
        v((nt, p.part, ff), BF16),
        v((ff, p.lanes), BF16),
        v((nt, p.part, ff), BF16),
        v((nt, p.share, p.lanes), BF16),
        v((nr, 16, p.lanes), F32),
        v((nr, 16, p.lanes), F32),
        v((nt + 1, 16, p.lanes), F32),
        v((nr, 16, p.lanes), F32),
        v((nc, GAP, 128), F32),
        v((nc, GAP, 128), F32),
        pltpu.SemaphoreType.DMA((5,)),
        pltpu.SemaphoreType.DMA((9, len(p.chunks))),
        pltpu.SemaphoreType.DMA((4,)),
        pltpu.SemaphoreType.DMA((len(p.chunks), 3)),
        pltpu.SemaphoreType.DMA((len(p.chunks), 4)),
        pltpu.SemaphoreType.DMA((3,)),
    ]
    return pl.pallas_call(
        functools.partial(kernel, plan),
        out_shape=(
            v((t, d), BF16),
            v((t, d), BF16),
            v((nr, p.part, ff), F32),
            v((nr, p.share, p.lanes), F32),
            v((16, d), F32),
            v((4, p.rows1, ff), F32),
            v((4, p.share, d), F32),
        ),
        in_specs=[anyplace, anyplace, vmem] + [anyplace] * 8 + [vmem],
        out_specs=(vmem,) * 7,
        scratch_shapes=scratch,
        compiler_params=pltpu.CompilerParams(
            collective_id=0, has_side_effects=True, vmem_limit_bytes=56_500_000
        ),
    )(frames, cotangent, lengths, *one, *two, small_master)


def padded_2(array, sides, width):
    for axis, dim in sides:
        devices, length = (lax.axis_size(axis), array.shape[dim])
        up = [(i, (i + 1) % devices) for i in range(devices - 1)]
        down = [(j, i) for i, j in up]
        last = lax.slice_in_dim(array, length - width, length, axis=dim)
        leading = lax.slice_in_dim(array, 0, width, axis=dim)
        before = lax.ppermute(last, axis, up)
        after = lax.ppermute(leading, axis, down)
        array = jnp.concatenate([before, array, after], axis=dim)
    return array


def cut_along(array, dim, devices):
    before, after = (array.shape[:dim], array.shape[dim + 1 :])
    return jnp.moveaxis(array.reshape(*before, devices, -1, *after), dim, 0)


def sent_and_summed(array, axis, dim):
    devices = lax.axis_size(axis)
    pieces = lax.all_to_all(cut_along(array, dim, devices), axis, 0, 0, tiled=True)
    return jnp.sum(pieces.astype(jnp.float32), axis=0)


def edge_masks(lengths_row, first_frame, frame_count):
    ends_at = jnp.cumsum(lengths_row, dtype=jnp.int32)
    places = first_frame + jnp.arange(frame_count, dtype=jnp.int32)
    passed = ends_at[None, :] <= places[:, None]
    lower = jnp.max(jnp.where(passed, ends_at[None, :], 0), axis=1)
    upper = jnp.min(jnp.where(passed, ends_at[-1], ends_at[None, :]), axis=1)
    mask_rows = []
    for tap_index in range(7):
        spot_now = places + (tap_index - 3)
        mask_rows.append(((spot_now >= lower) & (spot_now < upper)).astype(jnp.float32))
    return jnp.stack(mask_rows)


def depthwise(padded, tap_rows, masks, frame_count):
    summed = jnp.zeros((frame_count, padded.shape[1]), jnp.float32)
    for tap_index in range(7):
        window = padded[tap_index : tap_index + frame_count].astype(jnp.float32)
        summed = summed + tap_rows[tap_index][None, :] * window * masks[tap_index][:, None]
    return summed


def layer_norm(conv_out, norm_gain, norm_bias):
    centred = conv_out - jnp.mean(conv_out, axis=-1, keepdims=True)
    spread = jnp.mean(centred * centred, axis=-1, keepdims=True)
    return centred * lax.rsqrt(spread + norm_eps) * norm_gain[None, :] + norm_bias[None, :]


def exact_gelu(values):
    return jax.nn.gelu(values, approximate=False)


def frame_product(left_side, right_side):
    return lax.dot_general(
        left_side, right_side, (((0,), (0,)), ((), ())), preferred_element_type=jnp.float32
    )


def plain_body(
    frames,
    cotangent,
    lengths,
    w1_master,
    w1_first,
    w1_second,
    w1_average,
    w2_master,
    w2_first,
    w2_second,
    w2_average,
    small_master,
    small_first,
    small_second,
    small_average,
):
    frame_count = frames.shape[1]
    width = frames.shape[2]
    w1_low, w2_low = (
        lax.all_gather(w1_master.astype(jnp.bfloat16), "tm", axis=0, tiled=True),
        lax.all_gather(w2_master.astype(jnp.bfloat16), "tm", axis=0, tiled=True),
    )
    inputs = frames[0]
    upstream = cotangent[0].astype(jnp.float32)
    masks = edge_masks(lengths[0], lax.axis_index("tm") * frame_count, frame_count)
    tap_rows = small_master[0:7]
    layer_scale = small_master[14]
    padded = padded_2(inputs, (("tm", 0),), 3)
    conv_out = depthwise(padded, tap_rows, masks, frame_count) + small_master[7][None, :]
    normed, norm_back = jax.vjp(layer_norm, conv_out, small_master[8], small_master[9])
    normed_low = normed.astype(jnp.bfloat16)
    hidden = (
        jnp.dot(normed_low, w1_low, preferred_element_type=jnp.float32)
        + small_master[10:13].reshape(-1)[None, :]
    )
    activated, gelu_back = jax.vjp(exact_gelu, hidden)
    act_low = activated.astype(jnp.bfloat16)
    branch = (
        jnp.dot(act_low, w2_low, preferred_element_type=jnp.float32) + small_master[13][None, :]
    )
    output = (inputs.astype(jnp.float32) + layer_scale[None, :] * branch).astype(jnp.bfloat16)
    grad_scale = jnp.sum(upstream * branch, axis=0)
    grad_branch = (layer_scale[None, :] * upstream).astype(jnp.bfloat16)
    grad_act = lax.dot_general(
        grad_branch, w2_low, (((1,), (1,)), ((), ())), preferred_element_type=jnp.float32
    )
    grad_hidden = gelu_back(grad_act)[0].astype(jnp.bfloat16)
    grad_normed = lax.dot_general(
        grad_hidden, w1_low, (((1,), (1,)), ((), ())), preferred_element_type=jnp.float32
    )
    grad_conv, grad_gain, grad_shift = norm_back(grad_normed)
    grad_low = grad_conv.astype(jnp.bfloat16)
    grad_pad = padded_2(grad_low, (("tm", 0),), 3)
    input_grad = (upstream + depthwise(grad_pad, tap_rows[::-1], masks, frame_count)).astype(
        jnp.bfloat16
    )
    grad_float = grad_low.astype(jnp.float32)
    grad_taps = jnp.stack(
        [
            jnp.sum(
                grad_float
                * padded[tap_index : tap_index + frame_count].astype(jnp.float32)
                * masks[tap_index][:, None],
                axis=0,
            )
            for tap_index in range(7)
        ]
    )
    middle_rows = jnp.stack([jnp.sum(grad_float, axis=0), grad_gain, grad_shift])
    bias_rows = jnp.sum(grad_hidden.astype(jnp.float32), axis=0).reshape(3, width)
    last_rows = jnp.stack([jnp.sum(grad_branch.astype(jnp.float32), axis=0), grad_scale])
    small_grad = jnp.concatenate([grad_taps, middle_rows, bias_rows, last_rows], axis=0)
    full_one = frame_product(normed_low, grad_hidden)
    full_two = frame_product(act_low, grad_branch)
    share_one, share_two = (
        sent_and_summed(full_one.astype(jnp.bfloat16), "tm", 0),
        sent_and_summed(full_two.astype(jnp.bfloat16), "tm", 0),
    )
    grad_one, grad_two = (
        lax.psum(share_one.astype(jnp.bfloat16), "rows").astype(jnp.float32),
        lax.psum(share_two.astype(jnp.bfloat16), "rows").astype(jnp.float32),
    )
    small_total = lax.psum(small_grad, ("tm", "rows"))
    one_out = adamw_step(w1_master, w1_first, w1_second, w1_average, grad_one, rate_first)
    two_out = adamw_step(w2_master, w2_first, w2_second, w2_average, grad_two, rate_second)
    small_out = adamw_step(
        small_master, small_first, small_second, small_average, small_total, rate_small
    )
    return (
        output[None],
        input_grad[None],
        one_out[0],
        one_out[1],
        one_out[2],
        one_out[3],
        one_out[4],
        two_out[0],
        two_out[1],
        two_out[2],
        two_out[3],
        two_out[4],
        small_out[0],
        small_out[1],
        small_out[2],
        small_out[3],
        small_out[4],
    )


def body(
    frames,
    cotangent,
    lengths,
    w1_master,
    w1_first,
    w1_second,
    w1_average,
    w2_master,
    w2_first,
    w2_second,
    w2_average,
    small_master,
    small_first,
    small_second,
    small_average,
):
    nt, nr = lax.axis_size("tm"), lax.axis_size("rows")
    plan = Plan(nt, nr, frames.shape[1], frames.shape[2], w1_master.shape[1])
    kept = call(
        plan,
        frames,
        cotangent,
        lengths,
        (w1_master, w1_first, w1_second, w1_average),
        (w2_master, w2_first, w2_second, w2_average),
        small_master,
    )
    return finish(plan, kept, (small_master, small_first, small_second, small_average))


def solution(mesh):
    in_specs = (
        P("rows", "tm", None),
        P("rows", "tm", None),
        P("rows", None),
        P("tm", None),
        P("tm", None),
        P("tm", None),
        P("tm", None),
        P("tm", None),
        P("tm", None),
        P("tm", None),
        P("tm", None),
        P(),
        P(),
        P(),
        P(),
    )
    out_specs = (
        P("rows", "tm", None),
        P("rows", "tm", None),
        P("tm", None),
        P("tm", None),
        P("tm", None),
        P("tm", None),
        P("tm", None),
        P("tm", None),
        P("tm", None),
        P("tm", None),
        P("tm", None),
        P("tm", None),
        P(),
        P(),
        P(),
        P(),
        P(),
    )
    fits = mesh.shape["tm"] == 8 and mesh.shape["rows"] == 4
    return jax.shard_map(body if fits else plain_body, mesh=mesh, in_specs=in_specs, out_specs=out_specs, check_vma=False)
```

```python
import functools

import jax
import jax.numpy as jnp
import numpy as np
from jax import lax
from jax.experimental import pallas as pl
from jax.experimental.pallas import tpu as pltpu
from jax.sharding import PartitionSpec as P

ADAM_STEP = 3
norm_eps = 1e-06
adam_eps = 1e-08
weight_decay = 0.01
beta_first = 0.5
beta_second = 0.5
average_keep = 0.75
rate_first = 0.08
rate_second = 0.05
rate_small = 0.4

TAPS = 7
TILE = 128
GAP = 8
GRAIN = 16
HALO = 16
F32 = jnp.float32
BF16 = jnp.bfloat16
MESH = pl.DeviceIdType.MESH
RSQRT_HALF = np.float32(0.7071067811865476)
RSQRT_2PI = np.float32(0.3989422804014327)


def adamw_step(master, first_old, second_old, average_old, gradient, rate):
    first_new = beta_first * first_old + (1.0 - beta_first) * gradient
    second_new = beta_second * second_old + (1.0 - beta_second) * gradient * gradient
    first_hat = first_new / (1.0 - beta_first**ADAM_STEP)
    second_hat = second_new / (1.0 - beta_second**ADAM_STEP)
    master_new = master - rate * (
        first_hat / (jnp.sqrt(second_hat) + adam_eps) + weight_decay * master
    )
    average_new = average_keep * average_old + (1.0 - average_keep) * master_new
    return (master_new, first_new, second_new, average_new, master_new.astype(BF16))


class Plan:
    def __init__(self, nt, nr, frame_count, width, hidden):
        self.nt, self.nr, self.t, self.d, self.ff = nt, nr, frame_count, width, hidden
        self.share = hidden // nt
        self.rows1 = width // nt
        self.part = self.rows1 // nr
        self.lanes = width // nr
        self.nb = frame_count // TILE
        self.nc = width // 128
        self.chunks = []
        offset = begin = 0
        for run in (16, 16, 32, 32, 32, 32, 32):
            self.chunks.append((offset, run * nt, run, begin))
            offset += run * nt
            begin += run
        self.members = [(0, 1), (2,), (3, 4), (5, 6)]
        self.blocks = [
            (self.chunks[own[0]][0], sum(self.chunks[j][1] for j in own)) for own in self.members
        ]
        self.widest = max(size for _, size in self.blocks)
        self.m = 1024
        self.natural = []
        for _, _, run, begin in self.chunks:
            for k in range(nt):
                for o in range(0, run, GRAIN):
                    self.natural.append((self.share * k + begin + o) // GRAIN)
        self.regrouped = [self.natural.index(g) for g in range(hidden // GRAIN)]


def lane_permuted(tile_of, source, count):
    per = 128 // GRAIN
    out = []
    for tile in range(count):
        value, before = None, None
        for q in range(per):
            run = source[tile * per + q]
            now = (run // per, (q - run % per) % per)
            if now == before:
                continue
            before = now
            piece = tile_of(now[0])
            if now[1]:
                piece = pltpu.roll(piece, now[1] * GRAIN, 1)
            if value is None:
                value = piece
            else:
                lane = lax.broadcasted_iota(jnp.int32, piece.shape, 1)
                value = jnp.where(lane >= q * GRAIN, piece, value)
        out.append(value)
    return out


def fold(value):
    rows = value.shape[0]
    total = value[0:8]
    for g in range(1, rows // 8):
        total = total + value[8 * g : 8 * g + 8]
    return total


def kernel(
    plan,
    frames_hbm,
    cot_hbm,
    lengths_hbm,
    w1_hbm,
    w1_first_hbm,
    w1_second_hbm,
    w1_average_hbm,
    w2_hbm,
    w2_first_hbm,
    w2_second_hbm,
    w2_average_hbm,
    small_hbm,
    nm,
    gb,
    finw1,
    finw2,
    small_out,
    state1,
    state2,
    frx,
    ct,
    nmt,
    gbt,
    br,
    gn,
    xf,
    xhat,
    rstd,
    w1b,
    w2b,
    acc1,
    acc2,
    lengths_ref,
    small_ref,
    lens,
    flags,
    b1p,
    accs,
    accb,
    tmp,
    s1w1,
    s1w2,
    r1w1,
    r1w2,
    r2w1,
    r2w2,
    r3w1,
    r3w2,
    sma,
    smr,
    smq,
    smf,
    hprev,
    hnext,
    in_sem,
    send_sem,
    halo_sem,
    ag_sem,
    rs_sem,
    sm_sem,
):
    p = plan
    nt, nr, t_len = p.nt, p.nr, p.t
    me_t = lax.axis_index("tm")
    me_r = lax.axis_index("rows")
    near = me_r + 1 - 2 * (me_r % 2)
    far = (me_r + 2) % nr
    both = near + 2 - 4 * (near // 2)

    def remote(src, dst, send, recv, tm=None, rows=None):
        device = {"tm": me_t if tm is None else tm, "rows": me_r if rows is None else rows}
        return pltpu.make_async_remote_copy(
            src_ref=src, dst_ref=dst, send_sem=send, recv_sem=recv,
            device_id=device, device_id_type=MESH,
        )

    def arrived(view, sem):
        pltpu.make_async_copy(view, view, sem).wait()

    loads = [
        pltpu.make_async_copy(w1_hbm, state1.at[0], in_sem.at[0]),
        pltpu.make_async_copy(w2_hbm, state2.at[0], in_sem.at[1]),
        pltpu.make_async_copy(frames_hbm.at[0], frx.at[pl.ds(HALO, t_len)], in_sem.at[2]),
        pltpu.make_async_copy(cot_hbm.at[0], ct, in_sem.at[3]),
        pltpu.make_async_copy(lengths_hbm, lengths_ref, in_sem.at[5]),
        pltpu.make_async_copy(small_hbm, small_ref, in_sem.at[6]),
    ]
    for k in (0, 1, 5, 4, 2, 3):
        loads[k].start()

    barrier = pltpu.get_barrier_semaphore()
    for step in range(1, nt):
        pl.semaphore_signal(
            barrier, inc=1, device_id={"tm": (me_t + step) % nt, "rows": me_r}, device_id_type=MESH
        )
    for step in range(1, nr):
        pl.semaphore_signal(
            barrier, inc=1, device_id={"tm": me_t, "rows": (me_r + step) % nr}, device_id_type=MESH
        )

    loads[4].wait()
    loads[5].wait()
    lens[...] = jnp.zeros_like(lens)
    n_len = lengths_ref.shape[1]
    lens[0:1, 0:n_len] = lengths_ref[...].astype(F32)
    ends = lens[...]
    lane = lax.broadcasted_iota(jnp.int32, ends.shape, 1)
    shift = 1
    while shift < lens.shape[1]:
        ends = ends + jnp.where(lane >= shift, pltpu.roll(ends, shift, 1), 0.0)
        shift *= 2
    n_flag = flags.shape[0]
    spot = me_t * t_len + TILE * lax.broadcasted_iota(jnp.int32, (n_flag, lens.shape[1]), 0)
    hit = (ends[0:1, :] == spot.astype(F32)) | (spot == 0)
    edge = jnp.max(jnp.where(hit, 1.0, 0.0), axis=1, keepdims=True)
    flags[...] = jnp.broadcast_to(edge, flags.shape)
    accs[...] = jnp.zeros_like(accs)
    ones_row = lax.broadcasted_iota(jnp.int32, (16, t_len), 0) == 0
    nmt[p.d :, :] = jnp.where(ones_row, 1.0, 0.0).astype(BF16)
    bias_tiles = lane_permuted(
        lambda i: jnp.broadcast_to(small_ref[10 + i // p.nc : 11 + i // p.nc, 128 * (i % p.nc) : 128 * (i % p.nc) + 128], (8, 128)),
        p.natural,
        p.ff // 128,
    )
    for i, tile in enumerate(bias_tiles):
        b1p[:, 128 * i : 128 * i + 128] = tile

    loads[0].wait()
    loads[1].wait()
    own_rows = pl.ds(pl.multiple_of(me_r * p.part, p.part), p.part)
    own_lanes = pl.ds(pl.multiple_of(me_r * p.lanes, p.lanes), p.lanes)
    own1 = lane_permuted(lambda i: state1[0, own_rows, 128 * i : 128 * i + 128], p.natural, p.ff // 128)
    for i, tile in enumerate(own1):
        w1b[me_t, me_r, :, 128 * i : 128 * i + 128] = tile.astype(BF16)
    for jo, _, run, begin in p.chunks:
        w2b[me_r, pl.ds(pl.multiple_of(jo + run * me_t, run), run), :] = state2[0, begin : begin + run, own_lanes].astype(BF16)

    pl.semaphore_wait(barrier, nt + nr - 2)

    def halo_sends():
        after, before = (me_t + 1) % nt, (me_t + nt - 1) % nt
        return [
            remote(frames_hbm.at[0, pl.ds(t_len - HALO, HALO)], frx.at[pl.ds(0, HALO)], send_sem.at[7, 0], halo_sem.at[0], tm=after),
            remote(frames_hbm.at[0, pl.ds(0, HALO)], frx.at[pl.ds(HALO + t_len, HALO)], send_sem.at[7, 1], halo_sem.at[1], tm=before),
        ]

    def w1_part(j, q):
        jo, size = p.chunks[j][:2]
        return w1b.at[:, q, :, pl.ds(jo, size)]

    def w2_part(j, q):
        jo, size = p.chunks[j][:2]
        return w2b.at[q, pl.ds(jo, size), :]

    def spread_sends(j):
        jo, size, run, _ = p.chunks[j]
        out = []
        for step in range(1, nt):
            peer = (me_t + step) % nt
            one = w1b.at[me_t, me_r, :, pl.ds(jo, size)]
            two = w2b.at[me_r, pl.ds(pl.multiple_of(jo + run * me_t, run), run), :]
            out.append(remote(one, one, send_sem.at[0, j], ag_sem.at[j, 0], tm=peer))
            out.append(remote(two, two, send_sem.at[0, j], ag_sem.at[j, 0], tm=peer))
        return out

    def spread_wait(j, sem=None):
        jo, size = p.chunks[j][:2]
        arrived(w1b.at[pl.ds(0, nt - 1), pl.ds(0, 2), :, pl.ds(jo, size)], ag_sem.at[j, 0] if sem is None else sem)

    def far_sends(j):
        return [
            remote(w1_part(j, me_r), w1_part(j, me_r), send_sem.at[1, j], ag_sem.at[j, 1], rows=far),
            remote(w2_part(j, me_r), w2_part(j, me_r), send_sem.at[1, j], ag_sem.at[j, 1], rows=far),
        ]

    def far_wait(j, sem=None):
        jo, size = p.chunks[j][:2]
        arrived(w1b.at[:, pl.ds(0, 2), :, pl.ds(jo, size)], ag_sem.at[j, 1] if sem is None else sem)

    def near_sends(j, q):
        return [
            remote(w1_part(j, q), w1_part(j, q), send_sem.at[2, j], ag_sem.at[j, 2], rows=near),
            remote(w2_part(j, q), w2_part(j, q), send_sem.at[2, j], ag_sem.at[j, 2], rows=near),
        ]

    def near_wait(j, sem=None):
        jo, size = p.chunks[j][:2]
        arrived(w1b.at[:, :, :, pl.ds(jo, size)], ag_sem.at[j, 2] if sem is None else sem)

    def start(copies):
        for copy in copies:
            copy.start()

    def gather_one(j):
        spread_wait(j)
        start(far_sends(j))
        start(near_sends(j, me_r))

    def gather_two(j):
        far_wait(j)
        start(near_sends(j, far))

    def spread(j):
        start(spread_sends(j))

    spread(0)
    spread(1)
    start(halo_sends())

    rest = [
        pltpu.make_async_copy(source, target, in_sem.at[4])
        for source, target in (
            (w1_first_hbm, state1.at[1]),
            (w1_second_hbm, state1.at[2]),
            (w1_average_hbm, state1.at[3]),
            (w2_first_hbm, state2.at[1]),
            (w2_second_hbm, state2.at[2]),
            (w2_average_hbm, state2.at[3]),
        )
    ]
    for load in rest:
        load.start()
    loads[2].wait()
    loads[3].wait()

    gain = small_ref[8:9, :]
    shift_row = small_ref[9:10, :]
    scale = small_ref[14:15, :]

    first_row = jnp.where(lax.broadcasted_iota(jnp.int32, (8, TILE), 0) == 0, 1.0, 0.0).astype(BF16)

    def turn_tile(b):
        row = pl.multiple_of(b * TILE, TILE)
        nmt[0 : p.d, pl.ds(row, TILE)] = nm[pl.ds(row, TILE), :].T
        gbt[:, pl.ds(row, TILE)] = gb[pl.ds(row, TILE), :].T

    def forward_tile(b, turned=None):
        if turned is not None:
            turn_tile(turned)
        row = pl.multiple_of(b * TILE, TILE)
        starts_here = flags[pl.ds(b, 1), :]
        ends_here = flags[pl.ds(b + 1, 1), :]
        lead = frx[pl.ds(row, HALO), :].astype(F32)
        trail = frx[pl.ds(row + HALO + TILE, HALO), :].astype(F32)
        for c in range(p.nc):
            cols = slice(128 * c, 128 * c + 128)
            xf[b, c, GAP : GAP + TILE, :] = frx[pl.ds(row + HALO, TILE), cols].astype(F32)
            xf[b, c, 0:GAP, :] = jnp.where(starts_here > 0.5, 0.0, lead[HALO - GAP :, cols])
            xf[b, c, GAP + TILE :, :] = jnp.where(ends_here > 0.5, 0.0, trail[0:GAP, cols])
        for c in range(p.nc):
            cols = slice(128 * c, 128 * c + 128)
            total = jnp.broadcast_to(small_ref[7:8, cols], (TILE, 128))
            for k in range(TAPS):
                first = GAP - 3 + k
                total = total + small_ref[k : k + 1, cols] * xf[b, c, first : first + TILE, :]
            tmp[:, cols] = total
        step = 32
        for q in range(TILE // step):
            rows = pl.ds(row + q * step, step)
            value = tmp[q * step : q * step + step, :]
            centred = value - jnp.sum(value, axis=1, keepdims=True) * (1.0 / p.d)
            spread = jnp.sum(centred * centred, axis=1, keepdims=True) * (1.0 / p.d)
            inverse = lax.rsqrt(spread + norm_eps)
            unit = centred * inverse
            rstd[rows, :] = jnp.broadcast_to(inverse, (step, 128))
            xhat[rows, :] = unit.astype(BF16)
            nm[rows, :] = (unit * gain + shift_row).astype(BF16)
            low = (scale * ct[rows, :].astype(F32)).astype(BF16)
            gb[rows, :] = low
        accs[10] += jnp.dot(first_row, gb[pl.ds(row, TILE), :], preferred_element_type=F32)

    def forward_tiles(low, high):
        @pl.loop(low, high)
        def _(b):
            forward_tile(b, b - 1)

    nb = p.nb
    forward_tile(1)
    forward_tiles(2, nb // 4 - 1)
    spread(2)
    forward_tiles(nb // 4 - 1, nb * 5 // 12)
    gather_one(0)
    spread(3)
    spread(4)
    forward_tiles(nb * 5 // 12, nb * 7 // 12)
    gather_one(1)
    forward_tiles(nb * 7 // 12, nb * 3 // 4)
    gather_two(0)
    arrived(frx.at[pl.ds(HALO + t_len, HALO)], halo_sem.at[1])
    forward_tiles(nb * 3 // 4, nb)
    gather_two(1)
    gather_one(2)
    arrived(frx.at[pl.ds(0, HALO)], halo_sem.at[0])
    forward_tile(0, nb - 1)
    turn_tile(0)
    near_wait(0)
    near_wait(1)

    def parts_of(j):
        jo, size, run, begin = p.chunks[j]
        return jo, size, begin, run

    def pair_sends(j):
        jo, size, _, _ = parts_of(j)
        out = []
        for slot, q in ((0, near), (1, both)):
            out.append(remote(s1w1.at[:, q, :, pl.ds(jo, size)], r1w1.at[slot, :, :, pl.ds(jo, size)], send_sem.at[3, j], rs_sem.at[j, 0], rows=near))
            out.append(remote(s1w2.at[q, pl.ds(jo, size), :], r1w2.at[slot, pl.ds(jo, size), :], send_sem.at[3, j], rs_sem.at[j, 0], rows=near))
        return out

    def cross_sends(j):
        jo, size, _, _ = parts_of(j)
        return [
            remote(r1w1.at[1, :, :, pl.ds(jo, size)], r2w1.at[:, :, pl.ds(jo, size)], send_sem.at[4, j], rs_sem.at[j, 1], rows=far),
            remote(r1w2.at[1, pl.ds(jo, size), :], r2w2.at[pl.ds(jo, size), :], send_sem.at[4, j], rs_sem.at[j, 1], rows=far),
        ]

    def holder_sends(j):
        jo, size, start_row, run = parts_of(j)
        out = []
        for step in range(1, nt):
            peer = (me_t + step) % nt
            out.append(remote(r1w1.at[0, peer, :, pl.ds(jo, size)], r3w1.at[me_t, :, pl.ds(jo, size)], send_sem.at[5, j], rs_sem.at[j, 2], tm=peer))
            out.append(remote(r1w2.at[0, pl.ds(pl.multiple_of(jo + run * peer, run), run), :], r3w2.at[me_t, pl.ds(start_row, run), :], send_sem.at[5, j], rs_sem.at[j, 2], tm=peer))
        return out

    def final_sends(j):
        jo, size, start_row, run = parts_of(j)
        out = []
        for step in range(1, nr):
            peer = (me_r + step) % nr
            one = finw1.at[me_r, :, pl.ds(jo, size)]
            two = finw2.at[me_r, pl.ds(start_row, run), :]
            out.append(remote(one, one, send_sem.at[6, j], rs_sem.at[j, 3], rows=peer))
            out.append(remote(two, two, send_sem.at[6, j], rs_sem.at[j, 3], rows=peer))
        return out

    def reduced(j, kind, sem=None):
        jo, size, _, _ = parts_of(j)
        view = s1w1.at[:, :, :, pl.ds(jo, size)]
        if kind == 1:
            view = s1w1.at[:, pl.ds(0, 2), :, pl.ds(jo, size)]
        elif kind == 2:
            view = s1w1.at[pl.ds(0, nt - 1), pl.ds(0, 2), :, pl.ds(jo, size)]
        elif kind == 3:
            view = s1w1.at[pl.ds(0, 3 * nt // 4), pl.ds(0, 2), :, pl.ds(jo, size)]
        arrived(view, rs_sem.at[j, kind] if sem is None else sem)

    def sum_zero(block):
        first = p.blocks[block][0]
        for j in p.members[block]:
            jo, size, _, _ = parts_of(j)
            cols = slice(jo - first, jo - first + size)
            one = acc1[0 : p.d, cols].astype(BF16)
            s1w1[:, :, :, pl.ds(jo, size)] = one.reshape(nt, nr, p.part, size)
            accb[:, pl.ds(jo, size)] = acc1[p.d : p.d + 8, cols]
            two = acc2[:, cols].astype(BF16).T
            for q in range(nr):
                s1w2[q, pl.ds(jo, size), :] = two[:, p.lanes * q : p.lanes * q + p.lanes]
            start(pair_sends(j))

    def sum_one(j):
        jo, size, _, _ = parts_of(j)
        cols = pl.ds(jo, size)
        reduced(j, 0)
        one = s1w1[:, far, :, cols].astype(F32) + r1w1[1, :, :, cols].astype(F32)
        r1w1[1, :, :, cols] = one.astype(BF16)
        two = s1w2[far, cols, :].astype(F32) + r1w2[1, cols, :].astype(F32)
        r1w2[1, cols, :] = two.astype(BF16)
        start(cross_sends(j))

    def sum_two(j):
        jo, size, start_row, run = parts_of(j)
        cols = pl.ds(jo, size)
        reduced(j, 1)
        one = s1w1[:, me_r, :, cols].astype(F32) + r1w1[0, :, :, cols].astype(F32) + r2w1[:, :, cols].astype(F32)
        r1w1[0, :, :, cols] = one.astype(BF16)
        two = s1w2[me_r, cols, :].astype(F32) + r1w2[0, cols, :].astype(F32) + r2w2[cols, :].astype(F32)
        r1w2[0, cols, :] = two.astype(BF16)
        r3w1[me_t, :, cols] = r1w1[0, me_t, :, cols]
        r3w2[me_t, pl.ds(start_row, run), :] = r1w2[0, pl.ds(pl.multiple_of(jo + run * me_t, run), run), :]
        start(holder_sends(j))

    def sum_three(j):
        jo, size, start_row, run = parts_of(j)
        cols = pl.ds(jo, size)
        reduced(j, 2)
        one = r3w1[0, :, cols].astype(F32)
        two = r3w2[0, pl.ds(start_row, run), :].astype(F32)
        for k in range(1, nt):
            one = one + r3w1[k, :, cols].astype(F32)
            two = two + r3w2[k, pl.ds(start_row, run), :].astype(F32)
        finw1[me_r, :, cols] = one
        finw2[me_r, pl.ds(start_row, run), :] = two
        start(final_sends(j))

    def sum_wait(j):
        reduced(j, 3)

    m = p.m
    per = m // TILE

    def rows_add(ref, i, value, first):
        for s in range(per):
            for c in range(p.nc):
                piece = value[TILE * s : TILE * s + TILE, 128 * c : 128 * c + 128]
                place = (i * per + s, c, slice(GAP, GAP + TILE), slice(None))
                ref[place] = piece if first else ref[place] + piece

    bias_two = small_ref[13:14, :]
    last = len(p.blocks) - 1

    def weights_of(j):
        jo, size = p.blocks[j]
        cols = pl.ds(jo, size)
        w1 = w1b[:, :, :, cols].reshape(p.d, size)
        return w1, jnp.concatenate([w2b[q, cols, :] for q in range(nr)], axis=1)

    def back_dot(grad_hidden, w1):
        return lax.dot_general(
            grad_hidden, w1, (((1,), (1,)), ((), ())), preferred_element_type=F32
        )

    def main_block(j, between):
        jo, size = p.blocks[j]
        cols = pl.ds(jo, size)

        @pl.loop(0, t_len // m)
        def _(i):
            for at, task in between:
                pl.when(i == at)(task)
            rows = pl.ds(pl.multiple_of(i * m, m), m)
            w1, w2 = weights_of(j)
            hidden = jnp.dot(nm[rows, :], w1, preferred_element_type=F32) + b1p[0:1, cols]
            grad_act = back_dot(gb[rows, :], w2)
            prob = 0.5 * (1.0 + lax.erf(hidden * RSQRT_HALF))
            bell = jnp.exp(hidden * hidden * np.float32(-0.5)) * RSQRT_2PI
            act = (hidden * prob).astype(BF16)
            grad_hidden = (grad_act * (prob + hidden * bell)).astype(BF16)
            if j == last:
                nm[rows, 0:size] = act
                gb[rows, 0:size] = grad_hidden
            else:
                branch = jnp.dot(act, w2, preferred_element_type=F32)
                br[rows, :] = branch + bias_two if j == 0 else br[rows, :] + branch
                rows_add(gn, i, back_dot(grad_hidden, w1), j == 0)
            one = jnp.dot(nmt[:, rows], grad_hidden, preferred_element_type=F32)
            two = jnp.dot(gbt[:, rows], act, preferred_element_type=F32)
            acc1[:, 0:size] = one + jnp.where(i > 0, acc1[:, 0:size], 0.0)
            acc2[:, 0:size] = two + jnp.where(i > 0, acc2[:, 0:size], 0.0)

    def then(*calls):
        return [(at, functools.partial(task, j)) for at, task, j in calls]

    main_block(0, then((1, gather_one, 3), (1, spread, 5), (1, spread, 6), (2, gather_two, 2), (2, gather_one, 4)))
    sum_zero(0)
    near_wait(2)
    main_block(
        1,
        then((1, sum_one, 0), (1, sum_one, 1), (1, gather_two, 3), (1, gather_one, 5), (2, gather_two, 4), (2, gather_one, 6)),
    )
    sum_zero(1)
    near_wait(3)
    near_wait(4)
    main_block(
        2,
        then((1, sum_one, 2), (1, sum_two, 0), (1, sum_two, 1), (1, gather_two, 5), (2, gather_two, 6)),
    )
    sum_zero(2)
    sum_two(2)
    sum_three(0)
    sum_three(1)
    near_wait(5)
    near_wait(6)
    main_block(3, then((1, sum_one, 3), (1, sum_one, 4)))
    sum_zero(3)
    sum_two(3)
    sum_three(2)

    unit_rows = 2 * TILE

    def backward_dots(u):
        size = p.blocks[last][1]
        rows = pl.ds(pl.multiple_of(u * unit_rows, unit_rows), unit_rows)
        w1, w2 = weights_of(last)
        branch = jnp.dot(nm[rows, 0:size], w2, preferred_element_type=F32)
        br[rows, :] += branch
        back = back_dot(gb[rows, 0:size], w1)
        for s in range(2):
            for c in range(p.nc):
                piece = back[TILE * s : TILE * s + TILE, 128 * c : 128 * c + 128]
                gn[2 * u + s, c, GAP : GAP + TILE, :] += piece

    def backward_tile(b):
        row = pl.multiple_of(b * TILE, TILE)
        step = 32
        for q in range(TILE // step):
            rows = pl.ds(row + q * step, step)
            place = slice(GAP + q * step, GAP + q * step + step)
            accs[11] += fold(ct[rows, :].astype(F32) * br[rows, :])
            grad = jnp.concatenate([gn[b, c, place, :] for c in range(p.nc)], axis=1)
            unit = xhat[rows, :].astype(F32)
            both_of = grad * unit
            accs[8] += fold(both_of)
            accs[9] += fold(grad)
            u = grad * gain
            mean_u = jnp.sum(u, axis=1, keepdims=True) * (1.0 / p.d)
            mean_x = jnp.sum(both_of * gain, axis=1, keepdims=True) * (1.0 / p.d)
            inverse = rstd[rows, :]
            inverse = jnp.concatenate([inverse] * p.nc, axis=1)
            rounded = ((u - mean_u - unit * mean_x) * inverse).astype(BF16)
            low = rounded.astype(F32)
            accs[7] += fold(low)
            for c in range(p.nc):
                gn[b, c, place, :] = low[:, 128 * c : 128 * c + 128]
        for c in range(p.nc):
            cols = slice(128 * c, 128 * c + 128)
            low = gn[b, c, GAP : GAP + TILE, :]
            for k in range(TAPS):
                first = GAP - 3 + k
                accs[k, :, cols] += fold(low * xf[b, c, first : first + TILE, :])

    def edge_sends():
        after, before = (me_t + 1) % nt, (me_t + nt - 1) % nt
        return [
            remote(gn.at[nb - 1, :, pl.ds(TILE, GAP), :], hprev, send_sem.at[7, 2], halo_sem.at[2], tm=after),
            remote(gn.at[0, :, pl.ds(GAP, GAP), :], hnext, send_sem.at[7, 3], halo_sem.at[3], tm=before),
        ]

    backward_dots(0)
    units = nb // 2

    @pl.loop(0, units - 1)
    def _(u):
        for at, task in then(
            (1, sum_one, 5), (1, sum_one, 6), (2, sum_two, 4), (6, sum_two, 5), (6, sum_three, 3), (8, sum_three, 4), (9, sum_two, 6)
        ):
            pl.when(u == at)(task)
        backward_dots(u + 1)
        backward_tile(2 * u)
        backward_tile(2 * u + 1)

    @pl.loop(nb - 2, nb)
    def _(b):
        backward_tile(b)

    start(edge_sends())

    hidden_tiles = lane_permuted(lambda i: accb[:, 128 * i : 128 * i + 128], p.regrouped, p.ff // 128)
    for c in range(p.nc):
        cols = slice(128 * c, 128 * c + 128)
        line = []
        for k in range(10):
            line.append(jnp.sum(accs[k, :, cols], axis=0, keepdims=True))
        for i in range(3):
            line.append(jnp.sum(hidden_tiles[i * p.nc + c], axis=0, keepdims=True))
        for k in (10, 11):
            line.append(jnp.sum(accs[k, :, cols], axis=0, keepdims=True))
        line.append(jnp.zeros((1, 128), F32))
        sma[c] = jnp.concatenate(line, axis=0)

    def small_one_sends():
        out = []
        for step in range(1, nr):
            peer = (me_r + step) % nr
            out.append(remote(sma.at[peer], smr.at[me_r], send_sem.at[7, 4], sm_sem.at[0], rows=peer))
        return out

    def small_two_sends():
        out = []
        for step in range(1, nt):
            peer = (me_t + step) % nt
            out.append(remote(smq.at[nt], smq.at[me_t], send_sem.at[8, 0], sm_sem.at[1], tm=peer))
        return out

    def small_three_sends():
        out = []
        for step in range(1, nr):
            peer = (me_r + step) % nr
            out.append(remote(smf.at[me_r], smf.at[me_r], send_sem.at[8, 1], sm_sem.at[2], rows=peer))
        return out

    smr[me_r] = sma[me_r]
    start(small_one_sends())

    def small_two():
        arrived(smr.at[pl.ds(0, nr - 1)], sm_sem.at[0])
        total = smr[0]
        for k in range(1, nr):
            total = total + smr[k]
        smq[nt] = total
        smq[me_t] = total
        start(small_two_sends())

    def small_three():
        arrived(smq.at[pl.ds(0, nt - 1)], sm_sem.at[1])
        total = smq[0]
        for k in range(1, nt):
            total = total + smq[k]
        smf[me_r] = total
        start(small_three_sends())

    def exchange_edges(b):
        same = flags[pl.ds(b, 1), :] < 0.5
        for c in range(p.nc):
            gn[b, c, 0:GAP, :] = jnp.where(same, gn[b - 1, c, TILE : TILE + GAP, :], 0.0)
            gn[b - 1, c, GAP + TILE :, :] = jnp.where(same, gn[b, c, GAP : GAP + GAP, :], 0.0)

    def last_tile(b):
        row = pl.multiple_of(b * TILE, TILE)
        rows = pl.ds(row, TILE)
        for c in range(p.nc):
            cols = slice(128 * c, 128 * c + 128)
            source = frx[pl.ds(row + HALO, TILE), cols].astype(F32)
            nm[rows, cols] = (source + scale[:, cols] * br[rows, cols]).astype(BF16)
            total = ct[rows, cols].astype(F32)
            for k in range(TAPS):
                first = GAP + 3 - k
                total = total + small_ref[k : k + 1, cols] * gn[b, c, first : first + TILE, :]
            gb[rows, cols] = total.astype(BF16)

    exchange_edges(1)

    def last_tiles(low, high):
        @pl.loop(low, high)
        def _(b):
            exchange_edges(b + 1)
            last_tile(b)

    cut = [1, 1 + (nb - 2) // 2, 1 + (nb - 2) * 3 // 4, nb - 1]
    last_tiles(cut[0], cut[1])
    small_two()
    sum_three(5)
    last_tiles(cut[1], cut[2])
    sum_three(6)
    last_tiles(cut[2], cut[3])
    arrived(hprev, halo_sem.at[2])
    arrived(hnext, halo_sem.at[3])
    for c in range(p.nc):
        gn[0, c, 0:GAP, :] = jnp.where(flags[0:1, :] < 0.5, hprev[c], 0.0)
        gn[nb - 1, c, GAP + TILE :, :] = jnp.where(flags[nb : nb + 1, :] < 0.5, hnext[c], 0.0)

    @pl.loop(0, 2)
    def _(i):
        last_tile(i * (nb - 1))

    small_three()

    for j in range(len(p.chunks)):
        sum_wait(j)
        spread_wait(j, send_sem.at[0, j])
        far_wait(j, send_sem.at[1, j])
        near_wait(j, send_sem.at[2, j])
        for kind in range(4):
            reduced(j, kind, send_sem.at[3 + kind, j])
    for copy in halo_sends() + edge_sends():
        copy.wait_send()
    arrived(smf.at[pl.ds(0, nr - 1)], sm_sem.at[2])
    for c in range(p.nc):
        small_out[:, 128 * c : 128 * c + 128] = smf[c]

    for copy in small_one_sends() + small_two_sends() + small_three_sends():
        copy.wait_send()
    for load in rest:
        load.wait()


def finish_kernel(
    plan,
    nm, gb, grad1, grad2, grad_small, state1, state2,
    small_master, small_first, small_second, small_average,
    output, ingrad, *rest,
):
    p = plan
    outs1, outs2, outs_small = rest[0:5], rest[5:10], rest[10:15]
    new1, low1, new2, low2, new_small, low_small, sem = rest[15:]
    copies = [
        pltpu.make_async_copy(nm, output.at[0], sem.at[0]),
        pltpu.make_async_copy(gb, ingrad.at[0], sem.at[1]),
    ]
    for copy in copies:
        copy.start()

    def first_grad(q):
        tiles = lane_permuted(
            lambda i: grad1[q, :, 128 * i : 128 * i + 128], p.regrouped, p.ff // 128
        )
        return jnp.concatenate(tiles, axis=1)

    def second_grad(q):
        rows = slice(q * p.part, q * p.part + p.part)
        return jnp.concatenate([grad2[k, rows, :] for k in range(p.nr)], axis=1)

    count = 2
    got = adamw_step(
        small_master[...], small_first[...], small_second[...], small_average[...], grad_small[0:15], rate_small
    )
    for k in range(5):
        source = low_small if k == 4 else new_small.at[k]
        source[...] = got[k]
        copy = pltpu.make_async_copy(source, outs_small[k], sem.at[count])
        copy.start()
        copies.append(copy)
        count += 1
    for grad, state, new, low, outs, rate in (
        (first_grad, state1, new1, low1, outs1, rate_first),
        (second_grad, state2, new2, low2, outs2, rate_second),
    ):
        for q in range(low.shape[0] // p.part):
            rows = slice(q * p.part, q * p.part + p.part)
            got = adamw_step(
                state[0, rows], state[1, rows], state[2, rows], state[3, rows], grad(q), rate
            )
            for k in range(4):
                new[k, rows] = got[k]
            low[rows] = got[4]
        for k in range(5):
            source = low if k == 4 else new.at[k]
            copy = pltpu.make_async_copy(source, outs[k], sem.at[count])
            copy.start()
            copies.append(copy)
            count += 1
    for copy in copies:
        copy.wait()


def finish(plan, kept, smalls):
    vmem = pl.BlockSpec(memory_space=pltpu.VMEM)
    anyplace = pl.BlockSpec(memory_space=pl.ANY)
    kept = [pltpu.with_memory_space_constraint(value, pltpu.VMEM) for value in kept]
    shape1, shape2 = (plan.rows1, plan.ff), (plan.share, plan.d)
    whole = jax.ShapeDtypeStruct((1, plan.t, plan.d), BF16)

    def five(shape):
        return [jax.ShapeDtypeStruct(shape, F32)] * 4 + [jax.ShapeDtypeStruct(shape, BF16)]

    v = pltpu.VMEM
    return pl.pallas_call(
        functools.partial(finish_kernel, plan),
        out_shape=(whole, whole, *five(shape1), *five(shape2), *five(smalls[0].shape)),
        in_specs=[vmem] * 11,
        out_specs=(anyplace,) * 17,
        scratch_shapes=[
            v((4, *shape1), F32),
            v(shape1, BF16),
            v((4, *shape2), F32),
            v(shape2, BF16),
            v((4, *smalls[0].shape), F32),
            v(smalls[0].shape, BF16),
            pltpu.SemaphoreType.DMA((17,)),
        ],
        compiler_params=pltpu.CompilerParams(vmem_limit_bytes=8_000_000),
    )(*kept, *smalls)


def call(plan, frames, cotangent, lengths, one, two, small_master):
    p = plan
    t, d, ff, nt, nr, nb, nc = p.t, p.d, p.ff, p.nt, p.nr, p.nb, p.nc
    vmem = pl.BlockSpec(memory_space=pltpu.VMEM)
    anyplace = pl.BlockSpec(memory_space=pl.ANY)
    n_lens = -(-lengths.shape[1] // 128) * 128
    v = pltpu.VMEM
    scratch = [
        v((t + 2 * HALO, d), BF16),
        v((t, d), BF16),
        v((d + 16, t), BF16),
        v((d, t), BF16),
        v((t, d), F32),
        v((nb, nc, TILE + 2 * GAP, 128), F32),
        v((nb, nc, TILE + 2 * GAP, 128), F32),
        v((t, d), BF16),
        v((t, 128), F32),
        v((nt, nr, p.part, ff), BF16),
        v((nr, ff, p.lanes), BF16),
        v((d + 16, p.widest), F32),
        v((d, p.widest), F32),
        v(lengths.shape, jnp.int32),
        v(small_master.shape, F32),
        v((8, n_lens), F32),
        v((-(-(nb + 1) // 8) * 8, 128), F32),
        v((8, ff), F32),
        v((12, 8, d), F32),
        v((8, ff), F32),
        v((TILE, d), F32),
        v((nt, nr, p.part, ff), BF16),
        v((nr, ff, p.lanes), BF16),
        v((2, nt, p.part, ff), BF16),
        v((2, ff, p.lanes), BF16),
        v((nt, p.part, ff), BF16),
        v((ff, p.lanes), BF16),
        v((nt, p.part, ff), BF16),
        v((nt, p.share, p.lanes), BF16),
        v((nr, 16, p.lanes), F32),
        v((nr, 16, p.lanes), F32),
        v((nt + 1, 16, p.lanes), F32),
        v((nr, 16, p.lanes), F32),
        v((nc, GAP, 128), F32),
        v((nc, GAP, 128), F32),
        pltpu.SemaphoreType.DMA((7,)),
        pltpu.SemaphoreType.DMA((9, len(p.chunks))),
        pltpu.SemaphoreType.DMA((4,)),
        pltpu.SemaphoreType.DMA((len(p.chunks), 3)),
        pltpu.SemaphoreType.DMA((len(p.chunks), 4)),
        pltpu.SemaphoreType.DMA((3,)),
    ]
    return pl.pallas_call(
        functools.partial(kernel, plan),
        out_shape=(
            v((t, d), BF16),
            v((t, d), BF16),
            v((nr, p.part, ff), F32),
            v((nr, p.share, p.lanes), F32),
            v((16, d), F32),
            v((4, p.rows1, ff), F32),
            v((4, p.share, d), F32),
        ),
        in_specs=[anyplace] * 12,
        out_specs=(vmem,) * 7,
        scratch_shapes=scratch,
        compiler_params=pltpu.CompilerParams(
            collective_id=0, has_side_effects=True, vmem_limit_bytes=56_500_000
        ),
    )(frames, cotangent, lengths, *one, *two, small_master)


def padded_2(array, sides, width):
    for axis, dim in sides:
        devices, length = (lax.axis_size(axis), array.shape[dim])
        up = [(i, (i + 1) % devices) for i in range(devices - 1)]
        down = [(j, i) for i, j in up]
        last = lax.slice_in_dim(array, length - width, length, axis=dim)
        leading = lax.slice_in_dim(array, 0, width, axis=dim)
        before = lax.ppermute(last, axis, up)
        after = lax.ppermute(leading, axis, down)
        array = jnp.concatenate([before, array, after], axis=dim)
    return array


def cut_along(array, dim, devices):
    before, after = (array.shape[:dim], array.shape[dim + 1 :])
    return jnp.moveaxis(array.reshape(*before, devices, -1, *after), dim, 0)


def sent_and_summed(array, axis, dim):
    devices = lax.axis_size(axis)
    pieces = lax.all_to_all(cut_along(array, dim, devices), axis, 0, 0, tiled=True)
    return jnp.sum(pieces.astype(jnp.float32), axis=0)


def edge_masks(lengths_row, first_frame, frame_count):
    ends_at = jnp.cumsum(lengths_row, dtype=jnp.int32)
    places = first_frame + jnp.arange(frame_count, dtype=jnp.int32)
    passed = ends_at[None, :] <= places[:, None]
    lower = jnp.max(jnp.where(passed, ends_at[None, :], 0), axis=1)
    upper = jnp.min(jnp.where(passed, ends_at[-1], ends_at[None, :]), axis=1)
    mask_rows = []
    for tap_index in range(7):
        spot_now = places + (tap_index - 3)
        mask_rows.append(((spot_now >= lower) & (spot_now < upper)).astype(jnp.float32))
    return jnp.stack(mask_rows)


def depthwise(padded, tap_rows, masks, frame_count):
    summed = jnp.zeros((frame_count, padded.shape[1]), jnp.float32)
    for tap_index in range(7):
        window = padded[tap_index : tap_index + frame_count].astype(jnp.float32)
        summed = summed + tap_rows[tap_index][None, :] * window * masks[tap_index][:, None]
    return summed


def layer_norm(conv_out, norm_gain, norm_bias):
    centred = conv_out - jnp.mean(conv_out, axis=-1, keepdims=True)
    spread = jnp.mean(centred * centred, axis=-1, keepdims=True)
    return centred * lax.rsqrt(spread + norm_eps) * norm_gain[None, :] + norm_bias[None, :]


def exact_gelu(values):
    return jax.nn.gelu(values, approximate=False)


def frame_product(left_side, right_side):
    return lax.dot_general(
        left_side, right_side, (((0,), (0,)), ((), ())), preferred_element_type=jnp.float32
    )


def plain_body(
    frames,
    cotangent,
    lengths,
    w1_master,
    w1_first,
    w1_second,
    w1_average,
    w2_master,
    w2_first,
    w2_second,
    w2_average,
    small_master,
    small_first,
    small_second,
    small_average,
):
    frame_count = frames.shape[1]
    width = frames.shape[2]
    w1_low, w2_low = (
        lax.all_gather(w1_master.astype(jnp.bfloat16), "tm", axis=0, tiled=True),
        lax.all_gather(w2_master.astype(jnp.bfloat16), "tm", axis=0, tiled=True),
    )
    inputs = frames[0]
    upstream = cotangent[0].astype(jnp.float32)
    masks = edge_masks(lengths[0], lax.axis_index("tm") * frame_count, frame_count)
    tap_rows = small_master[0:7]
    layer_scale = small_master[14]
    padded = padded_2(inputs, (("tm", 0),), 3)
    conv_out = depthwise(padded, tap_rows, masks, frame_count) + small_master[7][None, :]
    normed, norm_back = jax.vjp(layer_norm, conv_out, small_master[8], small_master[9])
    normed_low = normed.astype(jnp.bfloat16)
    hidden = (
        jnp.dot(normed_low, w1_low, preferred_element_type=jnp.float32)
        + small_master[10:13].reshape(-1)[None, :]
    )
    activated, gelu_back = jax.vjp(exact_gelu, hidden)
    act_low = activated.astype(jnp.bfloat16)
    branch = (
        jnp.dot(act_low, w2_low, preferred_element_type=jnp.float32) + small_master[13][None, :]
    )
    output = (inputs.astype(jnp.float32) + layer_scale[None, :] * branch).astype(jnp.bfloat16)
    grad_scale = jnp.sum(upstream * branch, axis=0)
    grad_branch = (layer_scale[None, :] * upstream).astype(jnp.bfloat16)
    grad_act = lax.dot_general(
        grad_branch, w2_low, (((1,), (1,)), ((), ())), preferred_element_type=jnp.float32
    )
    grad_hidden = gelu_back(grad_act)[0].astype(jnp.bfloat16)
    grad_normed = lax.dot_general(
        grad_hidden, w1_low, (((1,), (1,)), ((), ())), preferred_element_type=jnp.float32
    )
    grad_conv, grad_gain, grad_shift = norm_back(grad_normed)
    grad_low = grad_conv.astype(jnp.bfloat16)
    grad_pad = padded_2(grad_low, (("tm", 0),), 3)
    input_grad = (upstream + depthwise(grad_pad, tap_rows[::-1], masks, frame_count)).astype(
        jnp.bfloat16
    )
    grad_float = grad_low.astype(jnp.float32)
    grad_taps = jnp.stack(
        [
            jnp.sum(
                grad_float
                * padded[tap_index : tap_index + frame_count].astype(jnp.float32)
                * masks[tap_index][:, None],
                axis=0,
            )
            for tap_index in range(7)
        ]
    )
    middle_rows = jnp.stack([jnp.sum(grad_float, axis=0), grad_gain, grad_shift])
    bias_rows = jnp.sum(grad_hidden.astype(jnp.float32), axis=0).reshape(3, width)
    last_rows = jnp.stack([jnp.sum(grad_branch.astype(jnp.float32), axis=0), grad_scale])
    small_grad = jnp.concatenate([grad_taps, middle_rows, bias_rows, last_rows], axis=0)
    full_one = frame_product(normed_low, grad_hidden)
    full_two = frame_product(act_low, grad_branch)
    share_one, share_two = (
        sent_and_summed(full_one.astype(jnp.bfloat16), "tm", 0),
        sent_and_summed(full_two.astype(jnp.bfloat16), "tm", 0),
    )
    grad_one, grad_two = (
        lax.psum(share_one.astype(jnp.bfloat16), "rows").astype(jnp.float32),
        lax.psum(share_two.astype(jnp.bfloat16), "rows").astype(jnp.float32),
    )
    small_total = lax.psum(small_grad, ("tm", "rows"))
    one_out = adamw_step(w1_master, w1_first, w1_second, w1_average, grad_one, rate_first)
    two_out = adamw_step(w2_master, w2_first, w2_second, w2_average, grad_two, rate_second)
    small_out = adamw_step(
        small_master, small_first, small_second, small_average, small_total, rate_small
    )
    return (
        output[None],
        input_grad[None],
        one_out[0],
        one_out[1],
        one_out[2],
        one_out[3],
        one_out[4],
        two_out[0],
        two_out[1],
        two_out[2],
        two_out[3],
        two_out[4],
        small_out[0],
        small_out[1],
        small_out[2],
        small_out[3],
        small_out[4],
    )


def body(
    frames,
    cotangent,
    lengths,
    w1_master,
    w1_first,
    w1_second,
    w1_average,
    w2_master,
    w2_first,
    w2_second,
    w2_average,
    small_master,
    small_first,
    small_second,
    small_average,
):
    nt, nr = lax.axis_size("tm"), lax.axis_size("rows")
    plan = Plan(nt, nr, frames.shape[1], frames.shape[2], w1_master.shape[1])
    kept = call(
        plan,
        frames,
        cotangent,
        lengths,
        (w1_master, w1_first, w1_second, w1_average),
        (w2_master, w2_first, w2_second, w2_average),
        small_master,
    )
    return finish(plan, kept, (small_master, small_first, small_second, small_average))


def solution(mesh):
    in_specs = (
        P("rows", "tm", None),
        P("rows", "tm", None),
        P("rows", None),
        P("tm", None),
        P("tm", None),
        P("tm", None),
        P("tm", None),
        P("tm", None),
        P("tm", None),
        P("tm", None),
        P("tm", None),
        P(),
        P(),
        P(),
        P(),
    )
    out_specs = (
        P("rows", "tm", None),
        P("rows", "tm", None),
        P("tm", None),
        P("tm", None),
        P("tm", None),
        P("tm", None),
        P("tm", None),
        P("tm", None),
        P("tm", None),
        P("tm", None),
        P("tm", None),
        P("tm", None),
        P(),
        P(),
        P(),
        P(),
        P(),
    )
    fits = mesh.shape["tm"] == 8 and mesh.shape["rows"] == 4
    return jax.shard_map(body if fits else plain_body, mesh=mesh, in_specs=in_specs, out_specs=out_specs, check_vma=False)
```

```python
import functools

import jax
import jax.numpy as jnp
import numpy as np
from jax import lax
from jax.experimental import pallas as pl
from jax.experimental.pallas import tpu as pltpu
from jax.sharding import PartitionSpec as P

ADAM_STEP = 3
norm_eps = 1e-06
adam_eps = 1e-08
weight_decay = 0.01
beta_first = 0.5
beta_second = 0.5
average_keep = 0.75
rate_first = 0.08
rate_second = 0.05
rate_small = 0.4

TAPS = 7
TILE = 128
GAP = 8
GRAIN = 16
HALO = 16
F32 = jnp.float32
BF16 = jnp.bfloat16
MESH = pl.DeviceIdType.MESH
RSQRT_HALF = np.float32(0.7071067811865476)
RSQRT_2PI = np.float32(0.3989422804014327)


def adamw_step(master, first_old, second_old, average_old, gradient, rate):
    first_new = beta_first * first_old + (1.0 - beta_first) * gradient
    second_new = beta_second * second_old + (1.0 - beta_second) * gradient * gradient
    first_hat = first_new / (1.0 - beta_first**ADAM_STEP)
    second_hat = second_new / (1.0 - beta_second**ADAM_STEP)
    master_new = master - rate * (
        first_hat / (jnp.sqrt(second_hat) + adam_eps) + weight_decay * master
    )
    average_new = average_keep * average_old + (1.0 - average_keep) * master_new
    return (master_new, first_new, second_new, average_new, master_new.astype(BF16))


class Plan:
    def __init__(self, nt, nr, frame_count, width, hidden):
        self.nt, self.nr, self.t, self.d, self.ff = nt, nr, frame_count, width, hidden
        self.share = hidden // nt
        self.rows1 = width // nt
        self.part = self.rows1 // nr
        self.lanes = width // nr
        self.nb = frame_count // TILE
        self.nc = width // 128
        self.chunks = []
        offset = begin = 0
        for run in (16, 16, 32, 32, 32, 32, 32):
            self.chunks.append((offset, run * nt, run, begin))
            offset += run * nt
            begin += run
        self.members = [(0, 1), (2,), (3, 4), (5, 6)]
        self.blocks = [
            (self.chunks[own[0]][0], sum(self.chunks[j][1] for j in own)) for own in self.members
        ]
        self.widest = max(size for _, size in self.blocks)
        self.m = 1024
        self.natural = []
        for _, _, run, begin in self.chunks:
            for k in range(nt):
                for o in range(0, run, GRAIN):
                    self.natural.append((self.share * k + begin + o) // GRAIN)
        self.regrouped = [self.natural.index(g) for g in range(hidden // GRAIN)]


def lane_permuted(tile_of, source, count):
    per = 128 // GRAIN
    out = []
    for tile in range(count):
        value, before = None, None
        for q in range(per):
            run = source[tile * per + q]
            now = (run // per, (q - run % per) % per)
            if now == before:
                continue
            before = now
            piece = tile_of(now[0])
            if now[1]:
                piece = pltpu.roll(piece, now[1] * GRAIN, 1)
            if value is None:
                value = piece
            else:
                lane = lax.broadcasted_iota(jnp.int32, piece.shape, 1)
                value = jnp.where(lane >= q * GRAIN, piece, value)
        out.append(value)
    return out


def fold(value):
    rows = value.shape[0]
    total = value[0:8]
    for g in range(1, rows // 8):
        total = total + value[8 * g : 8 * g + 8]
    return total


def kernel(
    plan,
    frames_hbm,
    cot_hbm,
    lengths_hbm,
    w1_hbm,
    w1_first_hbm,
    w1_second_hbm,
    w1_average_hbm,
    w2_hbm,
    w2_first_hbm,
    w2_second_hbm,
    w2_average_hbm,
    small_hbm,
    nm,
    gb,
    finw1,
    finw2,
    small_out,
    state1,
    state2,
    frx,
    ct,
    nmt,
    gbt,
    br,
    gn,
    xf,
    xhat,
    rstd,
    w1b,
    w2b,
    acc1,
    acc2,
    lengths_ref,
    small_ref,
    lens,
    flags,
    b1p,
    accs,
    accb,
    tmp,
    s1w1,
    s1w2,
    r1w1,
    r1w2,
    r2w1,
    r2w2,
    r3w1,
    r3w2,
    sma,
    smr,
    smq,
    smf,
    hprev,
    hnext,
    in_sem,
    send_sem,
    halo_sem,
    ag_sem,
    rs_sem,
    sm_sem,
):
    p = plan
    nt, nr, t_len = p.nt, p.nr, p.t
    me_t = lax.axis_index("tm")
    me_r = lax.axis_index("rows")
    near = me_r + 1 - 2 * (me_r % 2)
    far = (me_r + 2) % nr
    both = near + 2 - 4 * (near // 2)

    upper = me_t // (nt // 2)

    def peer_of(step):
        return (me_t + step * upper + (nt - step) * (1 - upper)) % nt

    def remote(src, dst, send, recv, tm=None, rows=None):
        device = {"tm": me_t if tm is None else tm, "rows": me_r if rows is None else rows}
        return pltpu.make_async_remote_copy(
            src_ref=src, dst_ref=dst, send_sem=send, recv_sem=recv,
            device_id=device, device_id_type=MESH,
        )

    def arrived(view, sem):
        pltpu.make_async_copy(view, view, sem).wait()

    loads = [
        pltpu.make_async_copy(w1_hbm, state1.at[0], in_sem.at[0]),
        pltpu.make_async_copy(w2_hbm, state2.at[0], in_sem.at[1]),
        pltpu.make_async_copy(frames_hbm.at[0], frx.at[pl.ds(HALO, t_len)], in_sem.at[2]),
        pltpu.make_async_copy(cot_hbm.at[0], ct, in_sem.at[3]),
        pltpu.make_async_copy(lengths_hbm, lengths_ref, in_sem.at[5]),
        pltpu.make_async_copy(small_hbm, small_ref, in_sem.at[6]),
    ]
    for k in (0, 1, 5, 4, 2, 3):
        loads[k].start()

    barrier = pltpu.get_barrier_semaphore()
    for step in range(1, nt):
        pl.semaphore_signal(
            barrier, inc=1, device_id={"tm": (me_t + step) % nt, "rows": me_r}, device_id_type=MESH
        )
    for step in range(1, nr):
        pl.semaphore_signal(
            barrier, inc=1, device_id={"tm": me_t, "rows": (me_r + step) % nr}, device_id_type=MESH
        )

    loads[4].wait()
    loads[5].wait()
    lens[...] = jnp.zeros_like(lens)
    n_len = lengths_ref.shape[1]
    lens[0:1, 0:n_len] = lengths_ref[...].astype(F32)
    ends = lens[...]
    lane = lax.broadcasted_iota(jnp.int32, ends.shape, 1)
    shift = 1
    while shift < lens.shape[1]:
        ends = ends + jnp.where(lane >= shift, pltpu.roll(ends, shift, 1), 0.0)
        shift *= 2
    n_flag = flags.shape[0]
    spot = me_t * t_len + TILE * lax.broadcasted_iota(jnp.int32, (n_flag, lens.shape[1]), 0)
    hit = (ends[0:1, :] == spot.astype(F32)) | (spot == 0)
    edge = jnp.max(jnp.where(hit, 1.0, 0.0), axis=1, keepdims=True)
    flags[...] = jnp.broadcast_to(edge, flags.shape)
    accs[...] = jnp.zeros_like(accs)
    ones_row = lax.broadcasted_iota(jnp.int32, (16, t_len), 0) == 0
    nmt[p.d :, :] = jnp.where(ones_row, 1.0, 0.0).astype(BF16)
    bias_tiles = lane_permuted(
        lambda i: jnp.broadcast_to(small_ref[10 + i // p.nc : 11 + i // p.nc, 128 * (i % p.nc) : 128 * (i % p.nc) + 128], (8, 128)),
        p.natural,
        p.ff // 128,
    )
    for i, tile in enumerate(bias_tiles):
        b1p[:, 128 * i : 128 * i + 128] = tile

    loads[0].wait()
    loads[1].wait()
    own_rows = pl.ds(pl.multiple_of(me_r * p.part, p.part), p.part)
    own_lanes = pl.ds(pl.multiple_of(me_r * p.lanes, p.lanes), p.lanes)
    own1 = lane_permuted(lambda i: state1[0, own_rows, 128 * i : 128 * i + 128], p.natural, p.ff // 128)
    for i, tile in enumerate(own1):
        w1b[me_t, me_r, :, 128 * i : 128 * i + 128] = tile.astype(BF16)
    for jo, _, run, begin in p.chunks:
        w2b[me_r, pl.ds(pl.multiple_of(jo + run * me_t, run), run), :] = state2[0, begin : begin + run, own_lanes].astype(BF16)

    pl.semaphore_wait(barrier, nt + nr - 2)

    def halo_sends():
        after, before = (me_t + 1) % nt, (me_t + nt - 1) % nt
        return [
            remote(frames_hbm.at[0, pl.ds(t_len - HALO, HALO)], frx.at[pl.ds(0, HALO)], send_sem.at[7, 0], halo_sem.at[0], tm=after),
            remote(frames_hbm.at[0, pl.ds(0, HALO)], frx.at[pl.ds(HALO + t_len, HALO)], send_sem.at[7, 1], halo_sem.at[1], tm=before),
        ]

    def w1_part(j, q):
        jo, size = p.chunks[j][:2]
        return w1b.at[:, q, :, pl.ds(jo, size)]

    def w2_part(j, q):
        jo, size = p.chunks[j][:2]
        return w2b.at[q, pl.ds(jo, size), :]

    def spread_sends(j):
        jo, size, run, _ = p.chunks[j]
        out = []
        for step in range(1, nt):
            peer = peer_of(step)
            one = w1b.at[me_t, me_r, :, pl.ds(jo, size)]
            two = w2b.at[me_r, pl.ds(pl.multiple_of(jo + run * me_t, run), run), :]
            out.append(remote(one, one, send_sem.at[0, j], ag_sem.at[j, 0], tm=peer))
            out.append(remote(two, two, send_sem.at[0, j], ag_sem.at[j, 0], tm=peer))
        return out

    def spread_wait(j, sem=None):
        jo, size = p.chunks[j][:2]
        arrived(w1b.at[pl.ds(0, nt - 1), pl.ds(0, 2), :, pl.ds(jo, size)], ag_sem.at[j, 0] if sem is None else sem)

    def far_sends(j):
        return [
            remote(w1_part(j, me_r), w1_part(j, me_r), send_sem.at[1, j], ag_sem.at[j, 1], rows=far),
            remote(w2_part(j, me_r), w2_part(j, me_r), send_sem.at[1, j], ag_sem.at[j, 1], rows=far),
        ]

    def far_wait(j, sem=None):
        jo, size = p.chunks[j][:2]
        arrived(w1b.at[:, pl.ds(0, 2), :, pl.ds(jo, size)], ag_sem.at[j, 1] if sem is None else sem)

    def near_sends(j, q):
        return [
            remote(w1_part(j, q), w1_part(j, q), send_sem.at[2, j], ag_sem.at[j, 2], rows=near),
            remote(w2_part(j, q), w2_part(j, q), send_sem.at[2, j], ag_sem.at[j, 2], rows=near),
        ]

    def near_wait(j, sem=None):
        jo, size = p.chunks[j][:2]
        arrived(w1b.at[:, :, :, pl.ds(jo, size)], ag_sem.at[j, 2] if sem is None else sem)

    def start(copies):
        for copy in copies:
            copy.start()

    def gather_one(j):
        spread_wait(j)
        start(far_sends(j))
        start(near_sends(j, me_r))

    def gather_two(j):
        far_wait(j)
        start(near_sends(j, far))

    def spread(j):
        start(spread_sends(j))

    spread(0)
    spread(1)
    start(halo_sends())

    rest = [
        pltpu.make_async_copy(source, target, in_sem.at[4])
        for source, target in (
            (w1_first_hbm, state1.at[1]),
            (w1_second_hbm, state1.at[2]),
            (w1_average_hbm, state1.at[3]),
            (w2_first_hbm, state2.at[1]),
            (w2_second_hbm, state2.at[2]),
            (w2_average_hbm, state2.at[3]),
        )
    ]
    for load in rest:
        load.start()
    loads[2].wait()
    loads[3].wait()

    gain = small_ref[8:9, :]
    shift_row = small_ref[9:10, :]
    scale = small_ref[14:15, :]

    first_row = jnp.where(lax.broadcasted_iota(jnp.int32, (8, TILE), 0) == 0, 1.0, 0.0).astype(BF16)

    def turn_tile(b):
        row = pl.multiple_of(b * TILE, TILE)
        nmt[0 : p.d, pl.ds(row, TILE)] = nm[pl.ds(row, TILE), :].T
        gbt[:, pl.ds(row, TILE)] = gb[pl.ds(row, TILE), :].T

    def forward_tile(b, turned=None):
        if turned is not None:
            turn_tile(turned)
        row = pl.multiple_of(b * TILE, TILE)
        starts_here = flags[pl.ds(b, 1), :]
        ends_here = flags[pl.ds(b + 1, 1), :]
        lead = frx[pl.ds(row, HALO), :].astype(F32)
        trail = frx[pl.ds(row + HALO + TILE, HALO), :].astype(F32)
        for c in range(p.nc):
            cols = slice(128 * c, 128 * c + 128)
            xf[b, c, GAP : GAP + TILE, :] = frx[pl.ds(row + HALO, TILE), cols].astype(F32)
            xf[b, c, 0:GAP, :] = jnp.where(starts_here > 0.5, 0.0, lead[HALO - GAP :, cols])
            xf[b, c, GAP + TILE :, :] = jnp.where(ends_here > 0.5, 0.0, trail[0:GAP, cols])
        for c in range(p.nc):
            cols = slice(128 * c, 128 * c + 128)
            total = jnp.broadcast_to(small_ref[7:8, cols], (TILE, 128))
            for k in range(TAPS):
                first = GAP - 3 + k
                total = total + small_ref[k : k + 1, cols] * xf[b, c, first : first + TILE, :]
            tmp[:, cols] = total
        step = 32
        for q in range(TILE // step):
            rows = pl.ds(row + q * step, step)
            value = tmp[q * step : q * step + step, :]
            centred = value - jnp.sum(value, axis=1, keepdims=True) * (1.0 / p.d)
            spread = jnp.sum(centred * centred, axis=1, keepdims=True) * (1.0 / p.d)
            inverse = lax.rsqrt(spread + norm_eps)
            unit = centred * inverse
            rstd[rows, :] = jnp.broadcast_to(inverse, (step, 128))
            xhat[rows, :] = unit.astype(BF16)
            nm[rows, :] = (unit * gain + shift_row).astype(BF16)
            low = (scale * ct[rows, :].astype(F32)).astype(BF16)
            gb[rows, :] = low
        accs[10] += jnp.dot(first_row, gb[pl.ds(row, TILE), :], preferred_element_type=F32)

    def forward_tiles(low, high):
        @pl.loop(low, high)
        def _(b):
            forward_tile(b, b - 1)

    nb = p.nb
    forward_tile(1)
    forward_tiles(2, nb // 4 - 1)
    spread(2)
    forward_tiles(nb // 4 - 1, nb * 3 // 8)
    gather_one(0)
    spread(3)
    spread(4)
    forward_tiles(nb * 3 // 8, nb // 2)
    gather_one(1)
    forward_tiles(nb // 2, nb * 2 // 3)
    gather_two(0)
    arrived(frx.at[pl.ds(HALO + t_len, HALO)], halo_sem.at[1])
    forward_tiles(nb * 2 // 3, nb * 5 // 6)
    gather_two(1)
    forward_tiles(nb * 5 // 6, nb)
    gather_one(2)
    arrived(frx.at[pl.ds(0, HALO)], halo_sem.at[0])
    forward_tile(0, nb - 1)
    turn_tile(0)
    near_wait(0)
    near_wait(1)

    def parts_of(j):
        jo, size, run, begin = p.chunks[j]
        return jo, size, begin, run

    def pair_sends(j):
        jo, size, _, _ = parts_of(j)
        out = []
        for slot, q in ((0, near), (1, both)):
            out.append(remote(s1w1.at[:, q, :, pl.ds(jo, size)], r1w1.at[slot, :, :, pl.ds(jo, size)], send_sem.at[3, j], rs_sem.at[j, 0], rows=near))
            out.append(remote(s1w2.at[q, pl.ds(jo, size), :], r1w2.at[slot, pl.ds(jo, size), :], send_sem.at[3, j], rs_sem.at[j, 0], rows=near))
        return out

    def cross_sends(j):
        jo, size, _, _ = parts_of(j)
        return [
            remote(r1w1.at[1, :, :, pl.ds(jo, size)], r2w1.at[:, :, pl.ds(jo, size)], send_sem.at[4, j], rs_sem.at[j, 1], rows=far),
            remote(r1w2.at[1, pl.ds(jo, size), :], r2w2.at[pl.ds(jo, size), :], send_sem.at[4, j], rs_sem.at[j, 1], rows=far),
        ]

    def holder_sends(j):
        jo, size, start_row, run = parts_of(j)
        out = []
        for step in range(1, nt):
            peer = peer_of(step)
            out.append(remote(r1w1.at[0, peer, :, pl.ds(jo, size)], r3w1.at[me_t, :, pl.ds(jo, size)], send_sem.at[5, j], rs_sem.at[j, 2], tm=peer))
            out.append(remote(r1w2.at[0, pl.ds(pl.multiple_of(jo + run * peer, run), run), :], r3w2.at[me_t, pl.ds(start_row, run), :], send_sem.at[5, j], rs_sem.at[j, 2], tm=peer))
        return out

    def final_sends(j):
        jo, size, start_row, run = parts_of(j)
        out = []
        for step in range(1, nr):
            peer = (me_r + step) % nr
            one = finw1.at[me_r, :, pl.ds(jo, size)]
            two = finw2.at[me_r, pl.ds(start_row, run), :]
            out.append(remote(one, one, send_sem.at[6, j], rs_sem.at[j, 3], rows=peer))
            out.append(remote(two, two, send_sem.at[6, j], rs_sem.at[j, 3], rows=peer))
        return out

    def reduced(j, kind, sem=None):
        jo, size, _, _ = parts_of(j)
        view = s1w1.at[:, :, :, pl.ds(jo, size)]
        if kind == 1:
            view = s1w1.at[:, pl.ds(0, 2), :, pl.ds(jo, size)]
        elif kind == 2:
            view = s1w1.at[pl.ds(0, nt - 1), pl.ds(0, 2), :, pl.ds(jo, size)]
        elif kind == 3:
            view = s1w1.at[pl.ds(0, 3 * nt // 4), pl.ds(0, 2), :, pl.ds(jo, size)]
        arrived(view, rs_sem.at[j, kind] if sem is None else sem)

    def sum_zero(block):
        first = p.blocks[block][0]
        for j in p.members[block]:
            jo, size, _, _ = parts_of(j)
            cols = slice(jo - first, jo - first + size)
            one = acc1[0 : p.d, cols].astype(BF16)
            s1w1[:, :, :, pl.ds(jo, size)] = one.reshape(nt, nr, p.part, size)
            accb[:, pl.ds(jo, size)] = acc1[p.d : p.d + 8, cols]
            two = acc2[:, cols].astype(BF16).T
            for q in range(nr):
                s1w2[q, pl.ds(jo, size), :] = two[:, p.lanes * q : p.lanes * q + p.lanes]
            start(pair_sends(j))

    def sum_one(j):
        jo, size, _, _ = parts_of(j)
        cols = pl.ds(jo, size)
        reduced(j, 0)
        one = s1w1[:, far, :, cols].astype(F32) + r1w1[1, :, :, cols].astype(F32)
        r1w1[1, :, :, cols] = one.astype(BF16)
        two = s1w2[far, cols, :].astype(F32) + r1w2[1, cols, :].astype(F32)
        r1w2[1, cols, :] = two.astype(BF16)
        start(cross_sends(j))

    def sum_two(j):
        jo, size, start_row, run = parts_of(j)
        cols = pl.ds(jo, size)
        reduced(j, 1)
        one = s1w1[:, me_r, :, cols].astype(F32) + r1w1[0, :, :, cols].astype(F32) + r2w1[:, :, cols].astype(F32)
        r1w1[0, :, :, cols] = one.astype(BF16)
        two = s1w2[me_r, cols, :].astype(F32) + r1w2[0, cols, :].astype(F32) + r2w2[cols, :].astype(F32)
        r1w2[0, cols, :] = two.astype(BF16)
        r3w1[me_t, :, cols] = r1w1[0, me_t, :, cols]
        r3w2[me_t, pl.ds(start_row, run), :] = r1w2[0, pl.ds(pl.multiple_of(jo + run * me_t, run), run), :]
        start(holder_sends(j))

    def sum_three(j):
        jo, size, start_row, run = parts_of(j)
        cols = pl.ds(jo, size)
        reduced(j, 2)
        one = r3w1[0, :, cols].astype(F32)
        two = r3w2[0, pl.ds(start_row, run), :].astype(F32)
        for k in range(1, nt):
            one = one + r3w1[k, :, cols].astype(F32)
            two = two + r3w2[k, pl.ds(start_row, run), :].astype(F32)
        finw1[me_r, :, cols] = one
        finw2[me_r, pl.ds(start_row, run), :] = two
        start(final_sends(j))

    def sum_wait(j):
        reduced(j, 3)

    m = p.m
    per = m // TILE

    def rows_add(ref, i, value, first):
        for s in range(per):
            for c in range(p.nc):
                piece = value[TILE * s : TILE * s + TILE, 128 * c : 128 * c + 128]
                place = (i * per + s, c, slice(GAP, GAP + TILE), slice(None))
                ref[place] = piece if first else ref[place] + piece

    bias_two = small_ref[13:14, :]
    last = len(p.blocks) - 1

    def weights_of(j):
        jo, size = p.blocks[j]
        cols = pl.ds(jo, size)
        w1 = w1b[:, :, :, cols].reshape(p.d, size)
        return w1, jnp.concatenate([w2b[q, cols, :] for q in range(nr)], axis=1)

    def back_dot(grad_hidden, w1):
        return lax.dot_general(
            grad_hidden, w1, (((1,), (1,)), ((), ())), preferred_element_type=F32
        )

    def main_block(j, between):
        jo, size = p.blocks[j]
        cols = pl.ds(jo, size)

        @pl.loop(0, t_len // m)
        def _(i):
            for at, task in between:
                pl.when(i == at)(task)
            rows = pl.ds(pl.multiple_of(i * m, m), m)
            w1, w2 = weights_of(j)
            hidden = jnp.dot(nm[rows, :], w1, preferred_element_type=F32) + b1p[0:1, cols]
            grad_act = back_dot(gb[rows, :], w2)
            prob = 0.5 * (1.0 + lax.erf(hidden * RSQRT_HALF))
            bell = jnp.exp(hidden * hidden * np.float32(-0.5)) * RSQRT_2PI
            act = (hidden * prob).astype(BF16)
            grad_hidden = (grad_act * (prob + hidden * bell)).astype(BF16)
            if j == last:
                nm[rows, 0:size] = act
                gb[rows, 0:size] = grad_hidden
            else:
                branch = jnp.dot(act, w2, preferred_element_type=F32)
                br[rows, :] = branch + bias_two if j == 0 else br[rows, :] + branch
                rows_add(gn, i, back_dot(grad_hidden, w1), j == 0)
            one = jnp.dot(nmt[:, rows], grad_hidden, preferred_element_type=F32)
            two = jnp.dot(gbt[:, rows], act, preferred_element_type=F32)
            acc1[:, 0:size] = one + jnp.where(i > 0, acc1[:, 0:size], 0.0)
            acc2[:, 0:size] = two + jnp.where(i > 0, acc2[:, 0:size], 0.0)

    def then(*calls):
        slots = {}
        for at, task, j in calls:
            slots.setdefault(at, []).append((task, j))

        def run(tasks):
            for task, j in tasks:
                task(j)

        return [(at, functools.partial(run, tasks)) for at, tasks in slots.items()]

    main_block(0, then((1, gather_one, 3), (1, spread, 5), (1, spread, 6), (2, gather_two, 2), (2, gather_one, 4)))
    sum_zero(0)
    near_wait(2)
    main_block(
        1,
        then((1, sum_one, 0), (1, sum_one, 1), (1, gather_two, 3), (1, gather_one, 5), (2, gather_two, 4), (2, gather_one, 6)),
    )
    sum_zero(1)
    near_wait(3)
    near_wait(4)
    main_block(
        2,
        then((1, sum_one, 2), (1, sum_two, 0), (1, sum_two, 1), (1, gather_two, 5), (2, gather_two, 6)),
    )
    sum_zero(2)
    sum_two(2)
    sum_three(0)
    sum_three(1)
    near_wait(5)
    near_wait(6)
    main_block(3, then((1, sum_one, 3), (1, sum_one, 4)))
    sum_zero(3)
    sum_two(3)
    sum_three(2)

    unit_rows = 2 * TILE

    def backward_dots(u, held):
        size = p.blocks[last][1]
        rows = pl.ds(pl.multiple_of(u * unit_rows, unit_rows), unit_rows)
        w1, w2 = weights_of(last)
        held[0:unit_rows, :] = jnp.dot(nm[rows, 0:size], w2, preferred_element_type=F32)
        held[unit_rows : 2 * unit_rows, :] = back_dot(gb[rows, 0:size], w1)

    def backward_tile(b, held, at):
        row = pl.multiple_of(b * TILE, TILE)
        step = 32
        for q in range(TILE // step):
            rows = pl.ds(row + q * step, step)
            place = slice(GAP + q * step, GAP + q * step + step)
            share = slice(at + q * step, at + q * step + step)
            branch = br[rows, :] + held[share, :]
            br[rows, :] = branch
            accs[11] += fold(ct[rows, :].astype(F32) * branch)
            share = slice(unit_rows + at + q * step, unit_rows + at + q * step + step)
            grad = jnp.concatenate([gn[b, c, place, :] for c in range(p.nc)], axis=1) + held[share, :]
            unit = xhat[rows, :].astype(F32)
            both_of = grad * unit
            accs[8] += fold(both_of)
            accs[9] += fold(grad)
            u = grad * gain
            mean_u = jnp.sum(u, axis=1, keepdims=True) * (1.0 / p.d)
            mean_x = jnp.sum(both_of * gain, axis=1, keepdims=True) * (1.0 / p.d)
            inverse = rstd[rows, :]
            inverse = jnp.concatenate([inverse] * p.nc, axis=1)
            rounded = ((u - mean_u - unit * mean_x) * inverse).astype(BF16)
            low = rounded.astype(F32)
            accs[7] += fold(low)
            for c in range(p.nc):
                gn[b, c, place, :] = low[:, 128 * c : 128 * c + 128]
        for c in range(p.nc):
            cols = slice(128 * c, 128 * c + 128)
            low = gn[b, c, GAP : GAP + TILE, :]
            for k in range(TAPS):
                first = GAP - 3 + k
                accs[k, :, cols] += fold(low * xf[b, c, first : first + TILE, :])

    def edge_sends():
        after, before = (me_t + 1) % nt, (me_t + nt - 1) % nt
        return [
            remote(gn.at[nb - 1, :, pl.ds(TILE, GAP), :], hprev, send_sem.at[7, 2], halo_sem.at[2], tm=after),
            remote(gn.at[0, :, pl.ds(GAP, GAP), :], hnext, send_sem.at[7, 3], halo_sem.at[3], tm=before),
        ]

    def backward_unit(u, held):
        backward_tile(2 * u, held, 0)
        backward_tile(2 * u + 1, held, TILE)

    units = nb // 2
    backward_dots(0, acc1)

    @pl.loop(0, units // 2)
    def _(v):
        for at, task in then((1, sum_one, 5), (1, sum_one, 6), (1, sum_two, 4), (4, sum_two, 5), (4, sum_three, 3), (5, sum_two, 6)):
            pl.when(v == at)(task)
        backward_dots(2 * v + 1, acc2)
        backward_unit(2 * v, acc1)
        backward_dots(2 * v + 2 - (2 * v + 2) // units, acc1)
        backward_unit(2 * v + 1, acc2)

    start(edge_sends())

    hidden_tiles = lane_permuted(lambda i: accb[:, 128 * i : 128 * i + 128], p.regrouped, p.ff // 128)
    for c in range(p.nc):
        cols = slice(128 * c, 128 * c + 128)
        line = []
        for k in range(10):
            line.append(jnp.sum(accs[k, :, cols], axis=0, keepdims=True))
        for i in range(3):
            line.append(jnp.sum(hidden_tiles[i * p.nc + c], axis=0, keepdims=True))
        for k in (10, 11):
            line.append(jnp.sum(accs[k, :, cols], axis=0, keepdims=True))
        line.append(jnp.zeros((1, 128), F32))
        sma[c] = jnp.concatenate(line, axis=0)

    def small_one_sends():
        out = []
        for step in range(1, nr):
            peer = (me_r + step) % nr
            out.append(remote(sma.at[peer], smr.at[me_r], send_sem.at[7, 4], sm_sem.at[0], rows=peer))
        return out

    def small_two_sends():
        out = []
        for step in range(1, nt):
            peer = peer_of(step)
            out.append(remote(smq.at[nt], smq.at[me_t], send_sem.at[8, 0], sm_sem.at[1], tm=peer))
        return out

    def small_three_sends():
        out = []
        for step in range(1, nr):
            peer = (me_r + step) % nr
            out.append(remote(smf.at[me_r], smf.at[me_r], send_sem.at[8, 1], sm_sem.at[2], rows=peer))
        return out

    smr[me_r] = sma[me_r]
    start(small_one_sends())

    def small_two():
        arrived(smr.at[pl.ds(0, nr - 1)], sm_sem.at[0])
        total = smr[0]
        for k in range(1, nr):
            total = total + smr[k]
        smq[nt] = total
        smq[me_t] = total
        start(small_two_sends())

    def small_three():
        arrived(smq.at[pl.ds(0, nt - 1)], sm_sem.at[1])
        total = smq[0]
        for k in range(1, nt):
            total = total + smq[k]
        smf[me_r] = total
        start(small_three_sends())

    def exchange_edges(b):
        same = flags[pl.ds(b, 1), :] < 0.5
        for c in range(p.nc):
            gn[b, c, 0:GAP, :] = jnp.where(same, gn[b - 1, c, TILE : TILE + GAP, :], 0.0)
            gn[b - 1, c, GAP + TILE :, :] = jnp.where(same, gn[b, c, GAP : GAP + GAP, :], 0.0)

    def last_tile(b):
        row = pl.multiple_of(b * TILE, TILE)
        rows = pl.ds(row, TILE)
        for c in range(p.nc):
            cols = slice(128 * c, 128 * c + 128)
            source = frx[pl.ds(row + HALO, TILE), cols].astype(F32)
            nm[rows, cols] = (source + scale[:, cols] * br[rows, cols]).astype(BF16)
            total = ct[rows, cols].astype(F32)
            for k in range(TAPS):
                first = GAP + 3 - k
                total = total + small_ref[k : k + 1, cols] * gn[b, c, first : first + TILE, :]
            gb[rows, cols] = total.astype(BF16)

    exchange_edges(1)

    def last_tiles(low, high):
        @pl.loop(low, high)
        def _(b):
            exchange_edges(b + 1)
            last_tile(b)

    cut = [1, 1 + (nb - 2) // 2, 1 + (nb - 2) * 3 // 4, nb - 1]
    last_tiles(cut[0], cut[1])
    sum_three(4)
    small_two()
    sum_three(5)
    last_tiles(cut[1], cut[2])
    sum_three(6)
    last_tiles(cut[2], cut[3])
    arrived(hprev, halo_sem.at[2])
    arrived(hnext, halo_sem.at[3])
    for c in range(p.nc):
        gn[0, c, 0:GAP, :] = jnp.where(flags[0:1, :] < 0.5, hprev[c], 0.0)
        gn[nb - 1, c, GAP + TILE :, :] = jnp.where(flags[nb : nb + 1, :] < 0.5, hnext[c], 0.0)

    @pl.loop(0, 2)
    def _(i):
        last_tile(i * (nb - 1))

    small_three()

    for j in range(len(p.chunks)):
        sum_wait(j)
        spread_wait(j, send_sem.at[0, j])
        far_wait(j, send_sem.at[1, j])
        near_wait(j, send_sem.at[2, j])
        for kind in range(4):
            reduced(j, kind, send_sem.at[3 + kind, j])
    for copy in halo_sends() + edge_sends():
        copy.wait_send()
    arrived(smf.at[pl.ds(0, nr - 1)], sm_sem.at[2])
    for c in range(p.nc):
        small_out[:, 128 * c : 128 * c + 128] = smf[c]

    for copy in small_one_sends() + small_two_sends() + small_three_sends():
        copy.wait_send()
    for load in rest:
        load.wait()


def finish_kernel(
    plan,
    nm, gb, grad1, grad2, grad_small, state1, state2,
    small_master, small_first, small_second, small_average,
    output, ingrad, *rest,
):
    p = plan
    outs1, outs2, outs_small = rest[0:5], rest[5:10], rest[10:15]
    new1, low1, new2, low2, new_small, low_small, sem = rest[15:]
    copies = [
        pltpu.make_async_copy(nm, output.at[0], sem.at[0]),
        pltpu.make_async_copy(gb, ingrad.at[0], sem.at[1]),
    ]
    for copy in copies:
        copy.start()

    def first_grad(q):
        tiles = lane_permuted(
            lambda i: grad1[q, :, 128 * i : 128 * i + 128], p.regrouped, p.ff // 128
        )
        return jnp.concatenate(tiles, axis=1)

    def second_grad(q):
        rows = slice(q * p.part, q * p.part + p.part)
        return jnp.concatenate([grad2[k, rows, :] for k in range(p.nr)], axis=1)

    count = 2
    got = adamw_step(
        small_master[...], small_first[...], small_second[...], small_average[...], grad_small[0:15], rate_small
    )
    for k in range(5):
        source = low_small if k == 4 else new_small.at[k]
        source[...] = got[k]
        copy = pltpu.make_async_copy(source, outs_small[k], sem.at[count])
        copy.start()
        copies.append(copy)
        count += 1
    for grad, state, new, low, outs, rate in (
        (first_grad, state1, new1, low1, outs1, rate_first),
        (second_grad, state2, new2, low2, outs2, rate_second),
    ):
        for q in range(low.shape[0] // p.part):
            rows = slice(q * p.part, q * p.part + p.part)
            got = adamw_step(
                state[0, rows], state[1, rows], state[2, rows], state[3, rows], grad(q), rate
            )
            for k in range(4):
                new[k, rows] = got[k]
            low[rows] = got[4]
        for k in range(5):
            source = low if k == 4 else new.at[k]
            copy = pltpu.make_async_copy(source, outs[k], sem.at[count])
            copy.start()
            copies.append(copy)
            count += 1
    for copy in copies:
        copy.wait()


def finish(plan, kept, smalls):
    vmem = pl.BlockSpec(memory_space=pltpu.VMEM)
    anyplace = pl.BlockSpec(memory_space=pl.ANY)
    kept = [pltpu.with_memory_space_constraint(value, pltpu.VMEM) for value in kept]
    shape1, shape2 = (plan.rows1, plan.ff), (plan.share, plan.d)
    whole = jax.ShapeDtypeStruct((1, plan.t, plan.d), BF16)

    def five(shape):
        return [jax.ShapeDtypeStruct(shape, F32)] * 4 + [jax.ShapeDtypeStruct(shape, BF16)]

    v = pltpu.VMEM
    return pl.pallas_call(
        functools.partial(finish_kernel, plan),
        out_shape=(whole, whole, *five(shape1), *five(shape2), *five(smalls[0].shape)),
        in_specs=[vmem] * 11,
        out_specs=(anyplace,) * 17,
        scratch_shapes=[
            v((4, *shape1), F32),
            v(shape1, BF16),
            v((4, *shape2), F32),
            v(shape2, BF16),
            v((4, *smalls[0].shape), F32),
            v(smalls[0].shape, BF16),
            pltpu.SemaphoreType.DMA((17,)),
        ],
        compiler_params=pltpu.CompilerParams(vmem_limit_bytes=8_000_000),
    )(*kept, *smalls)


def call(plan, frames, cotangent, lengths, one, two, small_master):
    p = plan
    t, d, ff, nt, nr, nb, nc = p.t, p.d, p.ff, p.nt, p.nr, p.nb, p.nc
    vmem = pl.BlockSpec(memory_space=pltpu.VMEM)
    anyplace = pl.BlockSpec(memory_space=pl.ANY)
    n_lens = -(-lengths.shape[1] // 128) * 128
    v = pltpu.VMEM
    scratch = [
        v((t + 2 * HALO, d), BF16),
        v((t, d), BF16),
        v((d + 16, t), BF16),
        v((d, t), BF16),
        v((t, d), F32),
        v((nb, nc, TILE + 2 * GAP, 128), F32),
        v((nb, nc, TILE + 2 * GAP, 128), F32),
        v((t, d), BF16),
        v((t, 128), F32),
        v((nt, nr, p.part, ff), BF16),
        v((nr, ff, p.lanes), BF16),
        v((d + 16, p.widest), F32),
        v((d, p.widest), F32),
        v(lengths.shape, jnp.int32),
        v(small_master.shape, F32),
        v((8, n_lens), F32),
        v((-(-(nb + 1) // 8) * 8, 128), F32),
        v((8, ff), F32),
        v((12, 8, d), F32),
        v((8, ff), F32),
        v((TILE, d), F32),
        v((nt, nr, p.part, ff), BF16),
        v((nr, ff, p.lanes), BF16),
        v((2, nt, p.part, ff), BF16),
        v((2, ff, p.lanes), BF16),
        v((nt, p.part, ff), BF16),
        v((ff, p.lanes), BF16),
        v((nt, p.part, ff), BF16),
        v((nt, p.share, p.lanes), BF16),
        v((nr, 16, p.lanes), F32),
        v((nr, 16, p.lanes), F32),
        v((nt + 1, 16, p.lanes), F32),
        v((nr, 16, p.lanes), F32),
        v((nc, GAP, 128), F32),
        v((nc, GAP, 128), F32),
        pltpu.SemaphoreType.DMA((7,)),
        pltpu.SemaphoreType.DMA((9, len(p.chunks))),
        pltpu.SemaphoreType.DMA((4,)),
        pltpu.SemaphoreType.DMA((len(p.chunks), 3)),
        pltpu.SemaphoreType.DMA((len(p.chunks), 4)),
        pltpu.SemaphoreType.DMA((3,)),
    ]
    return pl.pallas_call(
        functools.partial(kernel, plan),
        out_shape=(
            v((t, d), BF16),
            v((t, d), BF16),
            v((nr, p.part, ff), F32),
            v((nr, p.share, p.lanes), F32),
            v((16, d), F32),
            v((4, p.rows1, ff), F32),
            v((4, p.share, d), F32),
        ),
        in_specs=[anyplace] * 12,
        out_specs=(vmem,) * 7,
        scratch_shapes=scratch,
        compiler_params=pltpu.CompilerParams(
            collective_id=0, has_side_effects=True, vmem_limit_bytes=56_500_000
        ),
    )(frames, cotangent, lengths, *one, *two, small_master)


def padded_2(array, sides, width):
    for axis, dim in sides:
        devices, length = (lax.axis_size(axis), array.shape[dim])
        up = [(i, (i + 1) % devices) for i in range(devices - 1)]
        down = [(j, i) for i, j in up]
        last = lax.slice_in_dim(array, length - width, length, axis=dim)
        leading = lax.slice_in_dim(array, 0, width, axis=dim)
        before = lax.ppermute(last, axis, up)
        after = lax.ppermute(leading, axis, down)
        array = jnp.concatenate([before, array, after], axis=dim)
    return array


def cut_along(array, dim, devices):
    before, after = (array.shape[:dim], array.shape[dim + 1 :])
    return jnp.moveaxis(array.reshape(*before, devices, -1, *after), dim, 0)


def sent_and_summed(array, axis, dim):
    devices = lax.axis_size(axis)
    pieces = lax.all_to_all(cut_along(array, dim, devices), axis, 0, 0, tiled=True)
    return jnp.sum(pieces.astype(jnp.float32), axis=0)


def edge_masks(lengths_row, first_frame, frame_count):
    ends_at = jnp.cumsum(lengths_row, dtype=jnp.int32)
    places = first_frame + jnp.arange(frame_count, dtype=jnp.int32)
    passed = ends_at[None, :] <= places[:, None]
    lower = jnp.max(jnp.where(passed, ends_at[None, :], 0), axis=1)
    upper = jnp.min(jnp.where(passed, ends_at[-1], ends_at[None, :]), axis=1)
    mask_rows = []
    for tap_index in range(7):
        spot_now = places + (tap_index - 3)
        mask_rows.append(((spot_now >= lower) & (spot_now < upper)).astype(jnp.float32))
    return jnp.stack(mask_rows)


def depthwise(padded, tap_rows, masks, frame_count):
    summed = jnp.zeros((frame_count, padded.shape[1]), jnp.float32)
    for tap_index in range(7):
        window = padded[tap_index : tap_index + frame_count].astype(jnp.float32)
        summed = summed + tap_rows[tap_index][None, :] * window * masks[tap_index][:, None]
    return summed


def layer_norm(conv_out, norm_gain, norm_bias):
    centred = conv_out - jnp.mean(conv_out, axis=-1, keepdims=True)
    spread = jnp.mean(centred * centred, axis=-1, keepdims=True)
    return centred * lax.rsqrt(spread + norm_eps) * norm_gain[None, :] + norm_bias[None, :]


def exact_gelu(values):
    return jax.nn.gelu(values, approximate=False)


def frame_product(left_side, right_side):
    return lax.dot_general(
        left_side, right_side, (((0,), (0,)), ((), ())), preferred_element_type=jnp.float32
    )


def plain_body(
    frames,
    cotangent,
    lengths,
    w1_master,
    w1_first,
    w1_second,
    w1_average,
    w2_master,
    w2_first,
    w2_second,
    w2_average,
    small_master,
    small_first,
    small_second,
    small_average,
):
    frame_count = frames.shape[1]
    width = frames.shape[2]
    w1_low, w2_low = (
        lax.all_gather(w1_master.astype(jnp.bfloat16), "tm", axis=0, tiled=True),
        lax.all_gather(w2_master.astype(jnp.bfloat16), "tm", axis=0, tiled=True),
    )
    inputs = frames[0]
    upstream = cotangent[0].astype(jnp.float32)
    masks = edge_masks(lengths[0], lax.axis_index("tm") * frame_count, frame_count)
    tap_rows = small_master[0:7]
    layer_scale = small_master[14]
    padded = padded_2(inputs, (("tm", 0),), 3)
    conv_out = depthwise(padded, tap_rows, masks, frame_count) + small_master[7][None, :]
    normed, norm_back = jax.vjp(layer_norm, conv_out, small_master[8], small_master[9])
    normed_low = normed.astype(jnp.bfloat16)
    hidden = (
        jnp.dot(normed_low, w1_low, preferred_element_type=jnp.float32)
        + small_master[10:13].reshape(-1)[None, :]
    )
    activated, gelu_back = jax.vjp(exact_gelu, hidden)
    act_low = activated.astype(jnp.bfloat16)
    branch = (
        jnp.dot(act_low, w2_low, preferred_element_type=jnp.float32) + small_master[13][None, :]
    )
    output = (inputs.astype(jnp.float32) + layer_scale[None, :] * branch).astype(jnp.bfloat16)
    grad_scale = jnp.sum(upstream * branch, axis=0)
    grad_branch = (layer_scale[None, :] * upstream).astype(jnp.bfloat16)
    grad_act = lax.dot_general(
        grad_branch, w2_low, (((1,), (1,)), ((), ())), preferred_element_type=jnp.float32
    )
    grad_hidden = gelu_back(grad_act)[0].astype(jnp.bfloat16)
    grad_normed = lax.dot_general(
        grad_hidden, w1_low, (((1,), (1,)), ((), ())), preferred_element_type=jnp.float32
    )
    grad_conv, grad_gain, grad_shift = norm_back(grad_normed)
    grad_low = grad_conv.astype(jnp.bfloat16)
    grad_pad = padded_2(grad_low, (("tm", 0),), 3)
    input_grad = (upstream + depthwise(grad_pad, tap_rows[::-1], masks, frame_count)).astype(
        jnp.bfloat16
    )
    grad_float = grad_low.astype(jnp.float32)
    grad_taps = jnp.stack(
        [
            jnp.sum(
                grad_float
                * padded[tap_index : tap_index + frame_count].astype(jnp.float32)
                * masks[tap_index][:, None],
                axis=0,
            )
            for tap_index in range(7)
        ]
    )
    middle_rows = jnp.stack([jnp.sum(grad_float, axis=0), grad_gain, grad_shift])
    bias_rows = jnp.sum(grad_hidden.astype(jnp.float32), axis=0).reshape(3, width)
    last_rows = jnp.stack([jnp.sum(grad_branch.astype(jnp.float32), axis=0), grad_scale])
    small_grad = jnp.concatenate([grad_taps, middle_rows, bias_rows, last_rows], axis=0)
    full_one = frame_product(normed_low, grad_hidden)
    full_two = frame_product(act_low, grad_branch)
    share_one, share_two = (
        sent_and_summed(full_one.astype(jnp.bfloat16), "tm", 0),
        sent_and_summed(full_two.astype(jnp.bfloat16), "tm", 0),
    )
    grad_one, grad_two = (
        lax.psum(share_one.astype(jnp.bfloat16), "rows").astype(jnp.float32),
        lax.psum(share_two.astype(jnp.bfloat16), "rows").astype(jnp.float32),
    )
    small_total = lax.psum(small_grad, ("tm", "rows"))
    one_out = adamw_step(w1_master, w1_first, w1_second, w1_average, grad_one, rate_first)
    two_out = adamw_step(w2_master, w2_first, w2_second, w2_average, grad_two, rate_second)
    small_out = adamw_step(
        small_master, small_first, small_second, small_average, small_total, rate_small
    )
    return (
        output[None],
        input_grad[None],
        one_out[0],
        one_out[1],
        one_out[2],
        one_out[3],
        one_out[4],
        two_out[0],
        two_out[1],
        two_out[2],
        two_out[3],
        two_out[4],
        small_out[0],
        small_out[1],
        small_out[2],
        small_out[3],
        small_out[4],
    )


def body(
    frames,
    cotangent,
    lengths,
    w1_master,
    w1_first,
    w1_second,
    w1_average,
    w2_master,
    w2_first,
    w2_second,
    w2_average,
    small_master,
    small_first,
    small_second,
    small_average,
):
    nt, nr = lax.axis_size("tm"), lax.axis_size("rows")
    plan = Plan(nt, nr, frames.shape[1], frames.shape[2], w1_master.shape[1])
    kept = call(
        plan,
        frames,
        cotangent,
        lengths,
        (w1_master, w1_first, w1_second, w1_average),
        (w2_master, w2_first, w2_second, w2_average),
        small_master,
    )
    return finish(plan, kept, (small_master, small_first, small_second, small_average))


def solution(mesh):
    in_specs = (
        P("rows", "tm", None),
        P("rows", "tm", None),
        P("rows", None),
        P("tm", None),
        P("tm", None),
        P("tm", None),
        P("tm", None),
        P("tm", None),
        P("tm", None),
        P("tm", None),
        P("tm", None),
        P(),
        P(),
        P(),
        P(),
    )
    out_specs = (
        P("rows", "tm", None),
        P("rows", "tm", None),
        P("tm", None),
        P("tm", None),
        P("tm", None),
        P("tm", None),
        P("tm", None),
        P("tm", None),
        P("tm", None),
        P("tm", None),
        P("tm", None),
        P("tm", None),
        P(),
        P(),
        P(),
        P(),
        P(),
    )
    fits = mesh.shape["tm"] == 8 and mesh.shape["rows"] == 4
    return jax.shard_map(body if fits else plain_body, mesh=mesh, in_specs=in_specs, out_specs=out_specs, check_vma=False)
```

```python
import functools

import jax
import jax.numpy as jnp
import numpy as np
from jax import lax
from jax.experimental import pallas as pl
from jax.experimental.pallas import tpu as pltpu
from jax.sharding import PartitionSpec as P

ADAM_STEP = 3
norm_eps = 1e-06
adam_eps = 1e-08
weight_decay = 0.01
beta_first = 0.5
beta_second = 0.5
average_keep = 0.75
rate_first = 0.08
rate_second = 0.05
rate_small = 0.4

TAPS = 7
TILE = 128
GAP = 8
GRAIN = 16
HALO = 16
F32 = jnp.float32
BF16 = jnp.bfloat16
MESH = pl.DeviceIdType.MESH
RSQRT_HALF = np.float32(0.7071067811865476)
RSQRT_2PI = np.float32(0.3989422804014327)


def adamw_step(master, first_old, second_old, average_old, gradient, rate):
    first_new = beta_first * first_old + (1.0 - beta_first) * gradient
    second_new = beta_second * second_old + (1.0 - beta_second) * gradient * gradient
    first_hat = first_new / (1.0 - beta_first**ADAM_STEP)
    second_hat = second_new / (1.0 - beta_second**ADAM_STEP)
    master_new = master - rate * (
        first_hat / (jnp.sqrt(second_hat) + adam_eps) + weight_decay * master
    )
    average_new = average_keep * average_old + (1.0 - average_keep) * master_new
    return (master_new, first_new, second_new, average_new, master_new.astype(BF16))


class Plan:
    def __init__(self, nt, nr, frame_count, width, hidden):
        self.nt, self.nr, self.t, self.d, self.ff = nt, nr, frame_count, width, hidden
        self.share = hidden // nt
        self.rows1 = width // nt
        self.part = self.rows1 // nr
        self.lanes = width // nr
        self.nb = frame_count // TILE
        self.nc = width // 128
        self.chunks = []
        offset = begin = 0
        for run in (16, 16, 32, 32, 32, 32, 32):
            self.chunks.append((offset, run * nt, run, begin))
            offset += run * nt
            begin += run
        self.members = [(0, 1), (2,), (3, 4), (5, 6)]
        self.blocks = [
            (self.chunks[own[0]][0], sum(self.chunks[j][1] for j in own)) for own in self.members
        ]
        self.widest = max(size for _, size in self.blocks)
        self.m = 1024
        self.natural = []
        for _, _, run, begin in self.chunks:
            for k in range(nt):
                for o in range(0, run, GRAIN):
                    self.natural.append((self.share * k + begin + o) // GRAIN)
        self.regrouped = [self.natural.index(g) for g in range(hidden // GRAIN)]


def lane_permuted(tile_of, source, count):
    per = 128 // GRAIN
    out = []
    for tile in range(count):
        value, before = None, None
        for q in range(per):
            run = source[tile * per + q]
            now = (run // per, (q - run % per) % per)
            if now == before:
                continue
            before = now
            piece = tile_of(now[0])
            if now[1]:
                piece = pltpu.roll(piece, now[1] * GRAIN, 1)
            if value is None:
                value = piece
            else:
                lane = lax.broadcasted_iota(jnp.int32, piece.shape, 1)
                value = jnp.where(lane >= q * GRAIN, piece, value)
        out.append(value)
    return out


def fold(value):
    rows = value.shape[0]
    total = value[0:8]
    for g in range(1, rows // 8):
        total = total + value[8 * g : 8 * g + 8]
    return total


def kernel(
    plan,
    frames_hbm,
    cot_hbm,
    lengths_hbm,
    w1_hbm,
    w1_first_hbm,
    w1_second_hbm,
    w1_average_hbm,
    w2_hbm,
    w2_first_hbm,
    w2_second_hbm,
    w2_average_hbm,
    small_hbm,
    nm,
    gb,
    finw1,
    finw2,
    small_out,
    state1,
    state2,
    frx,
    ct,
    nmt,
    gbt,
    br,
    gn,
    xf,
    xhat,
    rstd,
    w1b,
    w2b,
    acc1,
    acc2,
    lengths_ref,
    small_ref,
    lens,
    flags,
    b1p,
    accs,
    accb,
    tmp,
    s1w1,
    s1w2,
    r1w1,
    r1w2,
    r2w1,
    r2w2,
    r3w1,
    r3w2,
    sma,
    smr,
    smq,
    smf,
    hprev,
    hnext,
    in_sem,
    send_sem,
    halo_sem,
    ag_sem,
    rs_sem,
    sm_sem,
):
    p = plan
    nt, nr, t_len = p.nt, p.nr, p.t
    me_t = lax.axis_index("tm")
    me_r = lax.axis_index("rows")
    near = me_r + 1 - 2 * (me_r % 2)
    far = (me_r + 2) % nr
    both = near + 2 - 4 * (near // 2)

    upper = me_t // (nt // 2)

    def peer_of(step):
        return (me_t + step * upper + (nt - step) * (1 - upper)) % nt

    def remote(src, dst, send, recv, tm=None, rows=None):
        device = {"tm": me_t if tm is None else tm, "rows": me_r if rows is None else rows}
        return pltpu.make_async_remote_copy(
            src_ref=src, dst_ref=dst, send_sem=send, recv_sem=recv,
            device_id=device, device_id_type=MESH,
        )

    def arrived(view, sem):
        pltpu.make_async_copy(view, view, sem).wait()

    loads = [
        pltpu.make_async_copy(w1_hbm, state1.at[0], in_sem.at[0]),
        pltpu.make_async_copy(w2_hbm, state2.at[0], in_sem.at[1]),
        pltpu.make_async_copy(frames_hbm.at[0], frx.at[pl.ds(HALO, t_len)], in_sem.at[2]),
        pltpu.make_async_copy(cot_hbm.at[0], ct, in_sem.at[3]),
        pltpu.make_async_copy(lengths_hbm, lengths_ref, in_sem.at[5]),
        pltpu.make_async_copy(small_hbm, small_ref, in_sem.at[6]),
    ]
    for k in (0, 1, 5, 4, 2, 3):
        loads[k].start()

    barrier = pltpu.get_barrier_semaphore()
    for step in range(1, nt):
        pl.semaphore_signal(
            barrier, inc=1, device_id={"tm": (me_t + step) % nt, "rows": me_r}, device_id_type=MESH
        )
    for step in range(1, nr):
        pl.semaphore_signal(
            barrier, inc=1, device_id={"tm": me_t, "rows": (me_r + step) % nr}, device_id_type=MESH
        )

    loads[4].wait()
    loads[5].wait()
    lens[...] = jnp.zeros_like(lens)
    n_len = lengths_ref.shape[1]
    lens[0:1, 0:n_len] = lengths_ref[...].astype(F32)
    ends = lens[...]
    lane = lax.broadcasted_iota(jnp.int32, ends.shape, 1)
    shift = 1
    while shift < lens.shape[1]:
        ends = ends + jnp.where(lane >= shift, pltpu.roll(ends, shift, 1), 0.0)
        shift *= 2
    n_flag = flags.shape[0]
    spot = me_t * t_len + TILE * lax.broadcasted_iota(jnp.int32, (n_flag, lens.shape[1]), 0)
    hit = (ends[0:1, :] == spot.astype(F32)) | (spot == 0)
    edge = jnp.max(jnp.where(hit, 1.0, 0.0), axis=1, keepdims=True)
    flags[...] = jnp.broadcast_to(edge, flags.shape)
    accs[...] = jnp.zeros_like(accs)
    ones_row = lax.broadcasted_iota(jnp.int32, (16, t_len), 0) == 0
    nmt[p.d :, :] = jnp.where(ones_row, 1.0, 0.0).astype(BF16)
    bias_tiles = lane_permuted(
        lambda i: jnp.broadcast_to(small_ref[10 + i // p.nc : 11 + i // p.nc, 128 * (i % p.nc) : 128 * (i % p.nc) + 128], (8, 128)),
        p.natural,
        p.ff // 128,
    )
    for i, tile in enumerate(bias_tiles):
        b1p[:, 128 * i : 128 * i + 128] = tile

    loads[0].wait()
    loads[1].wait()
    own_rows = pl.ds(pl.multiple_of(me_r * p.part, p.part), p.part)
    own_lanes = pl.ds(pl.multiple_of(me_r * p.lanes, p.lanes), p.lanes)
    own1 = lane_permuted(lambda i: state1[0, own_rows, 128 * i : 128 * i + 128], p.natural, p.ff // 128)
    for i, tile in enumerate(own1):
        w1b[me_t, me_r, :, 128 * i : 128 * i + 128] = tile.astype(BF16)
    for jo, _, run, begin in p.chunks:
        w2b[me_r, pl.ds(pl.multiple_of(jo + run * me_t, run), run), :] = state2[0, begin : begin + run, own_lanes].astype(BF16)

    pl.semaphore_wait(barrier, nt + nr - 2)

    def halo_sends():
        after, before = (me_t + 1) % nt, (me_t + nt - 1) % nt
        return [
            remote(frames_hbm.at[0, pl.ds(t_len - HALO, HALO)], frx.at[pl.ds(0, HALO)], send_sem.at[7, 0], halo_sem.at[0], tm=after),
            remote(frames_hbm.at[0, pl.ds(0, HALO)], frx.at[pl.ds(HALO + t_len, HALO)], send_sem.at[7, 1], halo_sem.at[1], tm=before),
        ]

    def w1_part(j, q):
        jo, size = p.chunks[j][:2]
        return w1b.at[:, q, :, pl.ds(jo, size)]

    def w2_part(j, q):
        jo, size = p.chunks[j][:2]
        return w2b.at[q, pl.ds(jo, size), :]

    def spread_sends(j):
        jo, size, run, _ = p.chunks[j]
        out = []
        for step in range(1, nt):
            peer = peer_of(step)
            one = w1b.at[me_t, me_r, :, pl.ds(jo, size)]
            two = w2b.at[me_r, pl.ds(pl.multiple_of(jo + run * me_t, run), run), :]
            out.append(remote(one, one, send_sem.at[0, j], ag_sem.at[j, 0], tm=peer))
            out.append(remote(two, two, send_sem.at[0, j], ag_sem.at[j, 0], tm=peer))
        return out

    def spread_wait(j, sem=None):
        jo, size = p.chunks[j][:2]
        arrived(w1b.at[pl.ds(0, nt - 1), pl.ds(0, 2), :, pl.ds(jo, size)], ag_sem.at[j, 0] if sem is None else sem)

    def far_sends(j):
        return [
            remote(w1_part(j, me_r), w1_part(j, me_r), send_sem.at[1, j], ag_sem.at[j, 1], rows=far),
            remote(w2_part(j, me_r), w2_part(j, me_r), send_sem.at[1, j], ag_sem.at[j, 1], rows=far),
        ]

    def far_wait(j, sem=None):
        jo, size = p.chunks[j][:2]
        arrived(w1b.at[:, pl.ds(0, 2), :, pl.ds(jo, size)], ag_sem.at[j, 1] if sem is None else sem)

    def near_sends(j, q):
        return [
            remote(w1_part(j, q), w1_part(j, q), send_sem.at[2, j], ag_sem.at[j, 2], rows=near),
            remote(w2_part(j, q), w2_part(j, q), send_sem.at[2, j], ag_sem.at[j, 2], rows=near),
        ]

    def near_wait(j, sem=None):
        jo, size = p.chunks[j][:2]
        arrived(w1b.at[:, :, :, pl.ds(jo, size)], ag_sem.at[j, 2] if sem is None else sem)

    def start(copies):
        for copy in copies:
            copy.start()

    def gather_one(j):
        spread_wait(j)
        start(far_sends(j))
        start(near_sends(j, me_r))

    def gather_two(j):
        far_wait(j)
        start(near_sends(j, far))

    def spread(j):
        start(spread_sends(j))

    spread(0)
    spread(1)
    start(halo_sends())

    rest = [
        pltpu.make_async_copy(source, target, in_sem.at[4])
        for source, target in (
            (w1_first_hbm, state1.at[1]),
            (w1_second_hbm, state1.at[2]),
            (w1_average_hbm, state1.at[3]),
            (w2_first_hbm, state2.at[1]),
            (w2_second_hbm, state2.at[2]),
            (w2_average_hbm, state2.at[3]),
        )
    ]
    for load in rest:
        load.start()
    loads[2].wait()
    loads[3].wait()

    gain = small_ref[8:9, :]
    shift_row = small_ref[9:10, :]
    scale = small_ref[14:15, :]

    first_row = jnp.where(lax.broadcasted_iota(jnp.int32, (8, TILE), 0) == 0, 1.0, 0.0).astype(BF16)

    def turn_tile(b):
        row = pl.multiple_of(b * TILE, TILE)
        nmt[0 : p.d, pl.ds(row, TILE)] = nm[pl.ds(row, TILE), :].T
        gbt[:, pl.ds(row, TILE)] = gb[pl.ds(row, TILE), :].T

    def forward_tile(b, turned=None):
        if turned is not None:
            turn_tile(turned)
        row = pl.multiple_of(b * TILE, TILE)
        starts_here = flags[pl.ds(b, 1), :]
        ends_here = flags[pl.ds(b + 1, 1), :]
        lead = frx[pl.ds(row, HALO), :].astype(F32)
        trail = frx[pl.ds(row + HALO + TILE, HALO), :].astype(F32)
        for c in range(p.nc):
            cols = slice(128 * c, 128 * c + 128)
            xf[b, c, GAP : GAP + TILE, :] = frx[pl.ds(row + HALO, TILE), cols].astype(F32)
            xf[b, c, 0:GAP, :] = jnp.where(starts_here > 0.5, 0.0, lead[HALO - GAP :, cols])
            xf[b, c, GAP + TILE :, :] = jnp.where(ends_here > 0.5, 0.0, trail[0:GAP, cols])
        for c in range(p.nc):
            cols = slice(128 * c, 128 * c + 128)
            total = jnp.broadcast_to(small_ref[7:8, cols], (TILE, 128))
            for k in range(TAPS):
                first = GAP - 3 + k
                total = total + small_ref[k : k + 1, cols] * xf[b, c, first : first + TILE, :]
            tmp[:, cols] = total
        step = 32
        for q in range(TILE // step):
            rows = pl.ds(row + q * step, step)
            value = tmp[q * step : q * step + step, :]
            centred = value - jnp.sum(value, axis=1, keepdims=True) * (1.0 / p.d)
            spread = jnp.sum(centred * centred, axis=1, keepdims=True) * (1.0 / p.d)
            inverse = lax.rsqrt(spread + norm_eps)
            unit = centred * inverse
            rstd[rows, :] = jnp.broadcast_to(inverse, (step, 128))
            xhat[rows, :] = unit.astype(BF16)
            nm[rows, :] = (unit * gain + shift_row).astype(BF16)
            low = (scale * ct[rows, :].astype(F32)).astype(BF16)
            gb[rows, :] = low
        accs[10] += jnp.dot(first_row, gb[pl.ds(row, TILE), :], preferred_element_type=F32)

    def forward_tiles(low, high):
        @pl.loop(low, high)
        def _(b):
            forward_tile(b, b - 1)

    nb = p.nb
    forward_tile(1)
    forward_tiles(2, nb // 4 - 1)
    spread(2)
    forward_tiles(nb // 4 - 1, nb * 3 // 8)
    gather_one(0)
    spread(3)
    spread(4)
    forward_tiles(nb * 3 // 8, nb // 2)
    gather_one(1)
    forward_tiles(nb // 2, nb * 2 // 3)
    gather_two(0)
    arrived(frx.at[pl.ds(HALO + t_len, HALO)], halo_sem.at[1])
    forward_tiles(nb * 2 // 3, nb * 5 // 6)
    gather_two(1)
    forward_tiles(nb * 5 // 6, nb)
    gather_one(2)
    arrived(frx.at[pl.ds(0, HALO)], halo_sem.at[0])
    forward_tile(0, nb - 1)
    turn_tile(0)
    near_wait(0)
    near_wait(1)

    def parts_of(j):
        jo, size, run, begin = p.chunks[j]
        return jo, size, begin, run

    def pair_sends(j):
        jo, size, _, _ = parts_of(j)
        out = []
        for slot, q in ((0, near), (1, both)):
            out.append(remote(s1w1.at[:, q, :, pl.ds(jo, size)], r1w1.at[slot, :, :, pl.ds(jo, size)], send_sem.at[3, j], rs_sem.at[j, 0], rows=near))
            out.append(remote(s1w2.at[q, pl.ds(jo, size), :], r1w2.at[slot, pl.ds(jo, size), :], send_sem.at[3, j], rs_sem.at[j, 0], rows=near))
        return out

    def cross_sends(j):
        jo, size, _, _ = parts_of(j)
        return [
            remote(r1w1.at[1, :, :, pl.ds(jo, size)], r2w1.at[:, :, pl.ds(jo, size)], send_sem.at[4, j], rs_sem.at[j, 1], rows=far),
            remote(r1w2.at[1, pl.ds(jo, size), :], r2w2.at[pl.ds(jo, size), :], send_sem.at[4, j], rs_sem.at[j, 1], rows=far),
        ]

    def holder_sends(j):
        jo, size, start_row, run = parts_of(j)
        out = []
        for step in range(1, nt):
            peer = peer_of(step)
            out.append(remote(r1w1.at[0, peer, :, pl.ds(jo, size)], r3w1.at[me_t, :, pl.ds(jo, size)], send_sem.at[5, j], rs_sem.at[j, 2], tm=peer))
            out.append(remote(r1w2.at[0, pl.ds(pl.multiple_of(jo + run * peer, run), run), :], r3w2.at[me_t, pl.ds(start_row, run), :], send_sem.at[5, j], rs_sem.at[j, 2], tm=peer))
        return out

    def final_sends(j):
        jo, size, start_row, run = parts_of(j)
        out = []
        for step in range(1, nr):
            peer = (me_r + step) % nr
            one = finw1.at[me_r, :, pl.ds(jo, size)]
            two = finw2.at[me_r, pl.ds(start_row, run), :]
            out.append(remote(one, one, send_sem.at[6, j], rs_sem.at[j, 3], rows=peer))
            out.append(remote(two, two, send_sem.at[6, j], rs_sem.at[j, 3], rows=peer))
        return out

    def reduced(j, kind, sem=None):
        jo, size, _, _ = parts_of(j)
        view = s1w1.at[:, :, :, pl.ds(jo, size)]
        if kind == 1:
            view = s1w1.at[:, pl.ds(0, 2), :, pl.ds(jo, size)]
        elif kind == 2:
            view = s1w1.at[pl.ds(0, nt - 1), pl.ds(0, 2), :, pl.ds(jo, size)]
        elif kind == 3:
            view = s1w1.at[pl.ds(0, 3 * nt // 4), pl.ds(0, 2), :, pl.ds(jo, size)]
        arrived(view, rs_sem.at[j, kind] if sem is None else sem)

    def sum_zero(block):
        first = p.blocks[block][0]
        for j in p.members[block]:
            jo, size, _, _ = parts_of(j)
            cols = slice(jo - first, jo - first + size)
            one = acc1[0 : p.d, cols].astype(BF16)
            s1w1[:, :, :, pl.ds(jo, size)] = one.reshape(nt, nr, p.part, size)
            accb[:, pl.ds(jo, size)] = acc1[p.d : p.d + 8, cols]
            two = acc2[:, cols].astype(BF16).T
            for q in range(nr):
                s1w2[q, pl.ds(jo, size), :] = two[:, p.lanes * q : p.lanes * q + p.lanes]
            start(pair_sends(j))

    def sum_one(j):
        jo, size, _, _ = parts_of(j)
        cols = pl.ds(jo, size)
        reduced(j, 0)
        one = s1w1[:, far, :, cols].astype(F32) + r1w1[1, :, :, cols].astype(F32)
        r1w1[1, :, :, cols] = one.astype(BF16)
        two = s1w2[far, cols, :].astype(F32) + r1w2[1, cols, :].astype(F32)
        r1w2[1, cols, :] = two.astype(BF16)
        start(cross_sends(j))

    def sum_two(j):
        jo, size, start_row, run = parts_of(j)
        cols = pl.ds(jo, size)
        reduced(j, 1)
        one = s1w1[:, me_r, :, cols].astype(F32) + r1w1[0, :, :, cols].astype(F32) + r2w1[:, :, cols].astype(F32)
        r1w1[0, :, :, cols] = one.astype(BF16)
        two = s1w2[me_r, cols, :].astype(F32) + r1w2[0, cols, :].astype(F32) + r2w2[cols, :].astype(F32)
        r1w2[0, cols, :] = two.astype(BF16)
        r3w1[me_t, :, cols] = r1w1[0, me_t, :, cols]
        r3w2[me_t, pl.ds(start_row, run), :] = r1w2[0, pl.ds(pl.multiple_of(jo + run * me_t, run), run), :]
        start(holder_sends(j))

    def sum_three(j):
        jo, size, start_row, run = parts_of(j)
        cols = pl.ds(jo, size)
        reduced(j, 2)
        one = r3w1[0, :, cols].astype(F32)
        two = r3w2[0, pl.ds(start_row, run), :].astype(F32)
        for k in range(1, nt):
            one = one + r3w1[k, :, cols].astype(F32)
            two = two + r3w2[k, pl.ds(start_row, run), :].astype(F32)
        finw1[me_r, :, cols] = one
        finw2[me_r, pl.ds(start_row, run), :] = two
        start(final_sends(j))

    def sum_wait(j):
        reduced(j, 3)

    m = p.m
    per = m // TILE

    def rows_add(ref, i, value, first):
        for s in range(per):
            for c in range(p.nc):
                piece = value[TILE * s : TILE * s + TILE, 128 * c : 128 * c + 128]
                place = (i * per + s, c, slice(GAP, GAP + TILE), slice(None))
                ref[place] = piece if first else ref[place] + piece

    bias_two = small_ref[13:14, :]
    last = len(p.blocks) - 1

    def weights_of(j):
        jo, size = p.blocks[j]
        cols = pl.ds(jo, size)
        w1 = w1b[:, :, :, cols].reshape(p.d, size)
        return w1, jnp.concatenate([w2b[q, cols, :] for q in range(nr)], axis=1)

    def back_dot(grad_hidden, w1):
        return lax.dot_general(
            grad_hidden, w1, (((1,), (1,)), ((), ())), preferred_element_type=F32
        )

    def main_block(j, between):
        jo, size = p.blocks[j]
        cols = pl.ds(jo, size)

        @pl.loop(0, t_len // m)
        def _(i):
            for at, task in between:
                pl.when(i == at)(task)
            rows = pl.ds(pl.multiple_of(i * m, m), m)
            w1, w2 = weights_of(j)
            hidden = jnp.dot(nm[rows, :], w1, preferred_element_type=F32) + b1p[0:1, cols]
            grad_act = back_dot(gb[rows, :], w2)
            prob = 0.5 * (1.0 + lax.erf(hidden * RSQRT_HALF))
            bell = jnp.exp(hidden * hidden * np.float32(-0.5)) * RSQRT_2PI
            act = (hidden * prob).astype(BF16)
            grad_hidden = (grad_act * (prob + hidden * bell)).astype(BF16)
            if j == last:
                nm[rows, 0:size] = act
                gb[rows, 0:size] = grad_hidden
            else:
                branch = jnp.dot(act, w2, preferred_element_type=F32)
                br[rows, :] = branch + bias_two if j == 0 else br[rows, :] + branch
                rows_add(gn, i, back_dot(grad_hidden, w1), j == 0)
            one = jnp.dot(nmt[:, rows], grad_hidden, preferred_element_type=F32)
            two = jnp.dot(gbt[:, rows], act, preferred_element_type=F32)
            acc1[:, 0:size] = one + jnp.where(i > 0, acc1[:, 0:size], 0.0)
            acc2[:, 0:size] = two + jnp.where(i > 0, acc2[:, 0:size], 0.0)

    def then(*calls):
        slots = {}
        for at, task, j in calls:
            slots.setdefault(at, []).append((task, j))

        def run(tasks):
            for task, j in tasks:
                task(j)

        return [(at, functools.partial(run, tasks)) for at, tasks in slots.items()]

    main_block(0, then((1, gather_one, 3), (1, spread, 5), (1, spread, 6), (2, gather_two, 2), (2, gather_one, 4)))
    sum_zero(0)
    near_wait(2)
    main_block(
        1,
        then((1, sum_one, 0), (1, sum_one, 1), (1, gather_two, 3), (1, gather_one, 5), (2, gather_two, 4), (2, gather_one, 6)),
    )
    sum_zero(1)
    near_wait(3)
    near_wait(4)
    main_block(
        2,
        then((1, sum_one, 2), (1, sum_two, 0), (1, sum_two, 1), (1, gather_two, 5), (2, gather_two, 6)),
    )
    sum_zero(2)
    sum_two(2)
    sum_three(0)
    sum_three(1)
    near_wait(5)
    near_wait(6)
    main_block(3, then((1, sum_one, 3), (1, sum_one, 4)))
    sum_zero(3)
    sum_two(3)
    sum_three(2)

    unit_rows = 2 * TILE

    def backward_dots(u, held):
        size = p.blocks[last][1]
        rows = pl.ds(pl.multiple_of(u * unit_rows, unit_rows), unit_rows)
        w1, w2 = weights_of(last)
        held[0:unit_rows, :] = jnp.dot(nm[rows, 0:size], w2, preferred_element_type=F32)
        held[unit_rows : 2 * unit_rows, :] = back_dot(gb[rows, 0:size], w1)

    def backward_tile(b, held, at):
        row = pl.multiple_of(b * TILE, TILE)
        step = 32
        for q in range(TILE // step):
            rows = pl.ds(row + q * step, step)
            place = slice(GAP + q * step, GAP + q * step + step)
            share = slice(at + q * step, at + q * step + step)
            branch = br[rows, :] + held[share, :]
            br[rows, :] = branch
            accs[11] += fold(ct[rows, :].astype(F32) * branch)
            share = slice(unit_rows + at + q * step, unit_rows + at + q * step + step)
            grad = jnp.concatenate([gn[b, c, place, :] for c in range(p.nc)], axis=1) + held[share, :]
            unit = xhat[rows, :].astype(F32)
            both_of = grad * unit
            accs[8] += fold(both_of)
            accs[9] += fold(grad)
            u = grad * gain
            mean_u = jnp.sum(u, axis=1, keepdims=True) * (1.0 / p.d)
            mean_x = jnp.sum(both_of * gain, axis=1, keepdims=True) * (1.0 / p.d)
            inverse = rstd[rows, :]
            inverse = jnp.concatenate([inverse] * p.nc, axis=1)
            rounded = ((u - mean_u - unit * mean_x) * inverse).astype(BF16)
            low = rounded.astype(F32)
            accs[7] += fold(low)
            for c in range(p.nc):
                gn[b, c, place, :] = low[:, 128 * c : 128 * c + 128]
        for c in range(p.nc):
            cols = slice(128 * c, 128 * c + 128)
            low = gn[b, c, GAP : GAP + TILE, :]
            for k in range(TAPS):
                first = GAP - 3 + k
                accs[k, :, cols] += fold(low * xf[b, c, first : first + TILE, :])

    def edge_sends():
        after, before = (me_t + 1) % nt, (me_t + nt - 1) % nt
        return [
            remote(gn.at[nb - 1, :, pl.ds(TILE, GAP), :], hprev, send_sem.at[7, 2], halo_sem.at[2], tm=after),
            remote(gn.at[0, :, pl.ds(GAP, GAP), :], hnext, send_sem.at[7, 3], halo_sem.at[3], tm=before),
        ]

    def backward_unit(u, held):
        backward_tile(2 * u, held, 0)
        backward_tile(2 * u + 1, held, TILE)

    units = nb // 2
    backward_dots(0, acc1)

    @pl.loop(0, units // 2)
    def _(v):
        for at, task in then((1, sum_one, 5), (1, sum_one, 6), (1, sum_two, 4), (4, sum_two, 5), (4, sum_three, 3)):
            pl.when(v == at)(task)
        backward_dots(2 * v + 1, acc2)
        backward_unit(2 * v, acc1)
        backward_dots(2 * v + 2 - (2 * v + 2) // units, acc1)
        backward_unit(2 * v + 1, acc2)

    sum_two(6)
    start(edge_sends())

    hidden_tiles = lane_permuted(lambda i: accb[:, 128 * i : 128 * i + 128], p.regrouped, p.ff // 128)
    for c in range(p.nc):
        cols = slice(128 * c, 128 * c + 128)
        line = []
        for k in range(10):
            line.append(jnp.sum(accs[k, :, cols], axis=0, keepdims=True))
        for i in range(3):
            line.append(jnp.sum(hidden_tiles[i * p.nc + c], axis=0, keepdims=True))
        for k in (10, 11):
            line.append(jnp.sum(accs[k, :, cols], axis=0, keepdims=True))
        line.append(jnp.zeros((1, 128), F32))
        sma[c] = jnp.concatenate(line, axis=0)

    def small_one_sends():
        out = []
        for step in range(1, nr):
            peer = (me_r + step) % nr
            out.append(remote(sma.at[peer], smr.at[me_r], send_sem.at[7, 4], sm_sem.at[0], rows=peer))
        return out

    def small_two_sends():
        out = []
        for step in range(1, nt):
            peer = peer_of(step)
            out.append(remote(smq.at[nt], smq.at[me_t], send_sem.at[8, 0], sm_sem.at[1], tm=peer))
        return out

    def small_three_sends():
        out = []
        for step in range(1, nr):
            peer = (me_r + step) % nr
            out.append(remote(smf.at[me_r], smf.at[me_r], send_sem.at[8, 1], sm_sem.at[2], rows=peer))
        return out

    smr[me_r] = sma[me_r]
    start(small_one_sends())

    def small_two():
        arrived(smr.at[pl.ds(0, nr - 1)], sm_sem.at[0])
        total = smr[0]
        for k in range(1, nr):
            total = total + smr[k]
        smq[nt] = total
        smq[me_t] = total
        start(small_two_sends())

    def small_three():
        arrived(smq.at[pl.ds(0, nt - 1)], sm_sem.at[1])
        total = smq[0]
        for k in range(1, nt):
            total = total + smq[k]
        smf[me_r] = total
        start(small_three_sends())

    def exchange_edges(b):
        same = flags[pl.ds(b, 1), :] < 0.5
        for c in range(p.nc):
            gn[b, c, 0:GAP, :] = jnp.where(same, gn[b - 1, c, TILE : TILE + GAP, :], 0.0)
            gn[b - 1, c, GAP + TILE :, :] = jnp.where(same, gn[b, c, GAP : GAP + GAP, :], 0.0)

    def last_tile(b):
        row = pl.multiple_of(b * TILE, TILE)
        rows = pl.ds(row, TILE)
        for c in range(p.nc):
            cols = slice(128 * c, 128 * c + 128)
            source = frx[pl.ds(row + HALO, TILE), cols].astype(F32)
            nm[rows, cols] = (source + scale[:, cols] * br[rows, cols]).astype(BF16)
            total = ct[rows, cols].astype(F32)
            for k in range(TAPS):
                first = GAP + 3 - k
                total = total + small_ref[k : k + 1, cols] * gn[b, c, first : first + TILE, :]
            gb[rows, cols] = total.astype(BF16)

    exchange_edges(1)

    def last_tiles(low, high):
        @pl.loop(low, high)
        def _(b):
            exchange_edges(b + 1)
            last_tile(b)

    cut = [1, 1 + (nb - 2) // 2, 1 + (nb - 2) * 3 // 4, nb - 1]
    last_tiles(cut[0], cut[1])
    sum_three(4)
    small_two()
    sum_three(5)
    last_tiles(cut[1], cut[2])
    sum_three(6)
    last_tiles(cut[2], cut[3])
    arrived(hprev, halo_sem.at[2])
    arrived(hnext, halo_sem.at[3])
    for c in range(p.nc):
        gn[0, c, 0:GAP, :] = jnp.where(flags[0:1, :] < 0.5, hprev[c], 0.0)
        gn[nb - 1, c, GAP + TILE :, :] = jnp.where(flags[nb : nb + 1, :] < 0.5, hnext[c], 0.0)

    @pl.loop(0, 2)
    def _(i):
        last_tile(i * (nb - 1))

    small_three()

    for j in range(len(p.chunks)):
        sum_wait(j)
        spread_wait(j, send_sem.at[0, j])
        far_wait(j, send_sem.at[1, j])
        near_wait(j, send_sem.at[2, j])
        for kind in range(4):
            reduced(j, kind, send_sem.at[3 + kind, j])
    for copy in halo_sends() + edge_sends():
        copy.wait_send()
    arrived(smf.at[pl.ds(0, nr - 1)], sm_sem.at[2])
    for c in range(p.nc):
        small_out[:, 128 * c : 128 * c + 128] = smf[c]

    for copy in small_one_sends() + small_two_sends() + small_three_sends():
        copy.wait_send()
    for load in rest:
        load.wait()


def finish_kernel(
    plan,
    nm, gb, grad1, grad2, grad_small, state1, state2,
    small_master, small_first, small_second, small_average,
    output, ingrad, *rest,
):
    p = plan
    outs1, outs2, outs_small = rest[0:5], rest[5:10], rest[10:15]
    new1, low1, new2, low2, new_small, low_small, sem = rest[15:]
    copies = [
        pltpu.make_async_copy(nm, output.at[0], sem.at[0]),
        pltpu.make_async_copy(gb, ingrad.at[0], sem.at[1]),
    ]
    for copy in copies:
        copy.start()

    def first_grad(q):
        tiles = lane_permuted(
            lambda i: grad1[q, :, 128 * i : 128 * i + 128], p.regrouped, p.ff // 128
        )
        return jnp.concatenate(tiles, axis=1)

    def second_grad(q):
        rows = slice(q * p.part, q * p.part + p.part)
        return jnp.concatenate([grad2[k, rows, :] for k in range(p.nr)], axis=1)

    count = 2
    got = adamw_step(
        small_master[...], small_first[...], small_second[...], small_average[...], grad_small[0:15], rate_small
    )
    for k in range(5):
        source = low_small if k == 4 else new_small.at[k]
        source[...] = got[k]
        copy = pltpu.make_async_copy(source, outs_small[k], sem.at[count])
        copy.start()
        copies.append(copy)
        count += 1
    for grad, state, new, low, outs, rate in (
        (first_grad, state1, new1, low1, outs1, rate_first),
        (second_grad, state2, new2, low2, outs2, rate_second),
    ):
        for q in range(low.shape[0] // p.part):
            rows = slice(q * p.part, q * p.part + p.part)
            got = adamw_step(
                state[0, rows], state[1, rows], state[2, rows], state[3, rows], grad(q), rate
            )
            for k in range(4):
                new[k, rows] = got[k]
            low[rows] = got[4]
        for k in range(5):
            source = low if k == 4 else new.at[k]
            copy = pltpu.make_async_copy(source, outs[k], sem.at[count])
            copy.start()
            copies.append(copy)
            count += 1
    for copy in copies:
        copy.wait()


def finish(plan, kept, smalls):
    vmem = pl.BlockSpec(memory_space=pltpu.VMEM)
    anyplace = pl.BlockSpec(memory_space=pl.ANY)
    kept = [pltpu.with_memory_space_constraint(value, pltpu.VMEM) for value in kept]
    shape1, shape2 = (plan.rows1, plan.ff), (plan.share, plan.d)
    whole = jax.ShapeDtypeStruct((1, plan.t, plan.d), BF16)

    def five(shape):
        return [jax.ShapeDtypeStruct(shape, F32)] * 4 + [jax.ShapeDtypeStruct(shape, BF16)]

    v = pltpu.VMEM
    return pl.pallas_call(
        functools.partial(finish_kernel, plan),
        out_shape=(whole, whole, *five(shape1), *five(shape2), *five(smalls[0].shape)),
        in_specs=[vmem] * 11,
        out_specs=(anyplace,) * 17,
        scratch_shapes=[
            v((4, *shape1), F32),
            v(shape1, BF16),
            v((4, *shape2), F32),
            v(shape2, BF16),
            v((4, *smalls[0].shape), F32),
            v(smalls[0].shape, BF16),
            pltpu.SemaphoreType.DMA((17,)),
        ],
        compiler_params=pltpu.CompilerParams(vmem_limit_bytes=8_000_000),
    )(*kept, *smalls)


def call(plan, frames, cotangent, lengths, one, two, small_master):
    p = plan
    t, d, ff, nt, nr, nb, nc = p.t, p.d, p.ff, p.nt, p.nr, p.nb, p.nc
    vmem = pl.BlockSpec(memory_space=pltpu.VMEM)
    anyplace = pl.BlockSpec(memory_space=pl.ANY)
    n_lens = -(-lengths.shape[1] // 128) * 128
    v = pltpu.VMEM
    scratch = [
        v((t + 2 * HALO, d), BF16),
        v((t, d), BF16),
        v((d + 16, t), BF16),
        v((d, t), BF16),
        v((t, d), F32),
        v((nb, nc, TILE + 2 * GAP, 128), F32),
        v((nb, nc, TILE + 2 * GAP, 128), F32),
        v((t, d), BF16),
        v((t, 128), F32),
        v((nt, nr, p.part, ff), BF16),
        v((nr, ff, p.lanes), BF16),
        v((d + 16, p.widest), F32),
        v((d, p.widest), F32),
        v(lengths.shape, jnp.int32),
        v(small_master.shape, F32),
        v((8, n_lens), F32),
        v((-(-(nb + 1) // 8) * 8, 128), F32),
        v((8, ff), F32),
        v((12, 8, d), F32),
        v((8, ff), F32),
        v((TILE, d), F32),
        v((nt, nr, p.part, ff), BF16),
        v((nr, ff, p.lanes), BF16),
        v((2, nt, p.part, ff), BF16),
        v((2, ff, p.lanes), BF16),
        v((nt, p.part, ff), BF16),
        v((ff, p.lanes), BF16),
        v((nt, p.part, ff), BF16),
        v((nt, p.share, p.lanes), BF16),
        v((nr, 16, p.lanes), F32),
        v((nr, 16, p.lanes), F32),
        v((nt + 1, 16, p.lanes), F32),
        v((nr, 16, p.lanes), F32),
        v((nc, GAP, 128), F32),
        v((nc, GAP, 128), F32),
        pltpu.SemaphoreType.DMA((7,)),
        pltpu.SemaphoreType.DMA((9, len(p.chunks))),
        pltpu.SemaphoreType.DMA((4,)),
        pltpu.SemaphoreType.DMA((len(p.chunks), 3)),
        pltpu.SemaphoreType.DMA((len(p.chunks), 4)),
        pltpu.SemaphoreType.DMA((3,)),
    ]
    return pl.pallas_call(
        functools.partial(kernel, plan),
        out_shape=(
            v((t, d), BF16),
            v((t, d), BF16),
            v((nr, p.part, ff), F32),
            v((nr, p.share, p.lanes), F32),
            v((16, d), F32),
            v((4, p.rows1, ff), F32),
            v((4, p.share, d), F32),
        ),
        in_specs=[anyplace] * 12,
        out_specs=(vmem,) * 7,
        scratch_shapes=scratch,
        compiler_params=pltpu.CompilerParams(
            collective_id=0, has_side_effects=True, vmem_limit_bytes=56_500_000
        ),
    )(frames, cotangent, lengths, *one, *two, small_master)


def padded_2(array, sides, width):
    for axis, dim in sides:
        devices, length = (lax.axis_size(axis), array.shape[dim])
        up = [(i, (i + 1) % devices) for i in range(devices - 1)]
        down = [(j, i) for i, j in up]
        last = lax.slice_in_dim(array, length - width, length, axis=dim)
        leading = lax.slice_in_dim(array, 0, width, axis=dim)
        before = lax.ppermute(last, axis, up)
        after = lax.ppermute(leading, axis, down)
        array = jnp.concatenate([before, array, after], axis=dim)
    return array


def cut_along(array, dim, devices):
    before, after = (array.shape[:dim], array.shape[dim + 1 :])
    return jnp.moveaxis(array.reshape(*before, devices, -1, *after), dim, 0)


def sent_and_summed(array, axis, dim):
    devices = lax.axis_size(axis)
    pieces = lax.all_to_all(cut_along(array, dim, devices), axis, 0, 0, tiled=True)
    return jnp.sum(pieces.astype(jnp.float32), axis=0)


def edge_masks(lengths_row, first_frame, frame_count):
    ends_at = jnp.cumsum(lengths_row, dtype=jnp.int32)
    places = first_frame + jnp.arange(frame_count, dtype=jnp.int32)
    passed = ends_at[None, :] <= places[:, None]
    lower = jnp.max(jnp.where(passed, ends_at[None, :], 0), axis=1)
    upper = jnp.min(jnp.where(passed, ends_at[-1], ends_at[None, :]), axis=1)
    mask_rows = []
    for tap_index in range(7):
        spot_now = places + (tap_index - 3)
        mask_rows.append(((spot_now >= lower) & (spot_now < upper)).astype(jnp.float32))
    return jnp.stack(mask_rows)


def depthwise(padded, tap_rows, masks, frame_count):
    summed = jnp.zeros((frame_count, padded.shape[1]), jnp.float32)
    for tap_index in range(7):
        window = padded[tap_index : tap_index + frame_count].astype(jnp.float32)
        summed = summed + tap_rows[tap_index][None, :] * window * masks[tap_index][:, None]
    return summed


def layer_norm(conv_out, norm_gain, norm_bias):
    centred = conv_out - jnp.mean(conv_out, axis=-1, keepdims=True)
    spread = jnp.mean(centred * centred, axis=-1, keepdims=True)
    return centred * lax.rsqrt(spread + norm_eps) * norm_gain[None, :] + norm_bias[None, :]


def exact_gelu(values):
    return jax.nn.gelu(values, approximate=False)


def frame_product(left_side, right_side):
    return lax.dot_general(
        left_side, right_side, (((0,), (0,)), ((), ())), preferred_element_type=jnp.float32
    )


def plain_body(
    frames,
    cotangent,
    lengths,
    w1_master,
    w1_first,
    w1_second,
    w1_average,
    w2_master,
    w2_first,
    w2_second,
    w2_average,
    small_master,
    small_first,
    small_second,
    small_average,
):
    frame_count = frames.shape[1]
    width = frames.shape[2]
    w1_low, w2_low = (
        lax.all_gather(w1_master.astype(jnp.bfloat16), "tm", axis=0, tiled=True),
        lax.all_gather(w2_master.astype(jnp.bfloat16), "tm", axis=0, tiled=True),
    )
    inputs = frames[0]
    upstream = cotangent[0].astype(jnp.float32)
    masks = edge_masks(lengths[0], lax.axis_index("tm") * frame_count, frame_count)
    tap_rows = small_master[0:7]
    layer_scale = small_master[14]
    padded = padded_2(inputs, (("tm", 0),), 3)
    conv_out = depthwise(padded, tap_rows, masks, frame_count) + small_master[7][None, :]
    normed, norm_back = jax.vjp(layer_norm, conv_out, small_master[8], small_master[9])
    normed_low = normed.astype(jnp.bfloat16)
    hidden = (
        jnp.dot(normed_low, w1_low, preferred_element_type=jnp.float32)
        + small_master[10:13].reshape(-1)[None, :]
    )
    activated, gelu_back = jax.vjp(exact_gelu, hidden)
    act_low = activated.astype(jnp.bfloat16)
    branch = (
        jnp.dot(act_low, w2_low, preferred_element_type=jnp.float32) + small_master[13][None, :]
    )
    output = (inputs.astype(jnp.float32) + layer_scale[None, :] * branch).astype(jnp.bfloat16)
    grad_scale = jnp.sum(upstream * branch, axis=0)
    grad_branch = (layer_scale[None, :] * upstream).astype(jnp.bfloat16)
    grad_act = lax.dot_general(
        grad_branch, w2_low, (((1,), (1,)), ((), ())), preferred_element_type=jnp.float32
    )
    grad_hidden = gelu_back(grad_act)[0].astype(jnp.bfloat16)
    grad_normed = lax.dot_general(
        grad_hidden, w1_low, (((1,), (1,)), ((), ())), preferred_element_type=jnp.float32
    )
    grad_conv, grad_gain, grad_shift = norm_back(grad_normed)
    grad_low = grad_conv.astype(jnp.bfloat16)
    grad_pad = padded_2(grad_low, (("tm", 0),), 3)
    input_grad = (upstream + depthwise(grad_pad, tap_rows[::-1], masks, frame_count)).astype(
        jnp.bfloat16
    )
    grad_float = grad_low.astype(jnp.float32)
    grad_taps = jnp.stack(
        [
            jnp.sum(
                grad_float
                * padded[tap_index : tap_index + frame_count].astype(jnp.float32)
                * masks[tap_index][:, None],
                axis=0,
            )
            for tap_index in range(7)
        ]
    )
    middle_rows = jnp.stack([jnp.sum(grad_float, axis=0), grad_gain, grad_shift])
    bias_rows = jnp.sum(grad_hidden.astype(jnp.float32), axis=0).reshape(3, width)
    last_rows = jnp.stack([jnp.sum(grad_branch.astype(jnp.float32), axis=0), grad_scale])
    small_grad = jnp.concatenate([grad_taps, middle_rows, bias_rows, last_rows], axis=0)
    full_one = frame_product(normed_low, grad_hidden)
    full_two = frame_product(act_low, grad_branch)
    share_one, share_two = (
        sent_and_summed(full_one.astype(jnp.bfloat16), "tm", 0),
        sent_and_summed(full_two.astype(jnp.bfloat16), "tm", 0),
    )
    grad_one, grad_two = (
        lax.psum(share_one.astype(jnp.bfloat16), "rows").astype(jnp.float32),
        lax.psum(share_two.astype(jnp.bfloat16), "rows").astype(jnp.float32),
    )
    small_total = lax.psum(small_grad, ("tm", "rows"))
    one_out = adamw_step(w1_master, w1_first, w1_second, w1_average, grad_one, rate_first)
    two_out = adamw_step(w2_master, w2_first, w2_second, w2_average, grad_two, rate_second)
    small_out = adamw_step(
        small_master, small_first, small_second, small_average, small_total, rate_small
    )
    return (
        output[None],
        input_grad[None],
        one_out[0],
        one_out[1],
        one_out[2],
        one_out[3],
        one_out[4],
        two_out[0],
        two_out[1],
        two_out[2],
        two_out[3],
        two_out[4],
        small_out[0],
        small_out[1],
        small_out[2],
        small_out[3],
        small_out[4],
    )


def body(
    frames,
    cotangent,
    lengths,
    w1_master,
    w1_first,
    w1_second,
    w1_average,
    w2_master,
    w2_first,
    w2_second,
    w2_average,
    small_master,
    small_first,
    small_second,
    small_average,
):
    nt, nr = lax.axis_size("tm"), lax.axis_size("rows")
    plan = Plan(nt, nr, frames.shape[1], frames.shape[2], w1_master.shape[1])
    kept = call(
        plan,
        frames,
        cotangent,
        lengths,
        (w1_master, w1_first, w1_second, w1_average),
        (w2_master, w2_first, w2_second, w2_average),
        small_master,
    )
    return finish(plan, kept, (small_master, small_first, small_second, small_average))


def solution(mesh):
    in_specs = (
        P("rows", "tm", None),
        P("rows", "tm", None),
        P("rows", None),
        P("tm", None),
        P("tm", None),
        P("tm", None),
        P("tm", None),
        P("tm", None),
        P("tm", None),
        P("tm", None),
        P("tm", None),
        P(),
        P(),
        P(),
        P(),
    )
    out_specs = (
        P("rows", "tm", None),
        P("rows", "tm", None),
        P("tm", None),
        P("tm", None),
        P("tm", None),
        P("tm", None),
        P("tm", None),
        P("tm", None),
        P("tm", None),
        P("tm", None),
        P("tm", None),
        P("tm", None),
        P(),
        P(),
        P(),
        P(),
        P(),
    )
    fits = mesh.shape["tm"] == 8 and mesh.shape["rows"] == 4
    return jax.shard_map(body if fits else plain_body, mesh=mesh, in_specs=in_specs, out_specs=out_specs, check_vma=False)
```
